256 devices in a mesh: gx: 8 (over y, z_hi), gy: 8 (over x, core), gz: 4 (over z_lo).
Axes of the slice: x: 4, y: 4, z: 8 (z_hi: 2, z_lo: 4; z = z_hi * 4 + z_lo), core: 2. Of those that a mesh axis runs over, the one named last changes fastest.
Arguments:
- volume: bfloat16 [32, 64, 64, 128], P('gz', 'gx', 'gy'), may hold values from -6 to 6
- cotangent: bfloat16 [32, 64, 64, 128], P('gz', 'gx', 'gy'), may hold values from -0.0390625 to 0.0390625
- w_conv: bfloat16 [128, 27, 128], replicated, may hold values from -0.109375 to 0.109375
- w_down: bfloat16 [8, 128, 512], replicated, may hold values from -0.25 to 0.25
- w_bottle: bfloat16 [512, 27, 512], P(None, None, 'gz'), may hold values from -0.0546875 to 0.0546875
- w_up: bfloat16 [8, 512, 128], replicated, may hold values from -0.375 to 0.375
Outputs:
- output: bfloat16 [32, 64, 64, 128], P('gz', 'gx', 'gy')
- grad_conv: float32 [128, 27, 128], P(('gx', 'gy'))
- grad_bottle: float32 [512, 27, 512], P(('gx', 'gy'), None, 'gz')
The draws below stay inside these ranges and needn't reach their ends.
All inputs are finite; a program needn't handle non-finite values.
Results may differ from the reference program's by a relative error of at most 0.015.
Values may be sent and summed in bfloat16 or wider, within the bound.
A program may use at most 64 MiB of HBM per device.

```python
import jax
import jax.numpy as jnp
from jax import lax

C = 128
CB = 512
ZF = 32
XF = 64
YF = 64


def block_levels(key, shape, shards, least, largest):
    level, own = 1.0, jax.random.fold_in(key, 6)
    for dim, shards_of in shards:
        draws = jnp.exp(jax.random.uniform(jax.random.fold_in(own, dim), (shards_of,), jnp.float32, least / len(shards), largest / len(shards)))
        level = level * jnp.repeat(draws, shape[dim] // shards_of).reshape([-1 if axis == dim else 1 for axis in range(len(shape))])
    return level


def scatter_about(own_key, shape, deviation, bound, cuts=(), kind=jnp.bfloat16):
    factor_of = block_levels(own_key, shape, cuts, -0.22, 0.18) if cuts else 1.0
    drawn = jax.random.normal(own_key, shape, jnp.float32) * deviation * factor_of
    return jnp.minimum(jnp.maximum(drawn, -bound), bound).astype(kind)


def setup_inputs(seed: int = 0) -> dict:
    key_of = jax.random.split(jax.random.key(seed), 7)
    volume = scatter_about(key_of[0], (ZF, XF, YF, C), 1.0, 6.0, ((0, 4), (1, 8), (2, 8)))
    cotangent = scatter_about(key_of[1], (ZF, XF, YF, C), ((ZF * XF * YF) ** -0.5), 0.0390625, ((0, 4), (1, 8), (2, 8)))
    w_conv = scatter_about(key_of[2], (C, 27, C), (27 * C) ** -0.5, 0.109375)
    w_down = scatter_about(key_of[3], (8, C, CB), (4 * C) ** -0.5, 0.25)
    w_bottle = scatter_about(key_of[4], (CB, 27, CB), (27 * CB) ** -0.5, 0.0546875, ((2, 4),))
    w_up = scatter_about(key_of[5], (8, CB, C), (CB // 2) ** -0.5, 0.375)
    return dict(volume=volume, cotangent=cotangent, w_conv=w_conv, w_down=w_down, w_bottle=w_bottle, w_up=w_up)


def silu_slope(values):
    sig = jax.nn.sigmoid(values)
    return sig * (1.0 + values * (1.0 - sig))

def conv_forward(padded, weight, extent):
    size_z, size_x, size_y = extent
    count_cells = size_z * size_x * size_y
    summed = jnp.zeros((count_cells, weight.shape[2]), jnp.float32)
    for tap_index in range(27):
        shift_z, shift_x, shift_y = (tap_index // 9, tap_index // 3 % 3, tap_index % 3)
        window = padded[shift_z:shift_z + size_z, shift_x:shift_x + size_x, shift_y:shift_y + size_y, :]
        window = window.reshape(count_cells, padded.shape[3])
        summed = summed + jnp.dot(window, weight[:, tap_index, :], preferred_element_type=jnp.float32)
    return summed.reshape(size_z, size_x, size_y, weight.shape[2])

def conv_weight_grad(padded, gradient, extent):
    size_z, size_x, size_y = extent
    count_cells = size_z * size_x * size_y
    flat_gradient = gradient.reshape(count_cells, gradient.shape[3])
    pieces = []
    for tap_index in range(27):
        shift_z, shift_x, shift_y = (tap_index // 9, tap_index // 3 % 3, tap_index % 3)
        window = padded[shift_z:shift_z + size_z, shift_x:shift_x + size_x, shift_y:shift_y + size_y, :]
        window = window.reshape(count_cells, padded.shape[3])
        pieces.append(lax.dot_general(window, flat_gradient, (((0,), (0,)), ((), ())), preferred_element_type=jnp.float32))
    return jnp.stack(pieces, axis=1)

def conv_input_grad(padded, weight, extent):
    size_z, size_x, size_y = extent
    count_cells = size_z * size_x * size_y
    summed = jnp.zeros((count_cells, weight.shape[0]), jnp.float32)
    for tap_index in range(27):
        shift_z, shift_x, shift_y = (2 - tap_index // 9, 2 - tap_index // 3 % 3, 2 - tap_index % 3)
        window = padded[shift_z:shift_z + size_z, shift_x:shift_x + size_x, shift_y:shift_y + size_y, :]
        window = window.reshape(count_cells, padded.shape[3])
        summed = summed + lax.dot_general(window, weight[:, tap_index, :], (((1,), (1,)), ((), ())), preferred_element_type=jnp.float32)
    return summed.reshape(size_z, size_x, size_y, weight.shape[0])

def pool_features(fine, kernel):
    size_z, size_x, size_y, channels = fine.shape
    blocks = fine.reshape(size_z // 2, 2, size_x // 2, 2, size_y // 2, 2, channels).astype(jnp.float32)
    kernel_cube = kernel.reshape(2, 2, 2, kernel.shape[1], kernel.shape[2]).astype(jnp.float32)
    return jnp.einsum('zaxbycf,abcfg->zxyg', blocks, kernel_cube)

def pool_adjoint(coarse_in, kernel):
    size_z, size_x, size_y, wide_channels = coarse_in.shape
    kernel_cube = kernel.reshape(2, 2, 2, kernel.shape[1], kernel.shape[2]).astype(jnp.float32)
    result = jnp.einsum('zxyg,abcfg->zaxbycf', coarse_in.astype(jnp.float32), kernel_cube)
    return result.reshape(2 * size_z, 2 * size_x, 2 * size_y, kernel.shape[1])

def lift_features(coarse_in, kernel):
    size_z, size_x, size_y, wide_channels = coarse_in.shape
    kernel_cube = kernel.reshape(2, 2, 2, kernel.shape[1], kernel.shape[2]).astype(jnp.float32)
    result = jnp.einsum('zxyg,abcgf->zaxbycf', coarse_in.astype(jnp.float32), kernel_cube)
    return result.reshape(2 * size_z, 2 * size_x, 2 * size_y, kernel.shape[2])

def lift_adjoint(fine, kernel):
    size_z, size_x, size_y, channels = fine.shape
    blocks = fine.reshape(size_z // 2, 2, size_x // 2, 2, size_y // 2, 2, channels).astype(jnp.float32)
    kernel_cube = kernel.reshape(2, 2, 2, kernel.shape[1], kernel.shape[2]).astype(jnp.float32)
    return jnp.einsum('zaxbycf,abcgf->zxyg', blocks, kernel_cube)

def reference(volume, cotangent, w_conv, w_down, w_bottle, w_up):
    size_z, size_x, size_y, channels = volume.shape
    fine_extent = (size_z, size_x, size_y)
    coarse_extent = (size_z // 2, size_x // 2, size_y // 2)
    padded = jnp.pad(volume, ((1, 1), (1, 1), (1, 1), (0, 0)))
    pre_hidden = conv_forward(padded, w_conv, fine_extent)
    hidden = jax.nn.silu(pre_hidden).astype(jnp.bfloat16)
    coarse = pool_features(hidden, w_down).astype(jnp.bfloat16)
    coarse_pad = jnp.pad(coarse, ((1, 1), (1, 1), (1, 1), (0, 0)))
    pre_bottle = conv_forward(coarse_pad, w_bottle, coarse_extent)
    bottle = jax.nn.silu(pre_bottle).astype(jnp.bfloat16)
    lifted = lift_features(bottle, w_up)
    output = (lifted + hidden.astype(jnp.float32)).astype(jnp.bfloat16)
    back_bottle = lift_adjoint(cotangent, w_up).astype(jnp.bfloat16)
    bottle_grad = (back_bottle.astype(jnp.float32) * silu_slope(pre_bottle)).astype(jnp.bfloat16)
    grad_bottle = conv_weight_grad(coarse_pad, bottle_grad, coarse_extent)
    grad_pad = jnp.pad(bottle_grad, ((1, 1), (1, 1), (1, 1), (0, 0)))
    coarse_grad = conv_input_grad(grad_pad, w_bottle, coarse_extent).astype(jnp.bfloat16)
    hidden_grad = ((pool_adjoint(coarse_grad, w_down) + cotangent.astype(jnp.float32)) * silu_slope(pre_hidden)).astype(jnp.bfloat16)
    grad_conv = conv_weight_grad(padded, hidden_grad, fine_extent)
    return (output, grad_conv, grad_bottle)
```

```python
import jax
import jax.numpy as jnp
from jax import lax
from jax.experimental import pallas as pl
from jax.experimental.pallas import tpu as pltpu
from jax.sharding import PartitionSpec as P

BF = jnp.bfloat16
F32 = jnp.float32
MESH = pl.DeviceIdType.MESH
TAPS = 27
COPIES = 64


def matmul(left, right):
    return jnp.dot(left, right, preferred_element_type=F32)


def matmul_nt(left, right):
    return lax.dot_general(left, right, (((1,), (1,)), ((), ())), preferred_element_type=F32)


def matmul_tn(left, right):
    return lax.dot_general(left, right, (((0,), (0,)), ((), ())), preferred_element_type=F32)


def slope_of(values):
    sig = jax.nn.sigmoid(values)
    return sig * (1.0 + values * (1.0 - sig))


def selection(rows, columns, column_of):
    row = lax.broadcasted_iota(jnp.int32, (rows, 128), 0)
    lane = lax.broadcasted_iota(jnp.int32, (rows, 128), 1)
    target = column_of(row)
    blocks = [
        jnp.where(target == lane + 128 * block, 1.0, 0.0).astype(BF) for block in range(columns // 128)
    ]
    return jnp.concatenate(blocks, axis=1)


def cell_of_sub(row):
    s, k = row >> 6, row & 63
    x = 2 * (k >> 4) + ((s >> 1) & 1)
    y = 2 * ((k >> 2) & 3) + (s & 1)
    z = 2 * (k & 3) + (s >> 2)
    return x, y, z


def sub_of_cell(x, y, z):
    s = (z & 1) * 4 + (x & 1) * 2 + (y & 1)
    k = ((x >> 1) * 4 + (y >> 1)) * 4 + (z >> 1)
    return s * 64 + k


def level_kernel(
    vol_hbm, cot_hbm, wc_hbm, wd_hbm, wb_hbm, wu_hbm,
    out_ref, gb_ref, gc_ref,
    vol, cot, wc, wd, wb, wu, load_sem,
    perm_xyz, perm_sub, perm_cot, perm_back, perm_out, perm_col, perm_group, perm_brick,
    plane_z, face_y, take_y, face_x, take_x,
    padded, columns, pre, cot_sub, slope_sub, hidden_sub,
    back_out, back_in, bricks, rim_out, rim_in, coarse_pad, wide, pre_low,
    grad_pad, grad_now, gface_y, gtake_y, gface_x, gtake_x,
    bottle_out, bottle_in, part_acc, part_out, part_in, fine_grad,
    gb_all, gb_one, gb_two, gb_d3, gb_three, gb_d4, gb_four, gb_d5, gb_five,
    gc_all, gc_one, gc_two, gc_e, gc_three, gc_e2, gc_four, gc_five, gc_full,
    send_sem, recv_sem,
):
    gx, gy, gz = lax.axis_index("gx"), lax.axis_index("gy"), lax.axis_index("gz")
    py, zh = gx >> 1, gx & 1
    px, core = gy >> 1, gy & 1
    used = [0]

    def remote(src, dst, device):
        slot = used[0]
        used[0] += 1
        return pltpu.make_async_remote_copy(
            src_ref=src, dst_ref=dst, send_sem=send_sem.at[slot], recv_sem=recv_sem.at[slot],
            device_id=device, device_id_type=MESH,
        )

    def around(position, step, count):
        return lax.rem(position + step, count)

    barrier = pltpu.get_barrier_semaphore()
    partners = [{"gx": around(gx, d, 8)} for d in (1, 2, 4, 6, 7)]
    partners += [{"gy": around(gy, d, 8)} for d in (1, 2, 4, 6, 7)]
    partners += [{"gz": around(gz, d, 4)} for d in (1, 2, 3)]
    for partner in partners:
        pl.semaphore_signal(barrier, inc=1, device_id=partner, device_id_type=MESH)

    loads = [
        pltpu.make_async_copy(src, dst, load_sem.at[i])
        for i, (src, dst) in enumerate(
            ((vol_hbm, vol), (cot_hbm, cot), (wu_hbm, wu), (wc_hbm, wc), (wd_hbm, wd), (wb_hbm, wb))
        )
    ]
    for load in loads:
        load.start()

    padded[...] = jnp.zeros_like(padded)
    coarse_pad[...] = jnp.zeros_like(coarse_pad)
    grad_pad[...] = jnp.zeros_like(grad_pad)
    wide[27] = jnp.zeros((256, 512), BF)
    for tap in range(TAPS, 32):
        gc_all[tap] = jnp.zeros((4, 32, 128), BF)

    @pl.when(gx == 0)
    def _():
        bricks[gz, 0:16] = jnp.zeros((16, 512), BF)

    @pl.when(gx == 7)
    def _():
        bricks[gz, 80:96] = jnp.zeros((16, 512), BF)

    def sub_to_xyz(row):
        x, y, z = cell_of_sub(row)
        return (x * 8 + y) * 8 + z

    def sub_to_zxy(row):
        x, y, z = cell_of_sub(row)
        return (z * 8 + x) * 8 + y

    perm_xyz[...] = selection(512, 512, lambda r: ((r & 7) * 8 + (r >> 6)) * 8 + ((r >> 3) & 7))
    perm_cot[...] = selection(512, 512, sub_to_zxy)

    loads[0].wait()
    pl.semaphore_wait(barrier, len(partners))

    def exchange(axis, position, count, low_src, high_dst, high_src, low_dst):
        down = remote(low_src, high_dst, {axis: around(position, count - 1, count)})
        up = remote(high_src, low_dst, {axis: around(position, 1, count)})

        @pl.when(position > 0)
        def _():
            down.start()

        @pl.when(position < count - 1)
        def _():
            up.start()

        def finish(on_low, on_high):
            @pl.when(position > 0)
            def _():
                down.wait_send()
                up.wait_recv()
                on_low()

            @pl.when(position < count - 1)
            def _():
                up.wait_send()
                down.wait_recv()
                on_high()

        return finish

    finish_z = exchange(
        "gz", gz, 4, vol.at[pl.ds(0, 64)], plane_z.at[1], vol.at[pl.ds(448, 64)], plane_z.at[0]
    )

    loads[1].wait()
    cot_sub[...] = matmul(perm_cot[...], cot[...]).astype(BF)
    loads[2].wait()
    back = jnp.zeros((64, 512), F32)
    for s in range(8):
        back = back + matmul_nt(cot_sub[pl.ds(64 * s, 64)], wu[s])
    for q in range(4):
        back_out[q] = back[:, 128 * q : 128 * (q + 1)].astype(BF)
    back_copies = []
    for d in (1, 2, 3):
        peer = around(gz, d, 4)
        copy = remote(back_out.at[peer], back_in.at[gz], {"gz": peer})
        copy.start()
        back_copies.append(copy)
    back_in[gz] = back_out[gz]

    main = matmul(perm_xyz[...], vol[...])
    padded[1:9, 1:9, 8:16, :] = main.reshape(8, 8, 8, 128)
    flat = padded.reshape(2400, 128)

    def at_row(x, y, z):
        return (x * 10 + y) * 24 + 7 + z

    def put_plane(side, z):
        plane = plane_z[side].astype(F32)
        for x in range(8):
            flat[pl.ds(at_row(x + 1, 1, z), 8, stride=24), :] = plane[8 * x : 8 * x + 8]

    finish_z(lambda: put_plane(0, 0), lambda: put_plane(1, 9))

    for side, y in ((0, 1), (1, 8)):
        face_y[side, 0:64] = padded[1:9, y, 8:16, :].reshape(64, 128).astype(BF)
        rims = [flat[pl.ds(at_row(1, y, z), 8, stride=240), :] for z in (0, 9)]
        face_y[side, 64:80] = jnp.concatenate(rims, axis=0).astype(BF)
    finish_y = exchange("gy", gy, 8, face_y.at[0], take_y.at[1], face_y.at[1], take_y.at[0])

    perm_sub[...] = selection(512, 512, sub_to_xyz)
    perm_back[...] = selection(512, 512, lambda r: sub_of_cell(r >> 6, (r >> 3) & 7, r & 7))
    perm_out[...] = selection(512, 512, lambda r: sub_of_cell((r >> 3) & 7, r & 7, r >> 6))
    perm_col[...] = selection(384, 384, lambda r: ((r & 15) >> 2) * 96 + (r >> 4) * 4 + (r & 3))
    perm_group[...] = selection(256, 256, lambda r: ((r & 15) >> 2) * 64 + (r >> 4) * 4 + (r & 3))
    perm_brick[...] = selection(256, 256, lambda r: ((r & 63) >> 2) * 16 + (r >> 6) * 4 + (r & 3))

    def put_y(side, y):
        face = take_y[side].astype(F32)
        padded[1:9, y, 8:16, :] = face[0:64].reshape(8, 8, 128)
        for i, z in enumerate((0, 9)):
            flat[pl.ds(at_row(1, y, z), 8, stride=240), :] = face[64 + 8 * i : 72 + 8 * i]

    finish_y(lambda: put_y(0, 0), lambda: put_y(1, 9))

    for side, x in ((0, 1), (1, 8)):
        face_x[side, 0:80] = padded[x, 0:10, 8:16, :].reshape(80, 128).astype(BF)
        for i, z in enumerate((0, 9)):
            first = flat[pl.ds(at_row(x, 0, z), 8, stride=24), :]
            rest = flat[pl.ds(at_row(x, 2, z), 8, stride=24), :]
            face_x[side, 80 + 16 * i : 96 + 16 * i] = jnp.concatenate([first, rest], axis=0).astype(BF)
    finish_x = exchange("gx", gx, 8, face_x.at[0], take_x.at[1], face_x.at[1], take_x.at[0])

    def put_x(side, x):
        face = take_x[side].astype(F32)
        padded[x, 0:10, 8:16, :] = face[0:80].reshape(10, 8, 128)
        for i, z in enumerate((0, 9)):
            flat[pl.ds(at_row(x, 0, z), 8, stride=24), :] = face[80 + 16 * i : 88 + 16 * i]
            flat[pl.ds(at_row(x, 2, z), 8, stride=24), :] = face[88 + 16 * i : 96 + 16 * i]

    finish_x(lambda: put_x(0, 0), lambda: put_x(1, 9))

    loads[3].wait()
    pre[...] = jnp.zeros_like(pre)
    for a in range(3):
        @pl.loop(0, 9)
        def _(step):
            b, c = step // 3, step % 3
            tap = a * 9 + step
            window = padded[pl.ds(b, 8), pl.ds(c, 8), 7 + a : 15 + a, :].reshape(512, 128).astype(BF)
            columns[tap] = window
            pre[...] += matmul(window, wc[tap])

    high = pre[...].astype(BF)
    low = (pre[...] - high.astype(F32)).astype(BF)
    pre_sub = matmul(perm_sub[...], high) + matmul(perm_sub[...], low)
    hidden_sub[...] = jax.nn.silu(pre_sub).astype(BF)
    slope_sub[...] = slope_of(pre_sub)

    loads[4].wait()
    coarse = jnp.zeros((64, 512), F32)
    for s in range(8):
        coarse = coarse + matmul(hidden_sub[pl.ds(64 * s, 64)], wd[s])
    bricks[gz, 16:80] = coarse.astype(BF)

    finish_cx = exchange(
        "gx", gx, 8,
        bricks.at[gz, pl.ds(16, 16)], bricks.at[gz, pl.ds(80, 16)],
        bricks.at[gz, pl.ds(64, 16)], bricks.at[gz, pl.ds(0, 16)],
    )
    brick_copies = []
    for d in (1, 2, 3):
        own = bricks.at[gz, pl.ds(16, 64)]
        copy = remote(own, own, {"gz": around(gz, d, 4)})
        copy.start()
        brick_copies.append(copy)
    finish_cx(lambda: None, lambda: None)
    for d in (1, 2, 3):
        for first in (0, 80):
            rim = bricks.at[gz, pl.ds(first, 16)]
            copy = remote(rim, rim, {"gz": around(gz, d, 4)})
            copy.start()
            brick_copies.append(copy)
    for copy in back_copies:
        copy.wait()
    for copy in brick_copies:
        copy.wait()

    column = matmul(perm_col[...], bricks[...].reshape(384, 512)).reshape(6, 4, 16, 512)
    coarse_pad[0:6, 1:5, 8:24, :] = column
    for side, y in ((0, 0), (1, 3)):
        rim_out[side] = column[:, y].reshape(96, 512).astype(BF)
    finish_cy = exchange("gy", gy, 8, rim_out.at[0], rim_in.at[1], rim_out.at[1], rim_in.at[0])

    back_column = matmul(perm_group[...], back_in[...].reshape(256, 128))

    def put_rim(side, y):
        coarse_pad[0:6, y, 8:24, :] = rim_in[side].astype(F32).reshape(6, 16, 512)

    finish_cy(lambda: put_rim(0, 0), lambda: put_rim(1, 5))

    loads[5].wait()
    pre_low[...] = jnp.zeros_like(pre_low)
    for a in range(3):
        @pl.loop(0, 9)
        def _(step):
            b, c = step // 3, step % 3
            tap = a * 9 + step
            window = coarse_pad[pl.ds(b, 4), pl.ds(c, 4), 7 + a : 23 + a, :].reshape(256, 512).astype(BF)
            wide[tap] = window
            pre_low[...] += matmul(window, wb[tap])

    bottle_grad = (back_column * slope_of(pre_low[...])).astype(BF)
    grad_now[...] = bottle_grad
    grad_wide = bottle_grad.astype(F32).reshape(4, 4, 16, 128)
    grad_pad[1:5, 1:5, 8:24, :] = grad_wide
    for side, y in ((0, 0), (1, 3)):
        gface_y[side] = grad_wide[:, y].reshape(64, 128).astype(BF)
    finish_gy = exchange("gy", gy, 8, gface_y.at[0], gtake_y.at[1], gface_y.at[1], gtake_y.at[0])

    bottle = jax.nn.silu(pre_low[...]).astype(BF)
    bottle_out[...] = matmul(perm_brick[...], bottle).astype(BF).reshape(4, 64, 128)
    bottle_copies = []
    for d in (1, 2, 3):
        peer = around(gz, d, 4)
        copy = remote(bottle_out.at[peer], bottle_in.at[gz], {"gz": peer})
        copy.start()
        bottle_copies.append(copy)
    bottle_in[gz] = bottle_out[gz]

    def put_gy(side, y):
        grad_pad[1:5, y, 8:24, :] = gtake_y[side].astype(F32).reshape(4, 16, 128)

    finish_gy(lambda: put_gy(0, 0), lambda: put_gy(1, 5))
    for side, x in ((0, 1), (1, 4)):
        gface_x[side] = grad_pad[x, 0:6, 8:24, :].reshape(96, 128).astype(BF)
    finish_gx = exchange("gx", gx, 8, gface_x.at[0], gtake_x.at[1], gface_x.at[1], gtake_x.at[0])

    mine, other = core * 14, (1 - core) * 14

    def bottle_taps(first):
        @pl.loop(0, 14)
        def _(step):
            term = matmul_tn(wide[first + step], grad_now[...])
            gb_all[first + step] = term.astype(BF).reshape(4, 128, 128)

    bottle_taps(other)
    gb_first = remote(gb_all.at[pl.ds(other, 14)], gb_one, {"gy": gy ^ 1})
    gb_first.start()
    bottle_taps(mine)

    def put_gx(side, x):
        grad_pad[x, 0:6, 8:24, :] = gtake_x[side].astype(F32).reshape(6, 16, 128)

    finish_gx(lambda: put_gx(0, 0), lambda: put_gx(1, 5))

    part_acc[...] = jnp.zeros_like(part_acc)
    for a in range(3):
        @pl.loop(0, 9)
        def _(step):
            b, c = step // 3, step % 3
            window = grad_pad[pl.ds(2 - b, 4), pl.ds(2 - c, 4), 9 - a : 25 - a, :].reshape(256, 128).astype(BF)
            part_acc[...] += matmul_nt(window, wb[a * 9 + step])

    part_out[...] = matmul(perm_brick[...], part_acc[...].astype(BF)).astype(BF).reshape(4, 64, 512)
    part_copies = []
    for d in (1, 2, 3):
        peer = around(gz, d, 4)
        copy = remote(part_out.at[peer], part_in.at[d - 1], {"gz": peer})
        copy.start()
        part_copies.append(copy)

    gb_first.wait()

    @pl.loop(0, 14)
    def _(step):
        total = gb_all[mine + step].astype(F32) + gb_one[step].astype(F32)
        gb_all[mine + step] = total.astype(BF)

    gb_second = []
    for d in (1, 2, 3):
        copy = remote(
            gb_all.at[pl.ds(mine, 14), around(py, d, 4)], gb_two.at[d - 1], {"gx": around(gx, 2 * d, 8)}
        )
        copy.start()
        gb_second.append(copy)

    for copy in bottle_copies:
        copy.wait()
    for s in range(8):
        lifted = jnp.zeros((64, 128), F32)
        for q in range(4):
            lifted = lifted + matmul(bottle_in[q], wu[s, pl.ds(128 * q, 128)])
        total = lifted + hidden_sub[pl.ds(64 * s, 64)].astype(F32)
        fine_grad[pl.ds(64 * s, 64)] = total.astype(BF)
    out_ref[...] = matmul(perm_out[...], fine_grad[...]).astype(BF)

    for copy in part_copies:
        copy.wait()
    coarse_grad = part_out[gz].astype(F32)
    for d in range(3):
        coarse_grad = coarse_grad + part_in[d].astype(F32)
    coarse_grad = coarse_grad.astype(BF)
    for s in range(8):
        rows = pl.ds(64 * s, 64)
        spread = matmul_nt(coarse_grad, wd[s]) + cot_sub[rows].astype(F32)
        fine_grad[rows] = (spread * slope_sub[rows]).astype(BF)
    fine_grad[...] = matmul(perm_back[...], fine_grad[...]).astype(BF)

    def fine_taps(first, count):
        @pl.loop(0, count)
        def _(step):
            term = matmul_tn(columns[first + step], fine_grad[...])
            gc_all[first + step] = term.astype(BF).reshape(4, 32, 128)

    keep, give = core * 16, (1 - core) * 16
    fine_taps(give, 16 - 5 * (1 - core))
    gc_first = remote(gc_all.at[pl.ds(give, 16)], gc_one, {"gy": gy ^ 1})
    gc_first.start()
    fine_taps(keep, 16 - 5 * core)

    for copy in gb_second:
        copy.wait()

    @pl.loop(0, 14)
    def _(step):
        total = gb_all[mine + step, py].astype(F32)
        for d in range(3):
            total = total + gb_two[d, step].astype(F32)
        gb_d3[step] = total.astype(BF).reshape(2, 4, 16, 128)

    gc_first.wait()

    @pl.loop(0, 16)
    def _(step):
        total = gc_all[keep + step].astype(F32) + gc_one[step].astype(F32)
        gc_all[keep + step] = total.astype(BF)

    gc_second = []
    for d in (1, 2, 3):
        peer = around(px, d, 4)
        copy = remote(gc_all.at[pl.ds(keep + 4 * peer, 4)], gc_two.at[d - 1], {"gy": around(gy, 2 * d, 8)})
        copy.start()
        gc_second.append(copy)
    gb_third = []
    for d in (1, 2, 3):
        copy = remote(gb_d3.at[:, :, around(px, d, 4)], gb_three.at[d - 1], {"gy": around(gy, 2 * d, 8)})
        copy.start()
        gb_third.append(copy)

    for copy in gc_second:
        copy.wait()
    total = gc_all[pl.ds(keep + 4 * px, 4)].astype(F32)
    for d in range(3):
        total = total + gc_two[d].astype(F32)
    gc_e[...] = total.astype(BF)
    gc_third = []
    for d in (1, 2, 3):
        copy = remote(gc_e.at[:, around(py, d, 4)], gc_three.at[d - 1], {"gx": around(gx, 2 * d, 8)})
        copy.start()
        gc_third.append(copy)

    for copy in gb_third:
        copy.wait()
    total = gb_d3[:, :, px].astype(F32)
    for d in range(3):
        total = total + gb_three[d].astype(F32)
    gb_d4[...] = total.astype(BF)
    gb_fourth = remote(gb_d4.at[:, 1 - zh], gb_four, {"gx": gx ^ 1})
    gb_fourth.start()

    for copy in gc_third:
        copy.wait()
    total = gc_e[:, py].astype(F32)
    for d in range(3):
        total = total + gc_three[d].astype(F32)
    gc_e2[...] = total.astype(BF).reshape(4, 2, 16, 128)
    gc_fourth = remote(gc_e2.at[:, 1 - zh], gc_four, {"gx": gx ^ 1})
    gc_fourth.start()

    gb_fourth.wait()
    gb_d5[...] = (gb_d4[:, zh].astype(F32) + gb_four[...].astype(F32)).reshape(14, 2, 8, 128)
    gb_fifth = remote(gb_d5.at[:, 1 - core], gb_five, {"gy": gy ^ 1})
    gb_fifth.start()

    gc_fourth.wait()
    gc_five[gz] = (gc_e2[:, zh].astype(F32) + gc_four[...].astype(F32)).astype(BF)
    gc_fifth = []
    for d in (1, 2, 3):
        copy = remote(gc_five.at[gz], gc_five.at[gz], {"gz": around(gz, d, 4)})
        copy.start()
        gc_fifth.append(copy)

    gb_fifth.wait()
    gb_ref[pl.ds(mine, 14)] = gb_d5[:, core]
    gb_ref[pl.ds(other, 14)] = gb_five[...]

    for copy in gc_fifth:
        copy.wait()
    total = gc_five[0].astype(F32)
    for q in (1, 2, 3):
        total = total + gc_five[q].astype(F32)
    gc_full[core, px] = total
    gathers = []
    for d in (1, 2, 3):
        copy = remote(gc_full.at[core, px], gc_full.at[core, px], {"gy": around(gy, 2 * d, 8)})
        copy.start()
        gathers.append(copy)
    for copy in gathers:
        copy.wait()
    last = remote(gc_full.at[core], gc_full.at[core], {"gy": gy ^ 1})
    last.start()
    last.wait()
    every = gc_full[...].reshape(32, 16, 128)
    chosen = jnp.zeros((32, 2, 128), F32)
    for j in range(8):
        chosen = chosen + jnp.where(gy == j, every[:, 2 * j : 2 * j + 2, :], 0.0)
    gc_ref[...] = chosen


def body(volume, cotangent, w_conv, w_down, w_bottle, w_up):
    vmem = pltpu.VMEM
    whole = pl.BlockSpec(memory_space=pl.ANY)
    held = pl.BlockSpec(memory_space=pltpu.VMEM)
    scratch = [
        vmem((512, 128), BF), vmem((512, 128), BF), vmem((27, 128, 128), BF), vmem((8, 128, 512), BF),
        vmem((27, 512, 128), BF), vmem((8, 512, 128), BF), pltpu.SemaphoreType.DMA((6,)),
        vmem((512, 512), BF), vmem((512, 512), BF), vmem((512, 512), BF), vmem((512, 512), BF),
        vmem((512, 512), BF), vmem((384, 384), BF), vmem((256, 256), BF), vmem((256, 256), BF),
        vmem((2, 64, 128), BF), vmem((2, 80, 128), BF), vmem((2, 80, 128), BF),
        vmem((2, 112, 128), BF), vmem((2, 112, 128), BF),
        vmem((10, 10, 24, 128), F32), vmem((27, 512, 128), BF), vmem((512, 128), F32),
        vmem((512, 128), BF), vmem((512, 128), F32), vmem((512, 128), BF),
        vmem((4, 64, 128), BF), vmem((4, 64, 128), BF), vmem((4, 96, 512), BF),
        vmem((2, 96, 512), BF), vmem((2, 96, 512), BF), vmem((6, 6, 32, 512), F32),
        vmem((28, 256, 512), BF), vmem((256, 128), F32),
        vmem((6, 6, 32, 128), F32), vmem((256, 128), BF), vmem((2, 64, 128), BF), vmem((2, 64, 128), BF),
        vmem((2, 96, 128), BF), vmem((2, 96, 128), BF),
        vmem((4, 64, 128), BF), vmem((4, 64, 128), BF), vmem((256, 512), F32), vmem((4, 64, 512), BF),
        vmem((3, 64, 512), BF), vmem((512, 128), BF),
        vmem((28, 4, 128, 128), BF), vmem((14, 4, 128, 128), BF), vmem((3, 14, 128, 128), BF),
        vmem((14, 2, 4, 16, 128), BF), vmem((3, 14, 2, 16, 128), BF), vmem((14, 2, 16, 128), BF),
        vmem((14, 16, 128), BF), vmem((14, 2, 8, 128), F32), vmem((14, 8, 128), F32),
        vmem((32, 4, 32, 128), BF), vmem((16, 4, 32, 128), BF), vmem((3, 4, 4, 32, 128), BF),
        vmem((4, 4, 32, 128), BF), vmem((3, 4, 32, 128), BF), vmem((4, 2, 16, 128), BF),
        vmem((4, 16, 128), BF), vmem((4, 4, 16, 128), BF), vmem((2, 4, 4, 16, 128), F32),
        pltpu.SemaphoreType.DMA((COPIES,)), pltpu.SemaphoreType.DMA((COPIES,)),
    ]
    out, gb, gc = pl.pallas_call(
        level_kernel,
        out_shape=(
            jax.ShapeDtypeStruct((512, 128), BF),
            jax.ShapeDtypeStruct((28, 8, 128), F32),
            jax.ShapeDtypeStruct((32, 2, 128), F32),
        ),
        in_specs=[whole] * 6,
        out_specs=(held,) * 3,
        scratch_shapes=scratch,
        compiler_params=pltpu.CompilerParams(
            collective_id=0, has_side_effects=True, vmem_limit_bytes=60 * 1024 * 1024
        ),
        name="level",
    )(
        volume.reshape(512, 128),
        cotangent.reshape(512, 128),
        jnp.transpose(w_conv, (1, 0, 2)),
        w_down,
        jnp.transpose(w_bottle, (1, 0, 2)),
        w_up,
    )
    return (
        out.reshape(volume.shape),
        jnp.transpose(gc[:TAPS], (1, 0, 2)),
        jnp.transpose(gb[:TAPS], (1, 0, 2)),
    )


def solution(mesh):
    in_specs = (
        P("gz", "gx", "gy", None),
        P("gz", "gx", "gy", None),
        P(),
        P(),
        P(None, None, "gz"),
        P(),
    )
    out_specs = (
        P("gz", "gx", "gy", None),
        P(("gx", "gy"), None, None),
        P(("gx", "gy"), None, "gz"),
    )
    return jax.shard_map(body, mesh=mesh, in_specs=in_specs, out_specs=out_specs, check_vma=False)
```

```python
import jax
import jax.numpy as jnp
from jax import lax
from jax.experimental import pallas as pl
from jax.experimental.pallas import tpu as pltpu
from jax.sharding import PartitionSpec as P

BF = jnp.bfloat16
F32 = jnp.float32
MESH = pl.DeviceIdType.MESH
TAPS = 27
COPIES = 96


def matmul(left, right):
    return jnp.dot(left, right, preferred_element_type=F32)


def matmul_nt(left, right):
    return lax.dot_general(left, right, (((1,), (1,)), ((), ())), preferred_element_type=F32)


def matmul_tn(left, right):
    return lax.dot_general(left, right, (((0,), (0,)), ((), ())), preferred_element_type=F32)


def slope_of(values):
    sig = jax.nn.sigmoid(values)
    return sig * (1.0 + values * (1.0 - sig))


def selection(rows, columns, column_of):
    row = lax.broadcasted_iota(jnp.int32, (rows, 128), 0)
    lane = lax.broadcasted_iota(jnp.int32, (rows, 128), 1)
    target = column_of(row)
    blocks = [
        jnp.where(target == lane + 128 * block, 1.0, 0.0).astype(BF) for block in range(columns // 128)
    ]
    return jnp.concatenate(blocks, axis=1)


def cell_of_sub(row):
    s, k = row >> 6, row & 63
    x = 2 * (k >> 4) + ((s >> 1) & 1)
    y = 2 * ((k >> 2) & 3) + (s & 1)
    z = 2 * (k & 3) + (s >> 2)
    return x, y, z


def sub_of_cell(x, y, z):
    s = (z & 1) * 4 + (x & 1) * 2 + (y & 1)
    k = ((x >> 1) * 4 + (y >> 1)) * 4 + (z >> 1)
    return s * 64 + k


def level_kernel(
    vol_hbm, cot_hbm, wc_hbm, wd_hbm, wb_hbm, wu_hbm,
    out_ref, gb_ref, gc_ref,
    vol, cot, wc, wd, wb, wu, load_sem,
    perm_xyz, perm_sub, perm_cot, perm_back, perm_out, perm_group, perm_rim, perm_brick, lift_z,
    plane_z, face_y, take_y, face_x, take_x,
    padded, columns, turned, pre, cot_sub, slope_sub, hidden_sub,
    back_out, back_in, bricks, rims, shifted, rim_out, rim_in, corner_out, corner_in, pre_low,
    grad_now, grad_shift, gface_y, gtake_y, gface_x, gtake_x,
    bottle_out, bottle_in, part_acc, part_out, part_in, fine_grad,
    gb_all, gb_one, gb_ya, gb_xb, gb_a, gb_b, gb_xa, gb_yb, gb_d4, gb_four, gb_d5, gb_five, gb_rows,
    gc_all, gc_one, gc_xa, gc_yb, gc_a, gc_b, gc_ya, gc_xb, gc_e2, gc_z, gc_half, gc_g,
    send_sem, recv_sem,
):
    gx, gy, gz = lax.axis_index("gx"), lax.axis_index("gy"), lax.axis_index("gz")
    py, zh = gx >> 1, gx & 1
    px, core = gy >> 1, gy & 1
    used = [0]

    def remote(src, dst, device):
        slot = used[0]
        used[0] += 1
        return pltpu.make_async_remote_copy(
            src_ref=src, dst_ref=dst, send_sem=send_sem.at[slot], recv_sem=recv_sem.at[slot],
            device_id=device, device_id_type=MESH,
        )

    def around(position, step, count):
        return lax.rem(position + step, count)

    barrier = pltpu.get_barrier_semaphore()
    partners = [{"gx": around(gx, d, 8)} for d in (1, 2, 4, 6, 7)]
    partners += [{"gy": around(gy, d, 8)} for d in range(1, 8)]
    partners += [{"gz": around(gz, d, 4)} for d in (1, 2, 3)]
    partners += [{"gx": gx ^ 1, "gz": around(gz, d, 4)} for d in (1, 2, 3)]
    for partner in partners:
        pl.semaphore_signal(barrier, inc=1, device_id=partner, device_id_type=MESH)

    loads = [
        pltpu.make_async_copy(src, dst, load_sem.at[i])
        for i, (src, dst) in enumerate(
            ((vol_hbm, vol), (cot_hbm, cot), (wu_hbm, wu), (wc_hbm, wc), (wd_hbm, wd), (wb_hbm, wb))
        )
    ]
    for load in loads:
        load.start()

    padded[...] = jnp.zeros_like(padded)
    for side in (0, 5):
        for a in range(3):
            shifted[a, side] = jnp.zeros((6, 16, 512), BF)
            grad_shift[a, side] = jnp.zeros((6, 16, 128), BF)
    for tap in range(TAPS, 32):
        gc_all[tap] = jnp.zeros((4, 32, 128), BF)
    gb_all[27] = jnp.zeros((4, 2, 4, 16, 128), BF)
    corner_in[2:4] = jnp.zeros((2, 32, 512), BF)
    for side in range(2):
        gtake_x[side, 96:128] = jnp.zeros((32, 128), BF)

    for side, edge in ((0, 0), (1, 7)):
        @pl.when(gx == edge)
        def _():
            rims[gz, 16 * side : 16 * side + 16] = jnp.zeros((16, 512), BF)
            gtake_x[side, 0:96] = jnp.zeros((96, 128), BF)

        @pl.when(gy == edge)
        def _():
            rim_in[side] = jnp.zeros((64, 512), BF)
            corner_in[side] = jnp.zeros((32, 512), BF)
            gtake_y[side] = jnp.zeros((64, 128), BF)

    def sub_to_xyz(row):
        x, y, z = cell_of_sub(row)
        return (x * 8 + y) * 8 + z

    def sub_to_zxy(row):
        x, y, z = cell_of_sub(row)
        return (z * 8 + x) * 8 + y

    perm_xyz[...] = selection(512, 512, lambda r: ((r & 7) * 8 + (r >> 6)) * 8 + ((r >> 3) & 7))
    perm_cot[...] = selection(512, 512, sub_to_zxy)

    loads[0].wait()
    pl.semaphore_wait(barrier, len(partners))

    def exchange(axis, position, count, low_src, high_dst, high_src, low_dst):
        down = remote(low_src, high_dst, {axis: around(position, count - 1, count)})
        up = remote(high_src, low_dst, {axis: around(position, 1, count)})

        @pl.when(position > 0)
        def _():
            down.start()

        @pl.when(position < count - 1)
        def _():
            up.start()

        def finish(on_low, on_high):
            @pl.when(position > 0)
            def _():
                down.wait_send()
                up.wait_recv()
                on_low()

            @pl.when(position < count - 1)
            def _():
                up.wait_send()
                down.wait_recv()
                on_high()

        return finish

    finish_z = exchange(
        "gz", gz, 4, vol.at[pl.ds(0, 64)], plane_z.at[1], vol.at[pl.ds(448, 64)], plane_z.at[0]
    )

    loads[1].wait()
    cot_sub[...] = matmul(perm_cot[...], cot[...]).astype(BF)
    loads[2].wait()
    back = jnp.zeros((64, 512), F32)
    for s in range(8):
        back = back + matmul_nt(cot_sub[pl.ds(64 * s, 64)], wu[s])
    for q in range(4):
        back_out[q] = back[:, 128 * q : 128 * (q + 1)].astype(BF)
    back_copies = []
    for d in (1, 2, 3):
        peer = around(gz, d, 4)
        copy = remote(back_out.at[peer], back_in.at[gz], {"gz": peer})
        copy.start()
        back_copies.append(copy)
    back_in[gz] = back_out[gz]

    main = matmul(perm_xyz[...], vol[...])
    padded[1:9, 1:9, 8:16, :] = main.reshape(8, 8, 8, 128)
    flat = padded.reshape(2400, 128)

    def at_row(x, y, z):
        return (x * 10 + y) * 24 + 7 + z

    def put_plane(side, z):
        plane = plane_z[side].astype(F32)
        for x in range(8):
            flat[pl.ds(at_row(x + 1, 1, z), 8, stride=24), :] = plane[8 * x : 8 * x + 8]

    finish_z(lambda: put_plane(0, 0), lambda: put_plane(1, 9))

    for side, y in ((0, 1), (1, 8)):
        face_y[side, 0:64] = padded[1:9, y, 8:16, :].reshape(64, 128).astype(BF)
        edges = [flat[pl.ds(at_row(1, y, z), 8, stride=240), :] for z in (0, 9)]
        face_y[side, 64:80] = jnp.concatenate(edges, axis=0).astype(BF)
    finish_y = exchange("gy", gy, 8, face_y.at[0], take_y.at[1], face_y.at[1], take_y.at[0])

    perm_sub[...] = selection(512, 512, sub_to_xyz)
    perm_back[...] = selection(512, 512, lambda r: sub_of_cell(r >> 6, (r >> 3) & 7, r & 7))
    perm_out[...] = selection(512, 512, lambda r: sub_of_cell((r >> 3) & 7, r & 7, r >> 6))

    def shifted_z(r, shift, column_of):
        z = (r & 15) + shift
        return jnp.where((z < 0) | (z > 15), -1, column_of(r, z & 15))

    for a in range(3):
        perm_group[a] = selection(
            256, 256, lambda r: shifted_z(r, a - 1, lambda r, z: (z >> 2) * 64 + (r >> 4) * 4 + (z & 3))
        )
        perm_rim[a] = selection(
            128, 128, lambda r: shifted_z(r, a - 1, lambda r, z: (z >> 2) * 32 + (r >> 4) * 4 + (z & 3))
        )
        lift_z[a] = selection(128, 128, lambda r: shifted_z(r, a - 1, lambda r, z: r - (r & 15) + z))
    perm_brick[...] = selection(256, 256, lambda r: ((r & 63) >> 2) * 16 + (r >> 6) * 4 + (r & 3))

    def put_y(side, y):
        face = take_y[side].astype(F32)
        padded[1:9, y, 8:16, :] = face[0:64].reshape(8, 8, 128)
        for i, z in enumerate((0, 9)):
            flat[pl.ds(at_row(1, y, z), 8, stride=240), :] = face[64 + 8 * i : 72 + 8 * i]

    finish_y(lambda: put_y(0, 0), lambda: put_y(1, 9))

    for side, x in ((0, 1), (1, 8)):
        face_x[side, 0:80] = padded[x, 0:10, 8:16, :].reshape(80, 128).astype(BF)
        for i, z in enumerate((0, 9)):
            first = flat[pl.ds(at_row(x, 0, z), 8, stride=24), :]
            rest = flat[pl.ds(at_row(x, 2, z), 8, stride=24), :]
            face_x[side, 80 + 16 * i : 96 + 16 * i] = jnp.concatenate([first, rest], axis=0).astype(BF)
    finish_x = exchange("gx", gx, 8, face_x.at[0], take_x.at[1], face_x.at[1], take_x.at[0])

    def put_x(side, x):
        face = take_x[side].astype(F32)
        padded[x, 0:10, 8:16, :] = face[0:80].reshape(10, 8, 128)
        for i, z in enumerate((0, 9)):
            flat[pl.ds(at_row(x, 0, z), 8, stride=24), :] = face[80 + 16 * i : 88 + 16 * i]
            flat[pl.ds(at_row(x, 2, z), 8, stride=24), :] = face[88 + 16 * i : 96 + 16 * i]

    finish_x(lambda: put_x(0, 0), lambda: put_x(1, 9))

    loads[3].wait()
    pre[...] = jnp.zeros_like(pre)

    @pl.loop(0, 9)
    def _(step):
        b, c = step // 3, step % 3
        windows = [
            padded[pl.ds(b, 8), pl.ds(c, 8), 7 + a : 15 + a, :].reshape(512, 128).astype(BF) for a in range(3)
        ]
        for a in range(3):
            columns[a * 9 + step] = windows[a]
        weights = jnp.concatenate([wc[a * 9 + step] for a in range(3)], axis=0)
        pre[...] += matmul(jnp.concatenate(windows, axis=1), weights)

    high = pre[...].astype(BF)
    low = (pre[...] - high.astype(F32)).astype(BF)
    pre_sub = matmul(perm_sub[...], high) + matmul(perm_sub[...], low)
    hidden_sub[...] = jax.nn.silu(pre_sub).astype(BF)
    slope_sub[...] = slope_of(pre_sub)

    loads[4].wait()
    coarse = jnp.zeros((64, 512), F32)
    for s in range(8):
        coarse = coarse + matmul(hidden_sub[pl.ds(64 * s, 64)], wd[s])
    bricks[gz] = coarse.astype(BF)

    finish_cx = exchange(
        "gx", gx, 8,
        bricks.at[gz, pl.ds(0, 16)], rims.at[gz, pl.ds(16, 16)],
        bricks.at[gz, pl.ds(48, 16)], rims.at[gz, pl.ds(0, 16)],
    )

    def send_column(ref):
        copies = []
        for d in (1, 2, 3):
            copy = remote(ref.at[gz], ref.at[gz], {"gz": around(gz, d, 4)})
            copy.start()
            copies.append(copy)
        return copies

    brick_copies = send_column(bricks)

    def turn(first, last):
        @pl.loop(first, last)
        def _(tap):
            turned[tap] = columns[tap].T

    turn(0, 16)
    finish_cx(lambda: None, lambda: None)
    rim_copies = send_column(rims)
    turn(16, 27)

    for copy in brick_copies:
        copy.wait()
    stack = bricks[...].reshape(256, 512)
    middle = matmul(perm_group[1], stack).astype(BF).reshape(4, 4, 16, 512)
    for side, y in ((0, 0), (1, 3)):
        rim_out[side] = middle[:, y].reshape(64, 512)
    finish_cy = exchange("gy", gy, 8, rim_out.at[0], rim_in.at[1], rim_out.at[1], rim_in.at[0])
    shifted[1, 1:5, 1:5] = middle
    for a in (0, 2):
        shifted[a, 1:5, 1:5] = matmul(perm_group[a], stack).astype(BF).reshape(4, 4, 16, 512)
    for copy in back_copies:
        copy.wait()
    back_column = matmul(perm_group[1], back_in[...].reshape(256, 128))

    loads[5].wait()
    finish_cy(lambda: None, lambda: None)
    for a in range(3):
        sides = matmul(lift_z[a], rim_in[...].reshape(128, 512)).astype(BF).reshape(2, 4, 16, 512)
        shifted[a, 1:5, 0] = sides[0]
        shifted[a, 1:5, 5] = sides[1]

    pre_low[...] = jnp.zeros_like(pre_low)

    def low_taps(first, last):
        @pl.loop(first, last)
        def _(step):
            b, c = step // 3, step % 3
            total = pre_low[...]
            for a in range(3):
                window = shifted[a, pl.ds(b, 4), pl.ds(c, 4)].reshape(256, 512)
                total = total + matmul(window, wb[a * 9 + step])
            pre_low[...] = total

    low_taps(0, 6)
    for copy in rim_copies:
        copy.wait()
    rim_rows = []
    for a in range(3):
        rim_rows.append(matmul(perm_rim[a], rims[...].reshape(128, 512)).astype(BF).reshape(2, 4, 16, 512))
    for side, y in ((0, 0), (1, 3)):
        corner_out[side] = rim_rows[1][:, y].reshape(32, 512)
    finish_cc = exchange("gy", gy, 8, corner_out.at[0], corner_in.at[1], corner_out.at[1], corner_in.at[0])
    low_taps(6, 9)
    for a in range(3):
        shifted[a, 0, 1:5] = rim_rows[a][0]
        shifted[a, 5, 1:5] = rim_rows[a][1]
    finish_cc(lambda: None, lambda: None)
    for a in range(3):
        corners = matmul(lift_z[a], corner_in[...].reshape(128, 512)).astype(BF).reshape(4, 2, 16, 512)
        for i, y in ((0, 0), (1, 5)):
            shifted[a, 0, y] = corners[i, 0]
            shifted[a, 5, y] = corners[i, 1]

    @pl.loop(0, 3)
    def _(c):
        low, high = pre_low[0:64], pre_low[192:256]
        for a in range(3):
            low = low + matmul(shifted[a, 0, pl.ds(c, 4)].reshape(64, 512), wb[a * 9 + c])
            high = high + matmul(shifted[a, 5, pl.ds(c, 4)].reshape(64, 512), wb[a * 9 + 6 + c])
        pre_low[0:64] = low
        pre_low[192:256] = high

    bottle_grad = (back_column * slope_of(pre_low[...])).astype(BF)
    grad_now[...] = bottle_grad
    middle = bottle_grad.astype(F32).reshape(4, 4, 16, 128)
    for side, y in ((0, 0), (1, 3)):
        gface_y[side] = middle[:, y].reshape(64, 128).astype(BF)
    finish_gy = exchange("gy", gy, 8, gface_y.at[0], gtake_y.at[1], gface_y.at[1], gtake_y.at[0])

    bottle = jax.nn.silu(pre_low[...]).astype(BF)
    bottle_out[...] = matmul(perm_brick[...], bottle).astype(BF).reshape(4, 64, 128)
    bottle_copies = []
    for d in (1, 2, 3):
        peer = around(gz, d, 4)
        copy = remote(bottle_out.at[peer], bottle_in.at[gz], {"gz": peer})
        copy.start()
        bottle_copies.append(copy)
    bottle_in[gz] = bottle_out[gz]

    for a in range(3):
        for half in range(2):
            moved = matmul(lift_z[a], grad_now[pl.ds(128 * half, 128)]).astype(BF)
            grad_shift[a, 1 + 2 * half : 3 + 2 * half, 1:5] = moved.reshape(2, 4, 16, 128)

    mine, other = core * 14, (1 - core) * 14

    def bottle_taps(first, last, base):
        @pl.loop(first, last)
        def _(step):
            tap = base + step
            depth, across = tap // 9, tap % 9
            b, c = across // 3, across % 3
            window = shifted[depth, pl.ds(b, 4), pl.ds(c, 4)].reshape(256, 512)
            gb_all[tap] = matmul_tn(window, grad_now[...]).astype(BF).reshape(4, 2, 4, 16, 128)

    bottle_taps(0, 8, other)
    finish_gy(lambda: None, lambda: None)
    for a in range(3):
        sides = matmul(lift_z[a], gtake_y[...].reshape(128, 128)).astype(BF).reshape(2, 4, 16, 128)
        grad_shift[a, 1:5, 0] = sides[0]
        grad_shift[a, 1:5, 5] = sides[1]
    for side, x in ((0, 1), (1, 4)):
        gface_x[side] = grad_shift[1, x].reshape(96, 128)
    finish_gx = exchange(
        "gx", gx, 8,
        gface_x.at[0], gtake_x.at[1, pl.ds(0, 96)], gface_x.at[1], gtake_x.at[0, pl.ds(0, 96)],
    )

    part_acc[...] = jnp.zeros_like(part_acc)

    @pl.loop(0, 9)
    def _(step):
        b, c = step // 3, step % 3
        windows = [grad_shift[2 - a, pl.ds(2 - b, 4), pl.ds(2 - c, 4)].reshape(256, 128) for a in range(3)]
        weights = jnp.concatenate([wb[a * 9 + step] for a in range(3)], axis=1)
        part_acc[...] += matmul_nt(jnp.concatenate(windows, axis=1), weights)

    finish_gx(lambda: None, lambda: None)
    for a in range(3):
        for side, x in ((0, 0), (1, 5)):
            moved = matmul(lift_z[a], gtake_x[side]).astype(BF)
            grad_shift[a, x] = moved[0:96].reshape(6, 16, 128)

    @pl.loop(0, 3)
    def _(c):
        for x, rows, b in ((0, 0, 2), (5, 192, 0)):
            windows = [grad_shift[2 - a, x, pl.ds(2 - c, 4)].reshape(64, 128) for a in range(3)]
            weights = jnp.concatenate([wb[a * 9 + 3 * b + c] for a in range(3)], axis=1)
            part_acc[rows : rows + 64] += matmul_nt(jnp.concatenate(windows, axis=1), weights)

    part_out[...] = matmul(perm_brick[...], part_acc[...].astype(BF)).astype(BF).reshape(4, 64, 512)
    part_copies = []
    for d in (1, 2, 3):
        peer = around(gz, d, 4)
        copy = remote(part_out.at[peer], part_in.at[d - 1], {"gz": peer})
        copy.start()
        part_copies.append(copy)

    bottle_taps(8, 13 + core, other)
    gb_first = remote(gb_all.at[pl.ds(other, 14)], gb_one, {"gy": gy ^ 1})
    gb_first.start()
    bottle_taps(0, 14 - core, mine)

    for copy in bottle_copies:
        copy.wait()
    for s in range(8):
        lifted = jnp.zeros((64, 128), F32)
        for q in range(4):
            lifted = lifted + matmul(bottle_in[q], wu[s, pl.ds(128 * q, 128)])
        total = lifted + hidden_sub[pl.ds(64 * s, 64)].astype(F32)
        fine_grad[pl.ds(64 * s, 64)] = total.astype(BF)
    out_ref[...] = matmul(perm_out[...], fine_grad[...]).astype(BF)

    gb_first.wait()

    @pl.loop(0, 14)
    def _(step):
        total = gb_all[mine + step].astype(F32) + gb_one[step].astype(F32)
        gb_all[mine + step] = total.astype(BF)

    def along_y(source_of, target):
        copies = []
        for d in (1, 2, 3):
            copy = remote(source_of(around(py, d, 4)), target.at[d - 1], {"gx": around(gx, 2 * d, 8)})
            copy.start()
            copies.append(copy)
        return copies

    def along_x(source_of, target):
        copies = []
        for d in (1, 2, 3):
            copy = remote(source_of(around(px, d, 4)), target.at[d - 1], {"gy": around(gy, 2 * d, 8)})
            copy.start()
            copies.append(copy)
        return copies

    gb_second = along_y(lambda y: gb_all.at[pl.ds(mine, 7), y], gb_ya)
    gb_second += along_x(lambda x: gb_all.at[pl.ds(mine + 7, 7), :, :, x], gb_xb)

    for copy in part_copies:
        copy.wait()
    coarse_grad = part_out[gz].astype(F32)
    for d in range(3):
        coarse_grad = coarse_grad + part_in[d].astype(F32)
    coarse_grad = coarse_grad.astype(BF)
    for s in range(8):
        rows = pl.ds(64 * s, 64)
        spread = matmul_nt(coarse_grad, wd[s]) + cot_sub[rows].astype(F32)
        fine_grad[rows] = (spread * slope_sub[rows]).astype(BF)
    fine_grad[...] = matmul(perm_back[...], fine_grad[...]).astype(BF)

    def fine_taps(first, last, base):
        @pl.loop(first, last)
        def _(step):
            term = matmul(turned[base + step], fine_grad[...])
            gc_all[base + step] = term.astype(BF).reshape(4, 32, 128)

    keep, give = core * 16, (1 - core) * 16
    fine_taps(0, 16 - 5 * (1 - core), give)
    gc_first = remote(gc_all.at[pl.ds(give, 16)], gc_one, {"gy": gy ^ 1})
    gc_first.start()
    fine_taps(0, 16 - 5 * core, keep)

    gc_first.wait()

    @pl.loop(0, 16)
    def _(step):
        total = gc_all[keep + step].astype(F32) + gc_one[step].astype(F32)
        gc_all[keep + step] = total.astype(BF)

    gc_second = along_x(lambda x: gc_all.at[pl.ds(keep + 2 * x, 2)], gc_xa)
    gc_second += along_y(lambda y: gc_all.at[pl.ds(keep + 8, 8), y], gc_yb)

    def summed(own, taken):
        total = own.astype(F32)
        for d in range(3):
            total = total + taken[d].astype(F32)
        return total

    for copy in gb_second:
        copy.wait()

    @pl.loop(0, 7)
    def _(step):
        total = gb_all[mine + step, py].astype(F32)
        other_half = gb_all[mine + 7 + step, :, :, px].astype(F32)
        for d in range(3):
            total = total + gb_ya[d, step].astype(F32)
            other_half = other_half + gb_xb[d, step].astype(F32)
        gb_a[step] = total.astype(BF)
        gb_b[step] = other_half.astype(BF)

    gb_third = along_x(lambda x: gb_a.at[:, :, x], gb_xa)
    gb_third += along_y(lambda y: gb_b.at[:, y], gb_yb)

    for copy in gc_second:
        copy.wait()
    gc_a[...] = summed(gc_all[pl.ds(keep + 2 * px, 2)], gc_xa).astype(BF)
    gc_b[...] = summed(gc_all[pl.ds(keep + 8, 8), py], gc_yb).astype(BF)
    gc_third = along_y(lambda y: gc_a.at[:, y], gc_ya)
    gc_third += along_x(lambda x: gc_b.at[pl.ds(2 * x, 2)], gc_xb)

    for copy in gb_third:
        copy.wait()
    gb_d4[0:7] = summed(gb_a[:, :, px], gb_xa).astype(BF)
    gb_d4[7:14] = summed(gb_b[:, py], gb_yb).astype(BF)
    gb_fourth = remote(gb_d4.at[:, 1 - zh], gb_four, {"gx": gx ^ 1})
    gb_fourth.start()

    for copy in gc_third:
        copy.wait()
    gc_e2[0:2] = summed(gc_a[:, py], gc_ya).astype(BF).reshape(2, 2, 16, 128)
    gc_e2[2:4] = summed(gc_b[pl.ds(2 * px, 2)], gc_xb).astype(BF).reshape(2, 2, 16, 128)
    slot = zh * 4 + gz
    gc_fourth = []
    for d in range(4):
        peer = around(gz, d, 4)
        copy = remote(gc_e2.at[:, 1 - zh], gc_z.at[slot], {"gx": gx ^ 1, "gz": peer})
        copy.start()
        gc_fourth.append(copy)
        if d > 0:
            copy = remote(gc_e2.at[:, zh], gc_z.at[slot], {"gz": peer})
            copy.start()
            gc_fourth.append(copy)
    gc_z[slot] = gc_e2[:, zh]

    gb_fourth.wait()
    gb_d5[...] = (gb_d4[:, zh].astype(F32) + gb_four[...].astype(F32)).reshape(14, 2, 8, 128)
    gb_fifth = remote(gb_d5.at[:, 1 - core], gb_five, {"gy": gy ^ 1})
    gb_fifth.start()

    for copy in gc_fourth:
        copy.wait()
    total = gc_z[0].astype(F32)
    for q in range(1, 8):
        total = total + gc_z[q].astype(F32)
    for half in range(2):
        gc_half[half] = total[:, 8 * half : 8 * half + 8]
    gathers = []
    for d in range(1, 8):
        peer = around(gy, d, 8)
        copy = remote(gc_half.at[peer >> 2], gc_g.at[gy], {"gy": peer})
        copy.start()
        gathers.append(copy)
    gc_g[gy] = gc_half[gy >> 2]

    gb_fifth.wait()
    for step in range(14):
        gb_rows[pl.ds(mine + step, 8, stride=32), :] = gb_d5[step, core]
        gb_rows[pl.ds(other + step, 8, stride=32), :] = gb_five[step]
    gb_ref[...] = gb_rows[...].reshape(8, 32, 128)[:, 0:TAPS]

    for copy in gathers:
        copy.wait()
    place = gy & 3
    for source in range(8):
        block = gc_g[source]
        chosen = jnp.zeros((4, 2, 128), F32)
        for j in range(4):
            chosen = chosen + jnp.where(place == j, block[:, 2 * j : 2 * j + 2, :], 0.0)
        first = (source & 1) * 16 + (source >> 1) * 2
        gc_ref[first : first + 2] = chosen[0:2]
        gc_ref[first + 8 : first + 10] = chosen[2:4]


def deliver_kernel(out_ref, gb_ref, out_final, gb_final):
    out_final[...] = out_ref[...]
    gb_final[...] = gb_ref[...]


def body(volume, cotangent, w_conv, w_down, w_bottle, w_up):
    vmem = pltpu.VMEM
    whole = pl.BlockSpec(memory_space=pl.ANY)
    held = pl.BlockSpec(memory_space=pltpu.VMEM)
    def kept(*shape):
        return vmem(shape, BF)

    scratch = [
        kept(512, 128), kept(512, 128), kept(27, 128, 128), kept(8, 128, 512),
        kept(27, 512, 128), kept(8, 512, 128), pltpu.SemaphoreType.DMA((6,)),
        kept(512, 512), kept(512, 512), kept(512, 512), kept(512, 512), kept(512, 512),
        kept(3, 256, 256), kept(3, 128, 128), kept(256, 256), kept(3, 128, 128),
        kept(2, 64, 128), kept(2, 80, 128), kept(2, 80, 128), kept(2, 112, 128), kept(2, 112, 128),
        vmem((10, 10, 24, 128), F32), kept(27, 512, 128), kept(27, 128, 512), vmem((512, 128), F32),
        kept(512, 128), vmem((512, 128), F32), kept(512, 128),
        kept(4, 64, 128), kept(4, 64, 128), kept(4, 64, 512), kept(4, 32, 512), kept(3, 6, 6, 16, 512),
        kept(2, 64, 512), kept(2, 64, 512), kept(2, 32, 512), kept(4, 32, 512), vmem((256, 128), F32),
        kept(256, 128), kept(3, 6, 6, 16, 128), kept(2, 64, 128), kept(2, 64, 128),
        kept(2, 96, 128), kept(2, 128, 128),
        kept(4, 64, 128), kept(4, 64, 128), vmem((256, 512), F32), kept(4, 64, 512),
        kept(3, 64, 512), kept(512, 128),
        kept(28, 4, 2, 4, 16, 128), kept(14, 4, 2, 4, 16, 128), kept(3, 7, 2, 4, 16, 128), kept(3, 7, 4, 2, 16, 128),
        kept(7, 2, 4, 16, 128), kept(7, 4, 2, 16, 128), kept(3, 7, 2, 16, 128), kept(3, 7, 2, 16, 128),
        kept(14, 2, 16, 128), kept(14, 16, 128), vmem((14, 2, 8, 128), F32), vmem((14, 8, 128), F32),
        vmem((256, 128), F32),
        kept(32, 4, 32, 128), kept(16, 4, 32, 128), kept(3, 2, 4, 32, 128), kept(3, 8, 32, 128),
        kept(2, 4, 32, 128), kept(8, 32, 128), kept(3, 2, 32, 128), kept(3, 2, 32, 128),
        kept(4, 2, 16, 128), kept(8, 4, 16, 128), vmem((2, 4, 8, 128), F32), vmem((8, 4, 8, 128), F32),
        pltpu.SemaphoreType.DMA((COPIES,)), pltpu.SemaphoreType.DMA((COPIES,)),
    ]
    out, gb, gc = pl.pallas_call(
        level_kernel,
        out_shape=(
            jax.ShapeDtypeStruct((512, 128), BF),
            jax.ShapeDtypeStruct((8, TAPS, 128), F32),
            jax.ShapeDtypeStruct((32, 2, 128), F32),
        ),
        in_specs=[whole] * 6,
        out_specs=(held,) * 3,
        scratch_shapes=scratch,
        compiler_params=pltpu.CompilerParams(
            collective_id=0, has_side_effects=True, vmem_limit_bytes=60 * 1024 * 1024
        ),
        name="level",
    )(
        volume.reshape(512, 128),
        cotangent.reshape(512, 128),
        jnp.transpose(w_conv, (1, 0, 2)),
        w_down,
        jnp.transpose(w_bottle, (1, 0, 2)),
        w_up,
    )
    out, gb = pl.pallas_call(
        deliver_kernel,
        out_shape=(jax.ShapeDtypeStruct(out.shape, BF), jax.ShapeDtypeStruct(gb.shape, F32)),
        in_specs=[held] * 2,
        out_specs=(held,) * 2,
        name="deliver",
    )(out, gb)
    return out.reshape(volume.shape), jnp.transpose(gc[:TAPS], (1, 0, 2)), gb


def solution(mesh):
    in_specs = (
        P("gz", "gx", "gy", None),
        P("gz", "gx", "gy", None),
        P(),
        P(),
        P(None, None, "gz"),
        P(),
    )
    out_specs = (
        P("gz", "gx", "gy", None),
        P(("gx", "gy"), None, None),
        P(("gx", "gy"), None, "gz"),
    )
    return jax.shard_map(body, mesh=mesh, in_specs=in_specs, out_specs=out_specs, check_vma=False)
```

```python
import jax
import jax.numpy as jnp
from jax import lax
from jax.experimental import pallas as pl
from jax.experimental.pallas import tpu as pltpu
from jax.sharding import PartitionSpec as P

BF = jnp.bfloat16
F32 = jnp.float32
MESH = pl.DeviceIdType.MESH
TAPS = 27
COPIES = 96


def matmul(left, right):
    return jnp.dot(left, right, preferred_element_type=F32)


def matmul_nt(left, right):
    return lax.dot_general(left, right, (((1,), (1,)), ((), ())), preferred_element_type=F32)


def matmul_tn(left, right):
    return lax.dot_general(left, right, (((0,), (0,)), ((), ())), preferred_element_type=F32)


def slope_of(values):
    sig = jax.nn.sigmoid(values)
    return sig * (1.0 + values * (1.0 - sig))


def selection(rows, columns, column_of):
    row = lax.broadcasted_iota(jnp.int32, (rows, 128), 0)
    lane = lax.broadcasted_iota(jnp.int32, (rows, 128), 1)
    target = column_of(row)
    blocks = [
        jnp.where(target == lane + 128 * block, 1.0, 0.0).astype(BF) for block in range(columns // 128)
    ]
    return jnp.concatenate(blocks, axis=1)


def cell_of_sub(row):
    s, k = row >> 6, row & 63
    x = 2 * (k >> 4) + ((s >> 1) & 1)
    y = 2 * ((k >> 2) & 3) + (s & 1)
    z = 2 * (k & 3) + (s >> 2)
    return x, y, z


def sub_of_cell(x, y, z):
    s = (z & 1) * 4 + (x & 1) * 2 + (y & 1)
    k = ((x >> 1) * 4 + (y >> 1)) * 4 + (z >> 1)
    return s * 64 + k


def level_kernel(
    vol_hbm, cot_hbm, wc_hbm, wd_hbm, wb_hbm, wu_hbm,
    out_ref, gb_ref, gc_ref,
    vol, cot, wc, wd, wb, wu, load_sem,
    perm_xyz, perm_sub, perm_cot, perm_back, perm_out, perm_group, perm_rim, perm_brick, lift_z,
    plane_z, face_y, take_y, face_x, take_x,
    padded, columns, turned, pre, cot_sub, slope_sub, hidden_sub,
    back_out, back_in, bricks, rims, shifted, rim_out, rim_in, corner_out, corner_in, pre_low,
    grad_now, grad_shift, gface_y, gtake_y, gface_x, gtake_x,
    bottle_out, bottle_in, part_acc, part_out, part_in, fine_grad,
    gb_all, gb_one, gb_ya, gb_ya2, gb_xb, gb_xb2, gb_a, gb_b, gb_xa, gb_xa2, gb_yb, gb_yb2, gb_d4, gb_four, gb_d5, gb_five,
    gc_all, gc_one, gc_xa, gc_yb, gc_a, gc_b, gc_ya, gc_xb, gc_e2, gc_z, gc_half, gc_g,
    send_sem, recv_sem,
):
    gx, gy, gz = lax.axis_index("gx"), lax.axis_index("gy"), lax.axis_index("gz")
    py, zh = gx >> 1, gx & 1
    px, core = gy >> 1, gy & 1
    used = [0]

    def remote(src, dst, device):
        slot = used[0]
        used[0] += 1
        return pltpu.make_async_remote_copy(
            src_ref=src, dst_ref=dst, send_sem=send_sem.at[slot], recv_sem=recv_sem.at[slot],
            device_id=device, device_id_type=MESH,
        )

    def around(position, step, count):
        return lax.rem(position + step, count)

    barrier = pltpu.get_barrier_semaphore()
    partners = [{"gx": around(gx, d, 8)} for d in (1, 2, 4, 6, 7)]
    partners += [{"gy": around(gy, d, 8)} for d in range(1, 8)]
    partners += [{"gz": around(gz, d, 4)} for d in (1, 2, 3)]
    partners += [{"gx": gx ^ 1, "gz": around(gz, d, 4)} for d in (1, 2, 3)]
    for partner in partners:
        pl.semaphore_signal(barrier, inc=1, device_id=partner, device_id_type=MESH)

    loads = [
        pltpu.make_async_copy(src, dst, load_sem.at[i])
        for i, (src, dst) in enumerate(
            ((vol_hbm, vol), (cot_hbm, cot), (wu_hbm, wu), (wc_hbm, wc), (wd_hbm, wd), (wb_hbm, wb))
        )
    ]
    for load in loads:
        load.start()

    padded[...] = jnp.zeros_like(padded)
    for side in (0, 5):
        for a in range(3):
            shifted[a, side] = jnp.zeros((6, 16, 512), BF)
            grad_shift[a, side] = jnp.zeros((6, 16, 128), BF)
    for tap in range(TAPS, 32):
        turned[tap] = jnp.zeros((128, 512), BF)
    gb_all[27] = jnp.zeros((4, 2, 4, 16, 128), BF)
    corner_in[2:4] = jnp.zeros((2, 32, 512), BF)
    for side in range(2):
        gtake_x[side, 96:128] = jnp.zeros((32, 128), BF)

    for side, edge in ((0, 0), (1, 7)):
        @pl.when(gx == edge)
        def _():
            rims[gz, 16 * side : 16 * side + 16] = jnp.zeros((16, 512), BF)
            gtake_x[side, 0:96] = jnp.zeros((96, 128), BF)

        @pl.when(gy == edge)
        def _():
            rim_in[side] = jnp.zeros((64, 512), BF)
            corner_in[side] = jnp.zeros((32, 512), BF)
            gtake_y[side] = jnp.zeros((64, 128), BF)

    def sub_to_xyz(row):
        x, y, z = cell_of_sub(row)
        return (x * 8 + y) * 8 + z

    def sub_to_zxy(row):
        x, y, z = cell_of_sub(row)
        return (z * 8 + x) * 8 + y

    perm_xyz[...] = selection(512, 512, lambda r: ((r & 7) * 8 + (r >> 6)) * 8 + ((r >> 3) & 7))
    perm_cot[...] = selection(512, 512, sub_to_zxy)

    loads[0].wait()
    pl.semaphore_wait(barrier, len(partners))

    def exchange(axis, position, count, low_src, high_dst, high_src, low_dst):
        down = remote(low_src, high_dst, {axis: around(position, count - 1, count)})
        up = remote(high_src, low_dst, {axis: around(position, 1, count)})

        @pl.when(position > 0)
        def _():
            down.start()

        @pl.when(position < count - 1)
        def _():
            up.start()

        def finish(on_low, on_high):
            @pl.when(position > 0)
            def _():
                down.wait_send()
                up.wait_recv()
                on_low()

            @pl.when(position < count - 1)
            def _():
                up.wait_send()
                down.wait_recv()
                on_high()

        return finish

    finish_z = exchange(
        "gz", gz, 4, vol.at[pl.ds(0, 64)], plane_z.at[1], vol.at[pl.ds(448, 64)], plane_z.at[0]
    )

    loads[1].wait()
    cot_sub[...] = matmul(perm_cot[...], cot[...]).astype(BF)
    loads[2].wait()
    back = jnp.zeros((64, 512), F32)
    for s in range(8):
        back = back + matmul_nt(cot_sub[pl.ds(64 * s, 64)], wu[s])
    for q in range(4):
        back_out[q] = back[:, 128 * q : 128 * (q + 1)].astype(BF)
    back_copies = []
    for d in (1, 2, 3):
        peer = around(gz, d, 4)
        copy = remote(back_out.at[peer], back_in.at[gz], {"gz": peer})
        copy.start()
        back_copies.append(copy)
    back_in[gz] = back_out[gz]

    main = matmul(perm_xyz[...], vol[...])
    padded[1:9, 1:9, 8:16, :] = main.reshape(8, 8, 8, 128)
    flat = padded.reshape(2400, 128)

    def at_row(x, y, z):
        return (x * 10 + y) * 24 + 7 + z

    def put_plane(side, z):
        plane = plane_z[side].astype(F32)
        for x in range(8):
            flat[pl.ds(at_row(x + 1, 1, z), 8, stride=24), :] = plane[8 * x : 8 * x + 8]

    finish_z(lambda: put_plane(0, 0), lambda: put_plane(1, 9))

    for side, y in ((0, 1), (1, 8)):
        face_y[side, 0:64] = padded[1:9, y, 8:16, :].reshape(64, 128).astype(BF)
        edges = [flat[pl.ds(at_row(1, y, z), 8, stride=240), :] for z in (0, 9)]
        face_y[side, 64:80] = jnp.concatenate(edges, axis=0).astype(BF)
    finish_y = exchange("gy", gy, 8, face_y.at[0], take_y.at[1], face_y.at[1], take_y.at[0])

    perm_sub[...] = selection(512, 512, sub_to_xyz)
    perm_back[...] = selection(512, 512, lambda r: sub_of_cell(r >> 6, (r >> 3) & 7, r & 7))
    perm_out[...] = selection(512, 512, lambda r: sub_of_cell((r >> 3) & 7, r & 7, r >> 6))

    def shifted_z(r, shift, column_of):
        z = (r & 15) + shift
        return jnp.where((z < 0) | (z > 15), -1, column_of(r, z & 15))

    for a in range(3):
        perm_group[a] = selection(
            256, 256, lambda r: shifted_z(r, a - 1, lambda r, z: (z >> 2) * 64 + (r >> 4) * 4 + (z & 3))
        )
        perm_rim[a] = selection(
            128, 128, lambda r: shifted_z(r, a - 1, lambda r, z: (z >> 2) * 32 + (r >> 4) * 4 + (z & 3))
        )
        lift_z[a] = selection(128, 128, lambda r: shifted_z(r, a - 1, lambda r, z: r - (r & 15) + z))
    perm_brick[...] = selection(256, 256, lambda r: ((r & 63) >> 2) * 16 + (r >> 6) * 4 + (r & 3))

    def put_y(side, y):
        face = take_y[side].astype(F32)
        padded[1:9, y, 8:16, :] = face[0:64].reshape(8, 8, 128)
        for i, z in enumerate((0, 9)):
            flat[pl.ds(at_row(1, y, z), 8, stride=240), :] = face[64 + 8 * i : 72 + 8 * i]

    finish_y(lambda: put_y(0, 0), lambda: put_y(1, 9))

    for side, x in ((0, 1), (1, 8)):
        face_x[side, 0:80] = padded[x, 0:10, 8:16, :].reshape(80, 128).astype(BF)
        for i, z in enumerate((0, 9)):
            first = flat[pl.ds(at_row(x, 0, z), 8, stride=24), :]
            rest = flat[pl.ds(at_row(x, 2, z), 8, stride=24), :]
            face_x[side, 80 + 16 * i : 96 + 16 * i] = jnp.concatenate([first, rest], axis=0).astype(BF)
    finish_x = exchange("gx", gx, 8, face_x.at[0], take_x.at[1], face_x.at[1], take_x.at[0])

    def put_x(side, x):
        face = take_x[side].astype(F32)
        padded[x, 0:10, 8:16, :] = face[0:80].reshape(10, 8, 128)
        for i, z in enumerate((0, 9)):
            flat[pl.ds(at_row(x, 0, z), 8, stride=24), :] = face[80 + 16 * i : 88 + 16 * i]
            flat[pl.ds(at_row(x, 2, z), 8, stride=24), :] = face[88 + 16 * i : 96 + 16 * i]

    finish_x(lambda: put_x(0, 0), lambda: put_x(1, 9))

    loads[3].wait()
    pre[...] = jnp.zeros_like(pre)

    @pl.loop(0, 9, unroll=3)
    def _(step):
        b, c = step // 3, step % 3
        windows = [
            padded[pl.ds(b, 8), pl.ds(c, 8), 7 + a : 15 + a, :].reshape(512, 128).astype(BF) for a in range(3)
        ]
        for a in range(3):
            columns[a * 9 + step] = windows[a]
        weights = jnp.concatenate([wc[a * 9 + step] for a in range(3)], axis=0)
        pre[...] += matmul(jnp.concatenate(windows, axis=1), weights)

    high = pre[...].astype(BF)
    low = (pre[...] - high.astype(F32)).astype(BF)
    pre_sub = matmul(perm_sub[...], high) + matmul(perm_sub[...], low)
    hidden_sub[...] = jax.nn.silu(pre_sub).astype(BF)
    slope_sub[...] = slope_of(pre_sub)

    loads[4].wait()
    coarse = jnp.zeros((64, 512), F32)
    for s in range(8):
        coarse = coarse + matmul(hidden_sub[pl.ds(64 * s, 64)], wd[s])
    bricks[gz] = coarse.astype(BF)

    finish_cx = exchange(
        "gx", gx, 8,
        bricks.at[gz, pl.ds(0, 16)], rims.at[gz, pl.ds(16, 16)],
        bricks.at[gz, pl.ds(48, 16)], rims.at[gz, pl.ds(0, 16)],
    )

    def send_column(ref):
        copies = []
        for d in (1, 2, 3):
            copy = remote(ref.at[gz], ref.at[gz], {"gz": around(gz, d, 4)})
            copy.start()
            copies.append(copy)
        return copies

    brick_copies = send_column(bricks)

    def turn(first, last):
        @pl.loop(first, last)
        def _(tap):
            turned[tap] = columns[tap].T

    turn(0, 16)
    finish_cx(lambda: None, lambda: None)
    rim_copies = send_column(rims)
    turn(16, 27)

    for copy in brick_copies:
        copy.wait()
    stack = bricks[...].reshape(256, 512)
    middle = matmul(perm_group[1], stack).astype(BF).reshape(4, 4, 16, 512)
    for side, y in ((0, 0), (1, 3)):
        rim_out[side] = middle[:, y].reshape(64, 512)
    finish_cy = exchange("gy", gy, 8, rim_out.at[0], rim_in.at[1], rim_out.at[1], rim_in.at[0])
    shifted[1, 1:5, 1:5] = middle
    for a in (0, 2):
        shifted[a, 1:5, 1:5] = matmul(perm_group[a], stack).astype(BF).reshape(4, 4, 16, 512)
    for copy in back_copies:
        copy.wait()
    back_column = matmul(perm_group[1], back_in[...].reshape(256, 128))

    loads[5].wait()
    finish_cy(lambda: None, lambda: None)
    for a in range(3):
        sides = matmul(lift_z[a], rim_in[...].reshape(128, 512)).astype(BF).reshape(2, 4, 16, 512)
        shifted[a, 1:5, 0] = sides[0]
        shifted[a, 1:5, 5] = sides[1]

    pre_low[...] = jnp.zeros_like(pre_low)

    def low_taps(first, last):
        @pl.loop(first, last, unroll=3)
        def _(step):
            b, c = step // 3, step % 3
            total = pre_low[...]
            for a in range(3):
                window = shifted[a, pl.ds(b, 4), pl.ds(c, 4)].reshape(256, 512)
                total = total + matmul(window, wb[a * 9 + step])
            pre_low[...] = total

    low_taps(0, 6)
    for copy in rim_copies:
        copy.wait()
    rim_rows = []
    for a in range(3):
        rim_rows.append(matmul(perm_rim[a], rims[...].reshape(128, 512)).astype(BF).reshape(2, 4, 16, 512))
    for side, y in ((0, 0), (1, 3)):
        corner_out[side] = rim_rows[1][:, y].reshape(32, 512)
    finish_cc = exchange("gy", gy, 8, corner_out.at[0], corner_in.at[1], corner_out.at[1], corner_in.at[0])
    low_taps(6, 9)
    for a in range(3):
        shifted[a, 0, 1:5] = rim_rows[a][0]
        shifted[a, 5, 1:5] = rim_rows[a][1]
    finish_cc(lambda: None, lambda: None)
    for a in range(3):
        corners = matmul(lift_z[a], corner_in[...].reshape(128, 512)).astype(BF).reshape(4, 2, 16, 512)
        for i, y in ((0, 0), (1, 5)):
            shifted[a, 0, y] = corners[i, 0]
            shifted[a, 5, y] = corners[i, 1]

    @pl.loop(0, 3)
    def _(c):
        low, high = pre_low[0:64], pre_low[192:256]
        for a in range(3):
            low = low + matmul(shifted[a, 0, pl.ds(c, 4)].reshape(64, 512), wb[a * 9 + c])
            high = high + matmul(shifted[a, 5, pl.ds(c, 4)].reshape(64, 512), wb[a * 9 + 6 + c])
        pre_low[0:64] = low
        pre_low[192:256] = high

    bottle_grad = (back_column * slope_of(pre_low[...])).astype(BF)
    grad_now[...] = bottle_grad
    middle = bottle_grad.astype(F32).reshape(4, 4, 16, 128)
    for side, y in ((0, 0), (1, 3)):
        gface_y[side] = middle[:, y].reshape(64, 128).astype(BF)
    finish_gy = exchange("gy", gy, 8, gface_y.at[0], gtake_y.at[1], gface_y.at[1], gtake_y.at[0])

    bottle = jax.nn.silu(pre_low[...]).astype(BF)
    bottle_out[...] = matmul(perm_brick[...], bottle).astype(BF).reshape(4, 64, 128)
    bottle_copies = []
    for d in (1, 2, 3):
        peer = around(gz, d, 4)
        copy = remote(bottle_out.at[peer], bottle_in.at[gz], {"gz": peer})
        copy.start()
        bottle_copies.append(copy)
    bottle_in[gz] = bottle_out[gz]

    for a in range(3):
        for half in range(2):
            moved = matmul(lift_z[a], grad_now[pl.ds(128 * half, 128)]).astype(BF)
            grad_shift[a, 1 + 2 * half : 3 + 2 * half, 1:5] = moved.reshape(2, 4, 16, 128)

    mine, other = core * 14, (1 - core) * 14

    def bottle_taps(first, last, base):
        @pl.loop(first, last)
        def _(step):
            tap = base + step
            depth, across = tap // 9, tap % 9
            b, c = across // 3, across % 3
            window = shifted[depth, pl.ds(b, 4), pl.ds(c, 4)].reshape(256, 512)
            gb_all[tap] = matmul_tn(window, grad_now[...]).astype(BF).reshape(4, 2, 4, 16, 128)

    bottle_taps(0, 8, other)
    finish_gy(lambda: None, lambda: None)
    for a in range(3):
        sides = matmul(lift_z[a], gtake_y[...].reshape(128, 128)).astype(BF).reshape(2, 4, 16, 128)
        grad_shift[a, 1:5, 0] = sides[0]
        grad_shift[a, 1:5, 5] = sides[1]
    for side, x in ((0, 1), (1, 4)):
        gface_x[side] = grad_shift[1, x].reshape(96, 128)
    finish_gx = exchange(
        "gx", gx, 8,
        gface_x.at[0], gtake_x.at[1, pl.ds(0, 96)], gface_x.at[1], gtake_x.at[0, pl.ds(0, 96)],
    )

    part_acc[...] = jnp.zeros_like(part_acc)

    @pl.loop(0, 9, unroll=3)
    def _(step):
        b, c = step // 3, step % 3
        windows = [grad_shift[2 - a, pl.ds(2 - b, 4), pl.ds(2 - c, 4)].reshape(256, 128) for a in range(3)]
        weights = jnp.concatenate([wb[a * 9 + step] for a in range(3)], axis=1)
        part_acc[...] += matmul_nt(jnp.concatenate(windows, axis=1), weights)

    finish_gx(lambda: None, lambda: None)
    for a in range(3):
        for side, x in ((0, 0), (1, 5)):
            moved = matmul(lift_z[a], gtake_x[side]).astype(BF)
            grad_shift[a, x] = moved[0:96].reshape(6, 16, 128)

    @pl.loop(0, 3)
    def _(c):
        for x, rows, b in ((0, 0, 2), (5, 192, 0)):
            windows = [grad_shift[2 - a, x, pl.ds(2 - c, 4)].reshape(64, 128) for a in range(3)]
            weights = jnp.concatenate([wb[a * 9 + 3 * b + c] for a in range(3)], axis=1)
            part_acc[rows : rows + 64] += matmul_nt(jnp.concatenate(windows, axis=1), weights)

    part_out[...] = matmul(perm_brick[...], part_acc[...].astype(BF)).astype(BF).reshape(4, 64, 512)
    part_copies = []
    for d in (1, 2, 3):
        peer = around(gz, d, 4)
        copy = remote(part_out.at[peer], part_in.at[d - 1], {"gz": peer})
        copy.start()
        part_copies.append(copy)

    bottle_taps(8, 13 + core, other)
    gb_first = remote(gb_all.at[pl.ds(other, 14)], gb_one, {"gy": gy ^ 1})
    gb_first.start()
    bottle_taps(0, 14 - core, mine)

    for copy in bottle_copies:
        copy.wait()
    for s in range(8):
        lifted = jnp.zeros((64, 128), F32)
        for q in range(4):
            lifted = lifted + matmul(bottle_in[q], wu[s, pl.ds(128 * q, 128)])
        total = lifted + hidden_sub[pl.ds(64 * s, 64)].astype(F32)
        fine_grad[pl.ds(64 * s, 64)] = total.astype(BF)
    out_ref[...] = matmul(perm_out[...], fine_grad[...]).astype(BF)

    gb_first.wait()

    @pl.loop(0, 14)
    def _(step):
        total = gb_all[mine + step].astype(F32) + gb_one[step].astype(F32)
        gb_all[mine + step] = total.astype(BF)

    def along_y(source_of, target):
        copies = []
        for d in (1, 2, 3):
            copy = remote(source_of(around(py, d, 4)), target.at[d - 1], {"gx": around(gx, 2 * d, 8)})
            copy.start()
            copies.append(copy)
        return copies

    def along_x(source_of, target):
        copies = []
        for d in (1, 2, 3):
            copy = remote(source_of(around(px, d, 4)), target.at[d - 1], {"gy": around(gy, 2 * d, 8)})
            copy.start()
            copies.append(copy)
        return copies

    def y_place(y):
        return {"gx": 2 * y + zh}

    def x_place(x):
        return {"gy": 2 * x + core}

    def begin_halving(position, place, mirrored, chunk, inbox):
        near, far = position ^ 1, 3 - position
        first, second = (far, near) if mirrored else (near, far)
        beyond = first ^ 1 if mirrored else 3 - first
        copies = [
            remote(chunk(first), inbox.at[0], place(first)), remote(chunk(beyond), inbox.at[1], place(first))
        ]
        for copy in copies:
            copy.start()

        def next_step():
            copies[1].wait()
            ref = chunk(second)
            ref[...] = (ref[...].astype(F32) + inbox[1].astype(F32)).astype(BF)
            last = remote(ref, inbox.at[2], place(second))
            last.start()
            copies[0].wait()

            def finish():
                own = chunk(position)
                total = own[...].astype(F32) + inbox[0].astype(F32)
                last.wait()
                return total + inbox[2].astype(F32)

            return finish

        return next_step

    parts = ((0, 4), (4, 3))
    inbox_a, inbox_b = (gb_ya, gb_ya2), (gb_xb, gb_xb2)
    inbox_c, inbox_d = (gb_xa, gb_xa2), (gb_yb, gb_yb2)
    gb_steps = []
    for i, (t, n) in enumerate(parts):
        gb_steps.append(begin_halving(
            py, y_place, i == 1, lambda y, t=t, n=n: gb_all.at[pl.ds(mine + t, n), y], inbox_a[i]
        ))
        gb_steps.append(begin_halving(
            px, x_place, i == 1, lambda x, t=t, n=n: gb_all.at[pl.ds(mine + 7 + t, n), :, :, x], inbox_b[i]
        ))

    for copy in part_copies:
        copy.wait()
    coarse_grad = part_out[gz].astype(F32)
    for d in range(3):
        coarse_grad = coarse_grad + part_in[d].astype(F32)
    coarse_grad = coarse_grad.astype(BF)
    for s in range(8):
        rows = pl.ds(64 * s, 64)
        spread = matmul_nt(coarse_grad, wd[s]) + cot_sub[rows].astype(F32)
        fine_grad[rows] = (spread * slope_sub[rows]).astype(BF)
    fine_grad[...] = matmul(perm_back[...], fine_grad[...]).astype(BF)

    def fine_taps(base):
        for step in range(4):
            lines = turned[pl.ds(base + 4 * step, 4)].reshape(512, 512)
            term = matmul(lines, fine_grad[...])
            gc_all[pl.ds(base + 4 * step, 4)] = term.astype(BF).reshape(4, 4, 32, 128)

    keep, give = core * 16, (1 - core) * 16
    fine_taps(give)
    gc_first = remote(gc_all.at[pl.ds(give, 16)], gc_one, {"gy": gy ^ 1})
    gc_first.start()
    fine_taps(keep)

    gb_ends = [step() for step in gb_steps]

    gc_first.wait()

    @pl.loop(0, 16)
    def _(step):
        total = gc_all[keep + step].astype(F32) + gc_one[step].astype(F32)
        gc_all[keep + step] = total.astype(BF)

    gc_second = along_x(lambda x: gc_all.at[pl.ds(keep + 2 * x, 2)], gc_xa)
    gc_second += along_y(lambda y: gc_all.at[pl.ds(keep + 8, 8), y], gc_yb)

    def summed(own, taken):
        total = own.astype(F32)
        for d in range(3):
            total = total + taken[d].astype(F32)
        return total

    gb_steps = []
    for i, (t, n) in enumerate(parts):
        gb_a[t : t + n] = gb_ends[2 * i]().astype(BF)
        gb_steps.append(begin_halving(
            px, x_place, i == 1, lambda x, t=t, n=n: gb_a.at[pl.ds(t, n), :, x], inbox_c[i]
        ))
        gb_b[t : t + n] = gb_ends[2 * i + 1]().astype(BF)
        gb_steps.append(begin_halving(
            py, y_place, i == 1, lambda y, t=t, n=n: gb_b.at[pl.ds(t, n), y], inbox_d[i]
        ))

    for copy in gc_second:
        copy.wait()
    gc_a[...] = summed(gc_all[pl.ds(keep + 2 * px, 2)], gc_xa).astype(BF)
    gc_b[...] = summed(gc_all[pl.ds(keep + 8, 8), py], gc_yb).astype(BF)
    gc_third = along_y(lambda y: gc_a.at[:, y], gc_ya)
    gc_third += along_x(lambda x: gc_b.at[pl.ds(2 * x, 2)], gc_xb)

    gb_last = [step() for step in gb_steps]
    for i, (t, n) in enumerate(parts):
        gb_d4[t : t + n] = gb_last[2 * i]().astype(BF)
        gb_d4[7 + t : 7 + t + n] = gb_last[2 * i + 1]().astype(BF)
    gb_fourth = remote(gb_d4.at[:, 1 - zh], gb_four, {"gx": gx ^ 1})
    gb_fourth.start()

    for copy in gc_third:
        copy.wait()
    gc_e2[0:2] = summed(gc_a[:, py], gc_ya).astype(BF).reshape(2, 2, 16, 128)
    gc_e2[2:4] = summed(gc_b[pl.ds(2 * px, 2)], gc_xb).astype(BF).reshape(2, 2, 16, 128)
    slot = zh * 4 + gz
    gc_fourth = []
    for d in range(4):
        peer = around(gz, d, 4)
        copy = remote(gc_e2.at[:, 1 - zh], gc_z.at[slot], {"gx": gx ^ 1, "gz": peer})
        copy.start()
        gc_fourth.append(copy)
        if d > 0:
            copy = remote(gc_e2.at[:, zh], gc_z.at[slot], {"gz": peer})
            copy.start()
            gc_fourth.append(copy)
    gc_z[slot] = gc_e2[:, zh]

    gb_fourth.wait()
    gb_d5[...] = (gb_d4[:, zh].astype(F32) + gb_four[...].astype(F32)).reshape(14, 2, 8, 128)
    gb_fifth = remote(gb_d5.at[:, 1 - core], gb_five, {"gy": gy ^ 1})
    gb_fifth.start()

    for copy in gc_fourth:
        copy.wait()
    total = gc_z[0].astype(F32)
    for q in range(1, 8):
        total = total + gc_z[q].astype(F32)
    for half in range(2):
        gc_half[half] = total[:, 8 * half : 8 * half + 8]
    gathers = []
    for d in range(1, 8):
        peer = around(gy, d, 8)
        copy = remote(gc_half.at[peer >> 2], gc_g.at[gy], {"gy": peer})
        copy.start()
        gathers.append(copy)
    gc_g[gy] = gc_half[gy >> 2]

    gb_fifth.wait()
    gb_ref[pl.ds(mine, 14)] = gb_d5[:, core]
    gb_ref[pl.ds(other, 14)] = gb_five[...]

    for copy in gathers:
        copy.wait()
    place = gy & 3
    for source in range(8):
        block = gc_g[source]
        chosen = jnp.zeros((4, 2, 128), F32)
        for j in range(4):
            chosen = chosen + jnp.where(place == j, block[:, 2 * j : 2 * j + 2, :], 0.0)
        first = (source & 1) * 16 + (source >> 1) * 2
        gc_ref[first : first + 2] = chosen[0:2]
        gc_ref[first + 8 : first + 10] = chosen[2:4]


def deliver_kernel(out_ref, gb_ref, gc_ref, out_final, gb_final, gc_final):
    out_final[...] = out_ref[...]
    gb_final[...] = gb_ref[0:TAPS]
    gc_final[...] = gc_ref[0:TAPS]


def body(volume, cotangent, w_conv, w_down, w_bottle, w_up):
    vmem = pltpu.VMEM
    whole = pl.BlockSpec(memory_space=pl.ANY)
    held = pl.BlockSpec(memory_space=pltpu.VMEM)
    def kept(*shape):
        return vmem(shape, BF)

    scratch = [
        kept(512, 128), kept(512, 128), kept(27, 128, 128), kept(8, 128, 512),
        kept(27, 512, 128), kept(8, 512, 128), pltpu.SemaphoreType.DMA((6,)),
        kept(512, 512), kept(512, 512), kept(512, 512), kept(512, 512), kept(512, 512),
        kept(3, 256, 256), kept(3, 128, 128), kept(256, 256), kept(3, 128, 128),
        kept(2, 64, 128), kept(2, 80, 128), kept(2, 80, 128), kept(2, 112, 128), kept(2, 112, 128),
        vmem((10, 10, 24, 128), F32), kept(27, 512, 128), kept(32, 128, 512), vmem((512, 128), F32),
        kept(512, 128), vmem((512, 128), F32), kept(512, 128),
        kept(4, 64, 128), kept(4, 64, 128), kept(4, 64, 512), kept(4, 32, 512), kept(3, 6, 6, 16, 512),
        kept(2, 64, 512), kept(2, 64, 512), kept(2, 32, 512), kept(4, 32, 512), vmem((256, 128), F32),
        kept(256, 128), kept(3, 6, 6, 16, 128), kept(2, 64, 128), kept(2, 64, 128),
        kept(2, 96, 128), kept(2, 128, 128),
        kept(4, 64, 128), kept(4, 64, 128), vmem((256, 512), F32), kept(4, 64, 512),
        kept(3, 64, 512), kept(512, 128),
        kept(28, 4, 2, 4, 16, 128), kept(14, 4, 2, 4, 16, 128),
        kept(3, 4, 2, 4, 16, 128), kept(3, 3, 2, 4, 16, 128), kept(3, 4, 4, 2, 16, 128), kept(3, 3, 4, 2, 16, 128),
        kept(7, 2, 4, 16, 128), kept(7, 4, 2, 16, 128),
        kept(3, 4, 2, 16, 128), kept(3, 3, 2, 16, 128), kept(3, 4, 2, 16, 128), kept(3, 3, 2, 16, 128),
        kept(14, 2, 16, 128), kept(14, 16, 128), vmem((14, 2, 8, 128), F32), vmem((14, 8, 128), F32),
        kept(32, 4, 32, 128), kept(16, 4, 32, 128), kept(3, 2, 4, 32, 128), kept(3, 8, 32, 128),
        kept(2, 4, 32, 128), kept(8, 32, 128), kept(3, 2, 32, 128), kept(3, 2, 32, 128),
        kept(4, 2, 16, 128), kept(8, 4, 16, 128), vmem((2, 4, 8, 128), F32), vmem((8, 4, 8, 128), F32),
        pltpu.SemaphoreType.DMA((COPIES,)), pltpu.SemaphoreType.DMA((COPIES,)),
    ]
    out, gb, gc = pl.pallas_call(
        level_kernel,
        out_shape=(
            jax.ShapeDtypeStruct((512, 128), BF),
            jax.ShapeDtypeStruct((28, 8, 128), F32),
            jax.ShapeDtypeStruct((32, 2, 128), F32),
        ),
        in_specs=[whole] * 6,
        out_specs=(held,) * 3,
        scratch_shapes=scratch,
        compiler_params=pltpu.CompilerParams(
            collective_id=0, has_side_effects=True, vmem_limit_bytes=60 * 1024 * 1024
        ),
        name="level",
    )(
        volume.reshape(512, 128),
        cotangent.reshape(512, 128),
        jnp.transpose(w_conv, (1, 0, 2)),
        w_down,
        jnp.transpose(w_bottle, (1, 0, 2)),
        w_up,
    )
    out, gb, gc = pl.pallas_call(
        deliver_kernel,
        out_shape=(
            jax.ShapeDtypeStruct(out.shape, BF),
            jax.ShapeDtypeStruct((TAPS, 8, 128), F32),
            jax.ShapeDtypeStruct((TAPS, 2, 128), F32),
        ),
        in_specs=[held] * 3,
        out_specs=(held,) * 3,
        name="deliver",
    )(out, gb, gc)
    return out.reshape(volume.shape), jnp.transpose(gc, (1, 0, 2)), jnp.transpose(gb, (1, 0, 2))


def solution(mesh):
    in_specs = (
        P("gz", "gx", "gy", None),
        P("gz", "gx", "gy", None),
        P(),
        P(),
        P(None, None, "gz"),
        P(),
    )
    out_specs = (
        P("gz", "gx", "gy", None),
        P(("gx", "gy"), None, None),
        P(("gx", "gy"), None, "gz"),
    )
    return jax.shard_map(body, mesh=mesh, in_specs=in_specs, out_specs=out_specs, check_vma=False)
```

```python
import jax
import jax.numpy as jnp
from jax import lax
from jax.experimental import pallas as pl
from jax.experimental.pallas import tpu as pltpu
from jax.sharding import PartitionSpec as P

BF = jnp.bfloat16
F32 = jnp.float32
MESH = pl.DeviceIdType.MESH
TAPS = 27
COPIES = 96


def matmul(left, right):
    return jnp.dot(left, right, preferred_element_type=F32)


def matmul_nt(left, right):
    return lax.dot_general(left, right, (((1,), (1,)), ((), ())), preferred_element_type=F32)


def matmul_tn(left, right):
    return lax.dot_general(left, right, (((0,), (0,)), ((), ())), preferred_element_type=F32)


def slope_of(values):
    sig = jax.nn.sigmoid(values)
    return sig * (1.0 + values * (1.0 - sig))


def selection(rows, columns, column_of):
    row = lax.broadcasted_iota(jnp.int32, (rows, 128), 0)
    lane = lax.broadcasted_iota(jnp.int32, (rows, 128), 1)
    target = column_of(row)
    blocks = [
        jnp.where(target == lane + 128 * block, 1.0, 0.0).astype(BF) for block in range(columns // 128)
    ]
    return jnp.concatenate(blocks, axis=1)


def cell_of_sub(row):
    s, k = row >> 6, row & 63
    x = 2 * (k >> 4) + ((s >> 1) & 1)
    y = 2 * ((k >> 2) & 3) + (s & 1)
    z = 2 * (k & 3) + (s >> 2)
    return x, y, z


def sub_of_cell(x, y, z):
    s = (z & 1) * 4 + (x & 1) * 2 + (y & 1)
    k = ((x >> 1) * 4 + (y >> 1)) * 4 + (z >> 1)
    return s * 64 + k


def level_kernel(
    vol_hbm, cot_hbm, wc_hbm, wd_hbm, wb_hbm, wu_hbm,
    out_ref, gb_ref, gc_ref,
    vol, cot, wc, wd, wb, wu, load_sem,
    perm_xyz, perm_sub, perm_cot, perm_back, perm_out, perm_group, perm_rim, perm_brick, lift_z,
    plane_z, face_y, take_y, face_x, take_x,
    padded, columns, turned, pre, cot_sub, slope_sub, hidden_sub,
    back_out, back_in, bricks, rims, shifted, rim_out, rim_in, corner_out, corner_in, pre_low,
    grad_now, grad_shift, gface_y, gtake_y, gface_x, gtake_x,
    bottle_out, bottle_in, part_acc, part_out, part_in, fine_grad,
    gb_all, gb_one, gb_ya, gb_ya2, gb_xb, gb_xb2, gb_a, gb_b, gb_xa, gb_xa2, gb_yb, gb_yb2, gb_d4, gb_four, gb_d5, gb_five,
    gc_all, gc_one, gc_xa, gc_yb, gc_a, gc_b, gc_ya, gc_xb, gc_e2, gc_z, gc_half, gc_g,
    send_sem, recv_sem,
):
    gx, gy, gz = lax.axis_index("gx"), lax.axis_index("gy"), lax.axis_index("gz")
    py, zh = gx >> 1, gx & 1
    px, core = gy >> 1, gy & 1
    used = [0]

    def remote(src, dst, device):
        slot = used[0]
        used[0] += 1
        return pltpu.make_async_remote_copy(
            src_ref=src, dst_ref=dst, send_sem=send_sem.at[slot], recv_sem=recv_sem.at[slot],
            device_id=device, device_id_type=MESH,
        )

    def around(position, step, count):
        return lax.rem(position + step, count)

    barrier = pltpu.get_barrier_semaphore()
    partners = [{"gx": around(gx, d, 8)} for d in (1, 2, 4, 6, 7)]
    partners += [{"gy": around(gy, d, 8)} for d in range(1, 8)]
    partners += [{"gz": around(gz, d, 4)} for d in (1, 2, 3)]
    partners += [{"gx": gx ^ 1, "gz": around(gz, d, 4)} for d in (1, 2, 3)]
    for partner in partners:
        pl.semaphore_signal(barrier, inc=1, device_id=partner, device_id_type=MESH)

    loads = [
        pltpu.make_async_copy(src, dst, load_sem.at[i])
        for i, (src, dst) in enumerate(
            ((vol_hbm, vol), (cot_hbm, cot), (wu_hbm, wu), (wc_hbm, wc), (wd_hbm, wd), (wb_hbm, wb))
        )
    ]
    for load in loads:
        load.start()

    padded[...] = jnp.zeros_like(padded)
    for side in (0, 5):
        for a in range(3):
            shifted[a, side] = jnp.zeros((6, 16, 512), BF)
            grad_shift[a, side] = jnp.zeros((6, 16, 128), BF)
    for tap in range(TAPS, 32):
        turned[tap] = jnp.zeros((128, 512), BF)
    gb_all[27] = jnp.zeros((4, 2, 4, 16, 128), BF)
    corner_in[2:4] = jnp.zeros((2, 32, 512), BF)
    for side in range(2):
        gtake_x[side, 96:128] = jnp.zeros((32, 128), BF)

    for side, edge in ((0, 0), (1, 7)):
        @pl.when(gx == edge)
        def _():
            rims[gz, 16 * side : 16 * side + 16] = jnp.zeros((16, 512), BF)
            gtake_x[side, 0:96] = jnp.zeros((96, 128), BF)

        @pl.when(gy == edge)
        def _():
            rim_in[side] = jnp.zeros((64, 512), BF)
            corner_in[side] = jnp.zeros((32, 512), BF)
            gtake_y[side] = jnp.zeros((64, 128), BF)

    def sub_to_xyz(row):
        x, y, z = cell_of_sub(row)
        return (x * 8 + y) * 8 + z

    def sub_to_zxy(row):
        x, y, z = cell_of_sub(row)
        return (z * 8 + x) * 8 + y

    perm_xyz[...] = selection(512, 512, lambda r: ((r & 7) * 8 + (r >> 6)) * 8 + ((r >> 3) & 7))
    perm_cot[...] = selection(512, 512, sub_to_zxy)

    loads[0].wait()
    pl.semaphore_wait(barrier, len(partners))

    def exchange(axis, position, count, low_src, high_dst, high_src, low_dst):
        down = remote(low_src, high_dst, {axis: around(position, count - 1, count)})
        up = remote(high_src, low_dst, {axis: around(position, 1, count)})

        @pl.when(position > 0)
        def _():
            down.start()

        @pl.when(position < count - 1)
        def _():
            up.start()

        def finish(on_low, on_high):
            @pl.when(position > 0)
            def _():
                down.wait_send()
                up.wait_recv()
                on_low()

            @pl.when(position < count - 1)
            def _():
                up.wait_send()
                down.wait_recv()
                on_high()

        return finish

    finish_z = exchange(
        "gz", gz, 4, vol.at[pl.ds(0, 64)], plane_z.at[1], vol.at[pl.ds(448, 64)], plane_z.at[0]
    )

    loads[1].wait()
    cot_sub[...] = matmul(perm_cot[...], cot[...]).astype(BF)
    loads[2].wait()
    back = jnp.zeros((64, 512), F32)
    for s in range(8):
        back = back + matmul_nt(cot_sub[pl.ds(64 * s, 64)], wu[s])
    for q in range(4):
        back_out[q] = back[:, 128 * q : 128 * (q + 1)].astype(BF)
    back_copies = []
    for d in (1, 2, 3):
        peer = around(gz, d, 4)
        copy = remote(back_out.at[peer], back_in.at[gz], {"gz": peer})
        copy.start()
        back_copies.append(copy)
    back_in[gz] = back_out[gz]

    main = matmul(perm_xyz[...], vol[...])
    padded[1:9, 1:9, 8:16, :] = main.reshape(8, 8, 8, 128)
    flat = padded.reshape(2400, 128)

    def at_row(x, y, z):
        return (x * 10 + y) * 24 + 7 + z

    def put_plane(side, z):
        plane = plane_z[side].astype(F32)
        for x in range(8):
            flat[pl.ds(at_row(x + 1, 1, z), 8, stride=24), :] = plane[8 * x : 8 * x + 8]

    finish_z(lambda: put_plane(0, 0), lambda: put_plane(1, 9))

    for side, y in ((0, 1), (1, 8)):
        face_y[side, 0:64] = padded[1:9, y, 8:16, :].reshape(64, 128).astype(BF)
        edges = [flat[pl.ds(at_row(1, y, z), 8, stride=240), :] for z in (0, 9)]
        face_y[side, 64:80] = jnp.concatenate(edges, axis=0).astype(BF)
    finish_y = exchange("gy", gy, 8, face_y.at[0], take_y.at[1], face_y.at[1], take_y.at[0])

    perm_sub[...] = selection(512, 512, sub_to_xyz)
    perm_back[...] = selection(512, 512, lambda r: sub_of_cell(r >> 6, (r >> 3) & 7, r & 7))
    perm_out[...] = selection(512, 512, lambda r: sub_of_cell((r >> 3) & 7, r & 7, r >> 6))

    def shifted_z(r, shift, column_of):
        z = (r & 15) + shift
        return jnp.where((z < 0) | (z > 15), -1, column_of(r, z & 15))

    for a in range(3):
        perm_group[a] = selection(
            256, 256, lambda r: shifted_z(r, a - 1, lambda r, z: (z >> 2) * 64 + (r >> 4) * 4 + (z & 3))
        )
        perm_rim[a] = selection(
            128, 128, lambda r: shifted_z(r, a - 1, lambda r, z: (z >> 2) * 32 + (r >> 4) * 4 + (z & 3))
        )
        lift_z[a] = selection(128, 128, lambda r: shifted_z(r, a - 1, lambda r, z: r - (r & 15) + z))
    perm_brick[...] = selection(256, 256, lambda r: ((r & 63) >> 2) * 16 + (r >> 6) * 4 + (r & 3))

    def put_y(side, y):
        face = take_y[side].astype(F32)
        padded[1:9, y, 8:16, :] = face[0:64].reshape(8, 8, 128)
        for i, z in enumerate((0, 9)):
            flat[pl.ds(at_row(1, y, z), 8, stride=240), :] = face[64 + 8 * i : 72 + 8 * i]

    finish_y(lambda: put_y(0, 0), lambda: put_y(1, 9))

    for side, x in ((0, 1), (1, 8)):
        face_x[side, 0:80] = padded[x, 0:10, 8:16, :].reshape(80, 128).astype(BF)
        for i, z in enumerate((0, 9)):
            first = flat[pl.ds(at_row(x, 0, z), 8, stride=24), :]
            rest = flat[pl.ds(at_row(x, 2, z), 8, stride=24), :]
            face_x[side, 80 + 16 * i : 96 + 16 * i] = jnp.concatenate([first, rest], axis=0).astype(BF)
    finish_x = exchange("gx", gx, 8, face_x.at[0], take_x.at[1], face_x.at[1], take_x.at[0])

    def put_x(side, x):
        face = take_x[side].astype(F32)
        padded[x, 0:10, 8:16, :] = face[0:80].reshape(10, 8, 128)
        for i, z in enumerate((0, 9)):
            flat[pl.ds(at_row(x, 0, z), 8, stride=24), :] = face[80 + 16 * i : 88 + 16 * i]
            flat[pl.ds(at_row(x, 2, z), 8, stride=24), :] = face[88 + 16 * i : 96 + 16 * i]

    finish_x(lambda: put_x(0, 0), lambda: put_x(1, 9))

    loads[3].wait()
    pre[...] = jnp.zeros_like(pre)

    @pl.loop(0, 9, unroll=3)
    def _(step):
        b, c = step // 3, step % 3
        windows = [
            padded[pl.ds(b, 8), pl.ds(c, 8), 7 + a : 15 + a, :].reshape(512, 128).astype(BF) for a in range(3)
        ]
        for a in range(3):
            columns[a * 9 + step] = windows[a]
        weights = jnp.concatenate([wc[a * 9 + step] for a in range(3)], axis=0)
        pre[...] += matmul(jnp.concatenate(windows, axis=1), weights)

    high = pre[...].astype(BF)
    low = (pre[...] - high.astype(F32)).astype(BF)
    pre_sub = matmul(perm_sub[...], high) + matmul(perm_sub[...], low)
    hidden_sub[...] = jax.nn.silu(pre_sub).astype(BF)
    slope_sub[...] = slope_of(pre_sub)

    loads[4].wait()
    coarse = jnp.zeros((64, 512), F32)
    for s in range(8):
        coarse = coarse + matmul(hidden_sub[pl.ds(64 * s, 64)], wd[s])
    bricks[gz] = coarse.astype(BF)

    finish_cx = exchange(
        "gx", gx, 8,
        bricks.at[gz, pl.ds(0, 16)], rims.at[gz, pl.ds(16, 16)],
        bricks.at[gz, pl.ds(48, 16)], rims.at[gz, pl.ds(0, 16)],
    )

    def send_column(ref):
        copies = []
        for d in (1, 2, 3):
            copy = remote(ref.at[gz], ref.at[gz], {"gz": around(gz, d, 4)})
            copy.start()
            copies.append(copy)
        return copies

    brick_copies = send_column(bricks)

    def turn(first, last):
        @pl.loop(first, last)
        def _(tap):
            turned[tap] = columns[tap].T

    turn(0, 16)
    finish_cx(lambda: None, lambda: None)
    rim_copies = send_column(rims)
    turn(16, 27)

    for copy in brick_copies:
        copy.wait()
    stack = bricks[...].reshape(256, 512)
    middle = matmul(perm_group[1], stack).astype(BF).reshape(4, 4, 16, 512)
    for side, y in ((0, 0), (1, 3)):
        rim_out[side] = middle[:, y].reshape(64, 512)
    finish_cy = exchange("gy", gy, 8, rim_out.at[0], rim_in.at[1], rim_out.at[1], rim_in.at[0])
    shifted[1, 1:5, 1:5] = middle
    for a in (0, 2):
        shifted[a, 1:5, 1:5] = matmul(perm_group[a], stack).astype(BF).reshape(4, 4, 16, 512)
    for copy in back_copies:
        copy.wait()
    back_column = matmul(perm_group[1], back_in[...].reshape(256, 128))

    loads[5].wait()
    finish_cy(lambda: None, lambda: None)
    for a in range(3):
        sides = matmul(lift_z[a], rim_in[...].reshape(128, 512)).astype(BF).reshape(2, 4, 16, 512)
        shifted[a, 1:5, 0] = sides[0]
        shifted[a, 1:5, 5] = sides[1]

    pre_low[...] = jnp.zeros_like(pre_low)

    def low_taps(first, last):
        @pl.loop(first, last, unroll=3)
        def _(step):
            b, c = step // 3, step % 3
            total = pre_low[...]
            for a in range(3):
                window = shifted[a, pl.ds(b, 4), pl.ds(c, 4)].reshape(256, 512)
                total = total + matmul(window, wb[a * 9 + step])
            pre_low[...] = total

    low_taps(0, 6)
    for copy in rim_copies:
        copy.wait()
    rim_rows = []
    for a in range(3):
        rim_rows.append(matmul(perm_rim[a], rims[...].reshape(128, 512)).astype(BF).reshape(2, 4, 16, 512))
    for side, y in ((0, 0), (1, 3)):
        corner_out[side] = rim_rows[1][:, y].reshape(32, 512)
    finish_cc = exchange("gy", gy, 8, corner_out.at[0], corner_in.at[1], corner_out.at[1], corner_in.at[0])
    low_taps(6, 9)
    for a in range(3):
        shifted[a, 0, 1:5] = rim_rows[a][0]
        shifted[a, 5, 1:5] = rim_rows[a][1]
    finish_cc(lambda: None, lambda: None)
    for a in range(3):
        corners = matmul(lift_z[a], corner_in[...].reshape(128, 512)).astype(BF).reshape(4, 2, 16, 512)
        for i, y in ((0, 0), (1, 5)):
            shifted[a, 0, y] = corners[i, 0]
            shifted[a, 5, y] = corners[i, 1]

    @pl.loop(0, 3)
    def _(c):
        low, high = pre_low[0:64], pre_low[192:256]
        for a in range(3):
            low = low + matmul(shifted[a, 0, pl.ds(c, 4)].reshape(64, 512), wb[a * 9 + c])
            high = high + matmul(shifted[a, 5, pl.ds(c, 4)].reshape(64, 512), wb[a * 9 + 6 + c])
        pre_low[0:64] = low
        pre_low[192:256] = high

    bottle_grad = (back_column * slope_of(pre_low[...])).astype(BF)
    grad_now[...] = bottle_grad
    middle = bottle_grad.astype(F32).reshape(4, 4, 16, 128)
    for side, y in ((0, 0), (1, 3)):
        gface_y[side] = middle[:, y].reshape(64, 128).astype(BF)
    finish_gy = exchange("gy", gy, 8, gface_y.at[0], gtake_y.at[1], gface_y.at[1], gtake_y.at[0])

    bottle = jax.nn.silu(pre_low[...]).astype(BF)
    bottle_out[...] = matmul(perm_brick[...], bottle).astype(BF).reshape(4, 64, 128)
    bottle_copies = []
    for d in (1, 2, 3):
        peer = around(gz, d, 4)
        copy = remote(bottle_out.at[peer], bottle_in.at[gz], {"gz": peer})
        copy.start()
        bottle_copies.append(copy)
    bottle_in[gz] = bottle_out[gz]

    for a in range(3):
        for half in range(2):
            moved = matmul(lift_z[a], grad_now[pl.ds(128 * half, 128)]).astype(BF)
            grad_shift[a, 1 + 2 * half : 3 + 2 * half, 1:5] = moved.reshape(2, 4, 16, 128)

    mine, other = core * 14, (1 - core) * 14

    def bottle_taps(first, last, base):
        @pl.loop(first, last)
        def _(step):
            tap = base + step
            depth, across = tap // 9, tap % 9
            b, c = across // 3, across % 3
            window = shifted[depth, pl.ds(b, 4), pl.ds(c, 4)].reshape(256, 512)
            gb_all[tap] = matmul_tn(window, grad_now[...]).astype(BF).reshape(4, 2, 4, 16, 128)

    bottle_taps(0, 8, other)
    finish_gy(lambda: None, lambda: None)
    for a in range(3):
        sides = matmul(lift_z[a], gtake_y[...].reshape(128, 128)).astype(BF).reshape(2, 4, 16, 128)
        grad_shift[a, 1:5, 0] = sides[0]
        grad_shift[a, 1:5, 5] = sides[1]
    for side, x in ((0, 1), (1, 4)):
        gface_x[side] = grad_shift[1, x].reshape(96, 128)
    finish_gx = exchange(
        "gx", gx, 8,
        gface_x.at[0], gtake_x.at[1, pl.ds(0, 96)], gface_x.at[1], gtake_x.at[0, pl.ds(0, 96)],
    )

    part_acc[...] = jnp.zeros_like(part_acc)

    @pl.loop(0, 9, unroll=3)
    def _(step):
        b, c = step // 3, step % 3
        windows = [grad_shift[2 - a, pl.ds(2 - b, 4), pl.ds(2 - c, 4)].reshape(256, 128) for a in range(3)]
        weights = jnp.concatenate([wb[a * 9 + step] for a in range(3)], axis=1)
        part_acc[...] += matmul_nt(jnp.concatenate(windows, axis=1), weights)

    finish_gx(lambda: None, lambda: None)
    for a in range(3):
        for side, x in ((0, 0), (1, 5)):
            moved = matmul(lift_z[a], gtake_x[side]).astype(BF)
            grad_shift[a, x] = moved[0:96].reshape(6, 16, 128)

    @pl.loop(0, 3)
    def _(c):
        for x, rows, b in ((0, 0, 2), (5, 192, 0)):
            windows = [grad_shift[2 - a, x, pl.ds(2 - c, 4)].reshape(64, 128) for a in range(3)]
            weights = jnp.concatenate([wb[a * 9 + 3 * b + c] for a in range(3)], axis=1)
            part_acc[rows : rows + 64] += matmul_nt(jnp.concatenate(windows, axis=1), weights)

    part_out[...] = matmul(perm_brick[...], part_acc[...].astype(BF)).astype(BF).reshape(4, 64, 512)
    part_copies = []
    for d in (1, 2, 3):
        peer = around(gz, d, 4)
        copy = remote(part_out.at[peer], part_in.at[d - 1], {"gz": peer})
        copy.start()
        part_copies.append(copy)

    bottle_taps(8, 13 + core, other)
    gb_first = remote(gb_all.at[pl.ds(other, 14)], gb_one, {"gy": gy ^ 1})
    gb_first.start()
    bottle_taps(0, 14 - core, mine)

    for copy in bottle_copies:
        copy.wait()
    for s in range(8):
        lifted = jnp.zeros((64, 128), F32)
        for q in range(4):
            lifted = lifted + matmul(bottle_in[q], wu[s, pl.ds(128 * q, 128)])
        total = lifted + hidden_sub[pl.ds(64 * s, 64)].astype(F32)
        fine_grad[pl.ds(64 * s, 64)] = total.astype(BF)
    out_ref[...] = matmul(perm_out[...], fine_grad[...]).astype(BF)

    gb_first.wait()

    @pl.loop(0, 14)
    def _(step):
        total = gb_all[mine + step].astype(F32) + gb_one[step].astype(F32)
        gb_all[mine + step] = total.astype(BF)

    def along_y(source_of, target):
        copies = []
        for d in (1, 2, 3):
            copy = remote(source_of(around(py, d, 4)), target.at[d - 1], {"gx": around(gx, 2 * d, 8)})
            copy.start()
            copies.append(copy)
        return copies

    def along_x(source_of, target):
        copies = []
        for d in (1, 2, 3):
            copy = remote(source_of(around(px, d, 4)), target.at[d - 1], {"gy": around(gy, 2 * d, 8)})
            copy.start()
            copies.append(copy)
        return copies

    def y_place(y):
        return {"gx": 2 * y + zh}

    def x_place(x):
        return {"gy": 2 * x + core}

    def begin_halving(position, place, mirrored, chunk, inbox):
        near, far = position ^ 1, 3 - position
        first, second = (far, near) if mirrored else (near, far)
        beyond = first ^ 1 if mirrored else 3 - first
        copies = [
            remote(chunk(first), inbox.at[0], place(first)), remote(chunk(beyond), inbox.at[1], place(first))
        ]
        for copy in copies:
            copy.start()

        def next_step():
            copies[1].wait()
            ref = chunk(second)
            ref[...] = (ref[...].astype(F32) + inbox[1].astype(F32)).astype(BF)
            last = remote(ref, inbox.at[2], place(second))
            last.start()
            copies[0].wait()

            def finish():
                own = chunk(position)
                total = own[...].astype(F32) + inbox[0].astype(F32)
                last.wait()
                return total + inbox[2].astype(F32)

            return finish

        return next_step

    parts = ((0, 4), (4, 3))
    inbox_a, inbox_b = (gb_ya, gb_ya2), (gb_xb, gb_xb2)
    inbox_c, inbox_d = (gb_xa, gb_xa2), (gb_yb, gb_yb2)
    gb_steps = []
    for i, (t, n) in enumerate(parts):
        gb_steps.append(begin_halving(
            py, y_place, i == 1, lambda y, t=t, n=n: gb_all.at[pl.ds(mine + t, n), y], inbox_a[i]
        ))
        gb_steps.append(begin_halving(
            px, x_place, i == 1, lambda x, t=t, n=n: gb_all.at[pl.ds(mine + 7 + t, n), :, :, x], inbox_b[i]
        ))

    for copy in part_copies:
        copy.wait()
    coarse_grad = part_out[gz].astype(F32)
    for d in range(3):
        coarse_grad = coarse_grad + part_in[d].astype(F32)
    coarse_grad = coarse_grad.astype(BF)
    for s in range(8):
        rows = pl.ds(64 * s, 64)
        spread = matmul_nt(coarse_grad, wd[s]) + cot_sub[rows].astype(F32)
        fine_grad[rows] = (spread * slope_sub[rows]).astype(BF)
    fine_grad[...] = matmul(perm_back[...], fine_grad[...]).astype(BF)

    def fine_taps(base):
        for step in range(4):
            lines = turned[pl.ds(base + 4 * step, 4)].reshape(512, 512)
            term = matmul(lines, fine_grad[...])
            gc_all[pl.ds(base + 4 * step, 4)] = term.astype(BF).reshape(4, 4, 32, 128)

    keep, give = core * 16, (1 - core) * 16
    fine_taps(give)
    gc_first = remote(gc_all.at[pl.ds(give, 16)], gc_one, {"gy": gy ^ 1})
    gc_first.start()
    fine_taps(keep)

    gc_first.wait()

    @pl.loop(0, 16)
    def _(step):
        total = gc_all[keep + step].astype(F32) + gc_one[step].astype(F32)
        gc_all[keep + step] = total.astype(BF)

    gc_second = along_x(lambda x: gc_all.at[pl.ds(keep + 2 * x, 2)], gc_xa)
    gc_second += along_y(lambda y: gc_all.at[pl.ds(keep + 8, 8), y], gc_yb)

    gb_ends = [step() for step in gb_steps]

    def summed(own, taken):
        total = own.astype(F32)
        for d in range(3):
            total = total + taken[d].astype(F32)
        return total

    for copy in gc_second:
        copy.wait()
    gc_a[...] = summed(gc_all[pl.ds(keep + 2 * px, 2)], gc_xa).astype(BF)
    gc_b[...] = summed(gc_all[pl.ds(keep + 8, 8), py], gc_yb).astype(BF)
    gc_third = along_y(lambda y: gc_a.at[:, y], gc_ya)
    gc_third += along_x(lambda x: gc_b.at[pl.ds(2 * x, 2)], gc_xb)

    gb_steps = []
    for i, (t, n) in enumerate(parts):
        gb_a[t : t + n] = gb_ends[2 * i]().astype(BF)
        gb_steps.append(begin_halving(
            px, x_place, i == 1, lambda x, t=t, n=n: gb_a.at[pl.ds(t, n), :, x], inbox_c[i]
        ))
        gb_b[t : t + n] = gb_ends[2 * i + 1]().astype(BF)
        gb_steps.append(begin_halving(
            py, y_place, i == 1, lambda y, t=t, n=n: gb_b.at[pl.ds(t, n), y], inbox_d[i]
        ))

    for copy in gc_third:
        copy.wait()
    gc_e2[0:2] = summed(gc_a[:, py], gc_ya).astype(BF).reshape(2, 2, 16, 128)
    gc_e2[2:4] = summed(gc_b[pl.ds(2 * px, 2)], gc_xb).astype(BF).reshape(2, 2, 16, 128)
    slot = zh * 4 + gz
    gc_fourth = []
    for d in range(4):
        peer = around(gz, d, 4)
        copy = remote(gc_e2.at[:, 1 - zh], gc_z.at[slot], {"gx": gx ^ 1, "gz": peer})
        copy.start()
        gc_fourth.append(copy)
        if d > 0:
            copy = remote(gc_e2.at[:, zh], gc_z.at[slot], {"gz": peer})
            copy.start()
            gc_fourth.append(copy)
    gc_z[slot] = gc_e2[:, zh]

    gb_last = [step() for step in gb_steps]
    for i, (t, n) in enumerate(parts):
        gb_d4[t : t + n] = gb_last[2 * i]().astype(BF)
        gb_d4[7 + t : 7 + t + n] = gb_last[2 * i + 1]().astype(BF)
    gb_fourth = remote(gb_d4.at[:, 1 - zh], gb_four, {"gx": gx ^ 1})
    gb_fourth.start()

    for copy in gc_fourth:
        copy.wait()
    total = gc_z[0].astype(F32)
    for q in range(1, 8):
        total = total + gc_z[q].astype(F32)
    for half in range(2):
        gc_half[half] = total[:, 8 * half : 8 * half + 8]
    gathers = []
    for d in range(1, 8):
        peer = around(gy, d, 8)
        copy = remote(gc_half.at[peer >> 2], gc_g.at[gy], {"gy": peer})
        copy.start()
        gathers.append(copy)
    gc_g[gy] = gc_half[gy >> 2]

    gb_fourth.wait()
    gb_d5[...] = (gb_d4[:, zh].astype(F32) + gb_four[...].astype(F32)).reshape(14, 2, 8, 128)
    gb_fifth = remote(gb_d5.at[:, 1 - core], gb_five, {"gy": gy ^ 1})
    gb_fifth.start()

    gb_fifth.wait()
    gb_ref[pl.ds(mine, 14)] = gb_d5[:, core]
    gb_ref[pl.ds(other, 14)] = gb_five[...]

    for copy in gathers:
        copy.wait()
    place = gy & 3
    for source in range(8):
        block = gc_g[source]
        chosen = jnp.zeros((4, 2, 128), F32)
        for j in range(4):
            chosen = chosen + jnp.where(place == j, block[:, 2 * j : 2 * j + 2, :], 0.0)
        first = (source & 1) * 16 + (source >> 1) * 2
        gc_ref[first : first + 2] = chosen[0:2]
        gc_ref[first + 8 : first + 10] = chosen[2:4]


def deliver_kernel(out_ref, gb_ref, gc_ref, out_final, gb_final, gc_final):
    out_final[...] = out_ref[...]
    gb_final[...] = gb_ref[0:TAPS]
    gc_final[...] = gc_ref[0:TAPS]


def body(volume, cotangent, w_conv, w_down, w_bottle, w_up):
    vmem = pltpu.VMEM
    whole = pl.BlockSpec(memory_space=pl.ANY)
    held = pl.BlockSpec(memory_space=pltpu.VMEM)
    def kept(*shape):
        return vmem(shape, BF)

    scratch = [
        kept(512, 128), kept(512, 128), kept(27, 128, 128), kept(8, 128, 512),
        kept(27, 512, 128), kept(8, 512, 128), pltpu.SemaphoreType.DMA((6,)),
        kept(512, 512), kept(512, 512), kept(512, 512), kept(512, 512), kept(512, 512),
        kept(3, 256, 256), kept(3, 128, 128), kept(256, 256), kept(3, 128, 128),
        kept(2, 64, 128), kept(2, 80, 128), kept(2, 80, 128), kept(2, 112, 128), kept(2, 112, 128),
        vmem((10, 10, 24, 128), F32), kept(27, 512, 128), kept(32, 128, 512), vmem((512, 128), F32),
        kept(512, 128), vmem((512, 128), F32), kept(512, 128),
        kept(4, 64, 128), kept(4, 64, 128), kept(4, 64, 512), kept(4, 32, 512), kept(3, 6, 6, 16, 512),
        kept(2, 64, 512), kept(2, 64, 512), kept(2, 32, 512), kept(4, 32, 512), vmem((256, 128), F32),
        kept(256, 128), kept(3, 6, 6, 16, 128), kept(2, 64, 128), kept(2, 64, 128),
        kept(2, 96, 128), kept(2, 128, 128),
        kept(4, 64, 128), kept(4, 64, 128), vmem((256, 512), F32), kept(4, 64, 512),
        kept(3, 64, 512), kept(512, 128),
        kept(28, 4, 2, 4, 16, 128), kept(14, 4, 2, 4, 16, 128),
        kept(3, 4, 2, 4, 16, 128), kept(3, 3, 2, 4, 16, 128), kept(3, 4, 4, 2, 16, 128), kept(3, 3, 4, 2, 16, 128),
        kept(7, 2, 4, 16, 128), kept(7, 4, 2, 16, 128),
        kept(3, 4, 2, 16, 128), kept(3, 3, 2, 16, 128), kept(3, 4, 2, 16, 128), kept(3, 3, 2, 16, 128),
        kept(14, 2, 16, 128), kept(14, 16, 128), vmem((14, 2, 8, 128), F32), vmem((14, 8, 128), F32),
        kept(32, 4, 32, 128), kept(16, 4, 32, 128), kept(3, 2, 4, 32, 128), kept(3, 8, 32, 128),
        kept(2, 4, 32, 128), kept(8, 32, 128), kept(3, 2, 32, 128), kept(3, 2, 32, 128),
        kept(4, 2, 16, 128), kept(8, 4, 16, 128), vmem((2, 4, 8, 128), F32), vmem((8, 4, 8, 128), F32),
        pltpu.SemaphoreType.DMA((COPIES,)), pltpu.SemaphoreType.DMA((COPIES,)),
    ]
    out, gb, gc = pl.pallas_call(
        level_kernel,
        out_shape=(
            jax.ShapeDtypeStruct((512, 128), BF),
            jax.ShapeDtypeStruct((28, 8, 128), F32),
            jax.ShapeDtypeStruct((32, 2, 128), F32),
        ),
        in_specs=[whole] * 6,
        out_specs=(held,) * 3,
        scratch_shapes=scratch,
        compiler_params=pltpu.CompilerParams(
            collective_id=0, has_side_effects=True, vmem_limit_bytes=60 * 1024 * 1024
        ),
        name="level",
    )(
        volume.reshape(512, 128),
        cotangent.reshape(512, 128),
        jnp.transpose(w_conv, (1, 0, 2)),
        w_down,
        jnp.transpose(w_bottle, (1, 0, 2)),
        w_up,
    )
    out, gb, gc = pl.pallas_call(
        deliver_kernel,
        out_shape=(
            jax.ShapeDtypeStruct(out.shape, BF),
            jax.ShapeDtypeStruct((TAPS, 8, 128), F32),
            jax.ShapeDtypeStruct((TAPS, 2, 128), F32),
        ),
        in_specs=[held] * 3,
        out_specs=(held,) * 3,
        name="deliver",
    )(out, gb, gc)
    return out.reshape(volume.shape), jnp.transpose(gc, (1, 0, 2)), jnp.transpose(gb, (1, 0, 2))


def solution(mesh):
    in_specs = (
        P("gz", "gx", "gy", None),
        P("gz", "gx", "gy", None),
        P(),
        P(),
        P(None, None, "gz"),
        P(),
    )
    out_specs = (
        P("gz", "gx", "gy", None),
        P(("gx", "gy"), None, None),
        P(("gx", "gy"), None, "gz"),
    )
    return jax.shard_map(body, mesh=mesh, in_specs=in_specs, out_specs=out_specs, check_vma=False)
```

```python
import jax
import jax.numpy as jnp
from jax import lax
from jax.experimental import pallas as pl
from jax.experimental.pallas import tpu as pltpu
from jax.sharding import PartitionSpec as P

BF = jnp.bfloat16
F32 = jnp.float32
MESH = pl.DeviceIdType.MESH
TAPS = 27
COPIES = 112


def matmul(left, right):
    return jnp.dot(left, right, preferred_element_type=F32)


def matmul_nt(left, right):
    return lax.dot_general(left, right, (((1,), (1,)), ((), ())), preferred_element_type=F32)


def matmul_tn(left, right):
    return lax.dot_general(left, right, (((0,), (0,)), ((), ())), preferred_element_type=F32)


def slope_of(values):
    sig = jax.nn.sigmoid(values)
    return sig * (1.0 + values * (1.0 - sig))


def selection(rows, columns, column_of):
    row = lax.broadcasted_iota(jnp.int32, (rows, 128), 0)
    lane = lax.broadcasted_iota(jnp.int32, (rows, 128), 1)
    target = column_of(row)
    blocks = [
        jnp.where(target == lane + 128 * block, 1.0, 0.0).astype(BF) for block in range(columns // 128)
    ]
    return jnp.concatenate(blocks, axis=1)


def cell_of_sub(row):
    s, k = row >> 6, row & 63
    x = 2 * (k >> 4) + ((s >> 1) & 1)
    y = 2 * ((k >> 2) & 3) + (s & 1)
    z = 2 * (k & 3) + (s >> 2)
    return x, y, z


def sub_of_cell(x, y, z):
    s = (z & 1) * 4 + (x & 1) * 2 + (y & 1)
    k = ((x >> 1) * 4 + (y >> 1)) * 4 + (z >> 1)
    return s * 64 + k


def level_kernel(
    vol_hbm, cot_hbm, wc_hbm, wd_hbm, wb_hbm, wu_hbm,
    out_ref, gb_ref, gc_ref,
    vol, cot, wc, wd, wb, wu, load_sem,
    perm_xyz, perm_sub, perm_cot, perm_back, perm_out, perm_group, perm_rim, perm_brick, lift_z,
    plane_z, face_main, take_main, face_y, take_y, face_x, take_x,
    padded, columns, turned, pre, cot_sub, slope_sub, hidden_sub,
    back_out, back_in, bricks, rims, shifted, rim_out, rim_in, corner_out, corner_in, pre_low,
    grad_now, grad_shift, gface_y, gtake_y, gface_x, gtake_x,
    bottle_out, bottle_in, part_acc, part_out, part_in, fine_grad,
    gb_all, gb_one, gb_ya, gb_ya2, gb_xb, gb_xb2, gb_a, gb_b, gb_xa, gb_xa2, gb_yb, gb_yb2, gb_d4, gb_four, gb_d5, gb_five,
    gc_all, gc_one, gc_xa, gc_yb, gc_a, gc_b, gc_ya, gc_xb, gc_e2, gc_z, gc_half, gc_g,
    send_sem, recv_sem,
):
    gx, gy, gz = lax.axis_index("gx"), lax.axis_index("gy"), lax.axis_index("gz")
    py, zh = gx >> 1, gx & 1
    px, core = gy >> 1, gy & 1
    used = [0]

    def remote(src, dst, device):
        slot = used[0]
        used[0] += 1
        return pltpu.make_async_remote_copy(
            src_ref=src, dst_ref=dst, send_sem=send_sem.at[slot], recv_sem=recv_sem.at[slot],
            device_id=device, device_id_type=MESH,
        )

    def around(position, step, count):
        return lax.rem(position + step, count)

    barrier = pltpu.get_barrier_semaphore()
    partners = [{"gx": around(gx, d, 8)} for d in (1, 2, 4, 6, 7)]
    partners += [{"gy": around(gy, d, 8)} for d in range(1, 8)]
    partners += [{"gz": around(gz, d, 4)} for d in (1, 2, 3)]
    partners += [{"gx": gx ^ 1, "gz": around(gz, d, 4)} for d in (1, 2, 3)]
    for partner in partners:
        pl.semaphore_signal(barrier, inc=1, device_id=partner, device_id_type=MESH)

    loads = [
        pltpu.make_async_copy(src, dst, load_sem.at[i])
        for i, (src, dst) in enumerate(
            ((vol_hbm, vol), (cot_hbm, cot), (wu_hbm, wu), (wc_hbm, wc), (wd_hbm, wd), (wb_hbm, wb))
        )
    ]
    for load in loads:
        load.start()

    padded[...] = jnp.zeros_like(padded)
    for side in (0, 5):
        for a in range(3):
            shifted[a, side] = jnp.zeros((6, 16, 512), BF)
            grad_shift[a, side] = jnp.zeros((6, 16, 128), BF)
    for tap in range(TAPS, 32):
        turned[tap] = jnp.zeros((128, 512), BF)
    gb_all[27] = jnp.zeros((4, 2, 4, 16, 128), BF)
    corner_in[2:4] = jnp.zeros((2, 32, 512), BF)
    for side in range(2):
        gtake_x[side, 96:128] = jnp.zeros((32, 128), BF)

    for side, edge in ((0, 0), (1, 7)):
        @pl.when(gx == edge)
        def _():
            rims[gz, 16 * side : 16 * side + 16] = jnp.zeros((16, 512), BF)
            gtake_x[side, 0:96] = jnp.zeros((96, 128), BF)

        @pl.when(gy == edge)
        def _():
            rim_in[side] = jnp.zeros((64, 512), BF)
            corner_in[side] = jnp.zeros((32, 512), BF)
            gtake_y[side] = jnp.zeros((64, 128), BF)

    def sub_to_xyz(row):
        x, y, z = cell_of_sub(row)
        return (x * 8 + y) * 8 + z

    def sub_to_zxy(row):
        x, y, z = cell_of_sub(row)
        return (z * 8 + x) * 8 + y

    perm_xyz[...] = selection(512, 512, lambda r: ((r & 7) * 8 + (r >> 6)) * 8 + ((r >> 3) & 7))
    perm_cot[...] = selection(512, 512, sub_to_zxy)

    loads[0].wait()
    pl.semaphore_wait(barrier, len(partners))

    def exchange(axis, position, count, low_src, high_dst, high_src, low_dst):
        down = remote(low_src, high_dst, {axis: around(position, count - 1, count)})
        up = remote(high_src, low_dst, {axis: around(position, 1, count)})

        @pl.when(position > 0)
        def _():
            down.start()

        @pl.when(position < count - 1)
        def _():
            up.start()

        def finish(on_low, on_high):
            @pl.when(position > 0)
            def _():
                down.wait_send()
                up.wait_recv()
                on_low()

            @pl.when(position < count - 1)
            def _():
                up.wait_send()
                down.wait_recv()
                on_high()

        return finish

    finish_z = exchange(
        "gz", gz, 4, vol.at[pl.ds(0, 64)], plane_z.at[1], vol.at[pl.ds(448, 64)], plane_z.at[0]
    )

    main = matmul(perm_xyz[...], vol[...])
    padded[1:9, 1:9, 8:16, :] = main.reshape(8, 8, 8, 128)
    face_main[0] = main[0:64].astype(BF)
    face_main[1] = main[448:512].astype(BF)
    finish_main = exchange(
        "gx", gx, 8, face_main.at[0], take_main.at[1], face_main.at[1], take_main.at[0]
    )

    loads[1].wait()
    cot_sub[...] = matmul(perm_cot[...], cot[...]).astype(BF)
    loads[2].wait()
    back = jnp.zeros((64, 512), F32)
    for s in range(8):
        back = back + matmul_nt(cot_sub[pl.ds(64 * s, 64)], wu[s])
    for q in range(4):
        back_out[q] = back[:, 128 * q : 128 * (q + 1)].astype(BF)
    back_copies = []
    for d in (1, 2, 3):
        peer = around(gz, d, 4)
        copy = remote(back_out.at[peer], back_in.at[gz], {"gz": peer})
        copy.start()
        back_copies.append(copy)
    back_in[gz] = back_out[gz]

    flat = padded.reshape(2400, 128)

    def at_row(x, y, z):
        return (x * 10 + y) * 24 + 7 + z

    def put_plane(side, z):
        plane = plane_z[side].astype(F32)
        for x in range(8):
            flat[pl.ds(at_row(x + 1, 1, z), 8, stride=24), :] = plane[8 * x : 8 * x + 8]

    finish_z(lambda: put_plane(0, 0), lambda: put_plane(1, 9))

    for side, y in ((0, 1), (1, 8)):
        face_y[side, 0:64] = padded[1:9, y, 8:16, :].reshape(64, 128).astype(BF)
        edges = [flat[pl.ds(at_row(1, y, z), 8, stride=240), :] for z in (0, 9)]
        face_y[side, 64:80] = jnp.concatenate(edges, axis=0).astype(BF)
    finish_y = exchange("gy", gy, 8, face_y.at[0], take_y.at[1], face_y.at[1], take_y.at[0])

    perm_sub[...] = selection(512, 512, sub_to_xyz)
    perm_back[...] = selection(512, 512, lambda r: sub_of_cell(r >> 6, (r >> 3) & 7, r & 7))
    perm_out[...] = selection(512, 512, lambda r: sub_of_cell((r >> 3) & 7, r & 7, r >> 6))

    def shifted_z(r, shift, column_of):
        z = (r & 15) + shift
        return jnp.where((z < 0) | (z > 15), -1, column_of(r, z & 15))

    for a in range(3):
        perm_group[a] = selection(
            256, 256, lambda r: shifted_z(r, a - 1, lambda r, z: (z >> 2) * 64 + (r >> 4) * 4 + (z & 3))
        )
        perm_rim[a] = selection(
            128, 128, lambda r: shifted_z(r, a - 1, lambda r, z: (z >> 2) * 32 + (r >> 4) * 4 + (z & 3))
        )
        lift_z[a] = selection(128, 128, lambda r: shifted_z(r, a - 1, lambda r, z: r - (r & 15) + z))
    perm_brick[...] = selection(256, 256, lambda r: ((r & 63) >> 2) * 16 + (r >> 6) * 4 + (r & 3))

    def put_y(side, y):
        face = take_y[side].astype(F32)
        padded[1:9, y, 8:16, :] = face[0:64].reshape(8, 8, 128)
        for i, z in enumerate((0, 9)):
            flat[pl.ds(at_row(1, y, z), 8, stride=240), :] = face[64 + 8 * i : 72 + 8 * i]

    finish_y(lambda: put_y(0, 0), lambda: put_y(1, 9))

    for side, x in ((0, 1), (1, 8)):
        ends = [padded[x, y, 8:16, :] for y in (0, 9)]
        face_x[side, 0:16] = jnp.concatenate(ends, axis=0).astype(BF)
        for i, z in enumerate((0, 9)):
            first = flat[pl.ds(at_row(x, 0, z), 8, stride=24), :]
            rest = flat[pl.ds(at_row(x, 2, z), 8, stride=24), :]
            face_x[side, 16 + 16 * i : 32 + 16 * i] = jnp.concatenate([first, rest], axis=0).astype(BF)
    finish_x = exchange("gx", gx, 8, face_x.at[0], take_x.at[1], face_x.at[1], take_x.at[0])

    loads[3].wait()
    pre[...] = jnp.zeros_like(pre)

    @pl.loop(0, 9, unroll=3)
    def _(step):
        b, c = step // 3, step % 3
        windows = [
            padded[pl.ds(b, 8), pl.ds(c, 8), 7 + a : 15 + a, :].reshape(512, 128).astype(BF) for a in range(3)
        ]
        for a in range(3):
            columns[a * 9 + step] = windows[a]
        weights = jnp.concatenate([wc[a * 9 + step] for a in range(3)], axis=0)
        pre[...] += matmul(jnp.concatenate(windows, axis=1), weights)

    def put_main(side, x):
        padded[x, 1:9, 8:16, :] = take_main[side].astype(F32).reshape(8, 8, 128)

    def put_x(side, x):
        face = take_x[side].astype(F32)
        padded[x, 0, 8:16, :] = face[0:8]
        padded[x, 9, 8:16, :] = face[8:16]
        for i, z in enumerate((0, 9)):
            flat[pl.ds(at_row(x, 0, z), 8, stride=24), :] = face[16 + 16 * i : 24 + 16 * i]
            flat[pl.ds(at_row(x, 2, z), 8, stride=24), :] = face[24 + 16 * i : 32 + 16 * i]

    finish_main(lambda: put_main(0, 0), lambda: put_main(1, 9))
    finish_x(lambda: put_x(0, 0), lambda: put_x(1, 9))

    for c in range(3):
        for x, first, b in ((0, 0, 0), (9, 448, 2)):
            windows = [padded[x, c : c + 8, 7 + a : 15 + a, :].reshape(64, 128).astype(BF) for a in range(3)]
            for a in range(3):
                columns[a * 9 + 3 * b + c, first : first + 64] = windows[a]
            weights = jnp.concatenate([wc[a * 9 + 3 * b + c] for a in range(3)], axis=0)
            pre[first : first + 64] += matmul(jnp.concatenate(windows, axis=1), weights)

    high = pre[...].astype(BF)
    low = (pre[...] - high.astype(F32)).astype(BF)
    pre_sub = matmul(perm_sub[...], high) + matmul(perm_sub[...], low)
    hidden_sub[...] = jax.nn.silu(pre_sub).astype(BF)
    slope_sub[...] = slope_of(pre_sub)

    loads[4].wait()
    coarse = jnp.zeros((64, 512), F32)
    for s in range(8):
        coarse = coarse + matmul(hidden_sub[pl.ds(64 * s, 64)], wd[s])
    bricks[gz] = coarse.astype(BF)

    finish_cx = exchange(
        "gx", gx, 8,
        bricks.at[gz, pl.ds(0, 16)], rims.at[gz, pl.ds(16, 16)],
        bricks.at[gz, pl.ds(48, 16)], rims.at[gz, pl.ds(0, 16)],
    )

    def send_column(ref):
        copies = []
        for d in (1, 2, 3):
            copy = remote(ref.at[gz], ref.at[gz], {"gz": around(gz, d, 4)})
            copy.start()
            copies.append(copy)
        return copies

    brick_copies = send_column(bricks)

    def turn(first, last):
        @pl.loop(first, last)
        def _(tap):
            turned[tap] = columns[tap].T

    turn(0, 16)
    finish_cx(lambda: None, lambda: None)
    rim_copies = send_column(rims)
    turn(16, 27)

    for copy in brick_copies:
        copy.wait()
    stack = bricks[...].reshape(256, 512)
    middle = matmul(perm_group[1], stack).astype(BF).reshape(4, 4, 16, 512)
    for side, y in ((0, 0), (1, 3)):
        rim_out[side] = middle[:, y].reshape(64, 512)
    finish_cy = exchange("gy", gy, 8, rim_out.at[0], rim_in.at[1], rim_out.at[1], rim_in.at[0])
    shifted[1, 1:5, 1:5] = middle
    for a in (0, 2):
        shifted[a, 1:5, 1:5] = matmul(perm_group[a], stack).astype(BF).reshape(4, 4, 16, 512)
    for copy in back_copies:
        copy.wait()
    back_column = matmul(perm_group[1], back_in[...].reshape(256, 128))

    loads[5].wait()
    finish_cy(lambda: None, lambda: None)
    for a in range(3):
        sides = matmul(lift_z[a], rim_in[...].reshape(128, 512)).astype(BF).reshape(2, 4, 16, 512)
        shifted[a, 1:5, 0] = sides[0]
        shifted[a, 1:5, 5] = sides[1]

    pre_low[...] = jnp.zeros_like(pre_low)

    def low_taps(first, last):
        @pl.loop(first, last, unroll=3)
        def _(step):
            b, c = step // 3, step % 3
            total = pre_low[...]
            for a in range(3):
                window = shifted[a, pl.ds(b, 4), pl.ds(c, 4)].reshape(256, 512)
                total = total + matmul(window, wb[a * 9 + step])
            pre_low[...] = total

    low_taps(0, 6)
    for copy in rim_copies:
        copy.wait()
    rim_rows = []
    for a in range(3):
        rim_rows.append(matmul(perm_rim[a], rims[...].reshape(128, 512)).astype(BF).reshape(2, 4, 16, 512))
    for side, y in ((0, 0), (1, 3)):
        corner_out[side] = rim_rows[1][:, y].reshape(32, 512)
    finish_cc = exchange("gy", gy, 8, corner_out.at[0], corner_in.at[1], corner_out.at[1], corner_in.at[0])
    low_taps(6, 9)
    for a in range(3):
        shifted[a, 0, 1:5] = rim_rows[a][0]
        shifted[a, 5, 1:5] = rim_rows[a][1]
    finish_cc(lambda: None, lambda: None)
    for a in range(3):
        corners = matmul(lift_z[a], corner_in[...].reshape(128, 512)).astype(BF).reshape(4, 2, 16, 512)
        for i, y in ((0, 0), (1, 5)):
            shifted[a, 0, y] = corners[i, 0]
            shifted[a, 5, y] = corners[i, 1]

    @pl.loop(0, 3)
    def _(c):
        low, high = pre_low[0:64], pre_low[192:256]
        for a in range(3):
            low = low + matmul(shifted[a, 0, pl.ds(c, 4)].reshape(64, 512), wb[a * 9 + c])
            high = high + matmul(shifted[a, 5, pl.ds(c, 4)].reshape(64, 512), wb[a * 9 + 6 + c])
        pre_low[0:64] = low
        pre_low[192:256] = high

    bottle_grad = (back_column * slope_of(pre_low[...])).astype(BF)
    grad_now[...] = bottle_grad
    middle = bottle_grad.astype(F32).reshape(4, 4, 16, 128)
    for side, y in ((0, 0), (1, 3)):
        gface_y[side] = middle[:, y].reshape(64, 128).astype(BF)
    finish_gy = exchange("gy", gy, 8, gface_y.at[0], gtake_y.at[1], gface_y.at[1], gtake_y.at[0])

    bottle = jax.nn.silu(pre_low[...]).astype(BF)
    bottle_out[...] = matmul(perm_brick[...], bottle).astype(BF).reshape(4, 64, 128)
    bottle_copies = []
    for d in (1, 2, 3):
        peer = around(gz, d, 4)
        copy = remote(bottle_out.at[peer], bottle_in.at[gz], {"gz": peer})
        copy.start()
        bottle_copies.append(copy)
    bottle_in[gz] = bottle_out[gz]

    for a in range(3):
        for half in range(2):
            moved = matmul(lift_z[a], grad_now[pl.ds(128 * half, 128)]).astype(BF)
            grad_shift[a, 1 + 2 * half : 3 + 2 * half, 1:5] = moved.reshape(2, 4, 16, 128)

    mine, other = core * 14, (1 - core) * 14

    def bottle_taps(first, last, base):
        @pl.loop(first, last)
        def _(step):
            tap = base + step
            depth, across = tap // 9, tap % 9
            b, c = across // 3, across % 3
            window = shifted[depth, pl.ds(b, 4), pl.ds(c, 4)].reshape(256, 512)
            gb_all[tap] = matmul_tn(window, grad_now[...]).astype(BF).reshape(4, 2, 4, 16, 128)

    bottle_taps(0, 8, other)
    finish_gy(lambda: None, lambda: None)
    for a in range(3):
        sides = matmul(lift_z[a], gtake_y[...].reshape(128, 128)).astype(BF).reshape(2, 4, 16, 128)
        grad_shift[a, 1:5, 0] = sides[0]
        grad_shift[a, 1:5, 5] = sides[1]
    for side, x in ((0, 1), (1, 4)):
        gface_x[side] = grad_shift[1, x].reshape(96, 128)
    finish_gx = exchange(
        "gx", gx, 8,
        gface_x.at[0], gtake_x.at[1, pl.ds(0, 96)], gface_x.at[1], gtake_x.at[0, pl.ds(0, 96)],
    )

    part_acc[...] = jnp.zeros_like(part_acc)

    @pl.loop(0, 9, unroll=3)
    def _(step):
        b, c = step // 3, step % 3
        windows = [grad_shift[2 - a, pl.ds(2 - b, 4), pl.ds(2 - c, 4)].reshape(256, 128) for a in range(3)]
        weights = jnp.concatenate([wb[a * 9 + step] for a in range(3)], axis=1)
        part_acc[...] += matmul_nt(jnp.concatenate(windows, axis=1), weights)

    finish_gx(lambda: None, lambda: None)
    for a in range(3):
        for side, x in ((0, 0), (1, 5)):
            moved = matmul(lift_z[a], gtake_x[side]).astype(BF)
            grad_shift[a, x] = moved[0:96].reshape(6, 16, 128)

    @pl.loop(0, 3)
    def _(c):
        for x, rows, b in ((0, 0, 2), (5, 192, 0)):
            windows = [grad_shift[2 - a, x, pl.ds(2 - c, 4)].reshape(64, 128) for a in range(3)]
            weights = jnp.concatenate([wb[a * 9 + 3 * b + c] for a in range(3)], axis=1)
            part_acc[rows : rows + 64] += matmul_nt(jnp.concatenate(windows, axis=1), weights)

    part_out[...] = matmul(perm_brick[...], part_acc[...].astype(BF)).astype(BF).reshape(4, 64, 512)
    part_copies = []
    for d in (1, 2, 3):
        peer = around(gz, d, 4)
        copy = remote(part_out.at[peer], part_in.at[d - 1], {"gz": peer})
        copy.start()
        part_copies.append(copy)

    bottle_taps(8, 13 + core, other)
    gb_first = remote(gb_all.at[pl.ds(other, 14)], gb_one, {"gy": gy ^ 1})
    gb_first.start()
    bottle_taps(0, 14 - core, mine)

    for copy in bottle_copies:
        copy.wait()
    for s in range(8):
        lifted = jnp.zeros((64, 128), F32)
        for q in range(4):
            lifted = lifted + matmul(bottle_in[q], wu[s, pl.ds(128 * q, 128)])
        total = lifted + hidden_sub[pl.ds(64 * s, 64)].astype(F32)
        fine_grad[pl.ds(64 * s, 64)] = total.astype(BF)
    out_ref[...] = matmul(perm_out[...], fine_grad[...]).astype(BF)

    gb_first.wait()

    @pl.loop(0, 14)
    def _(step):
        total = gb_all[mine + step].astype(F32) + gb_one[step].astype(F32)
        gb_all[mine + step] = total.astype(BF)

    def along_y(source_of, target):
        copies = []
        for d in (1, 2, 3):
            copy = remote(source_of(around(py, d, 4)), target.at[d - 1], {"gx": around(gx, 2 * d, 8)})
            copy.start()
            copies.append(copy)
        return copies

    def along_x(source_of, target):
        copies = []
        for d in (1, 2, 3):
            copy = remote(source_of(around(px, d, 4)), target.at[d - 1], {"gy": around(gy, 2 * d, 8)})
            copy.start()
            copies.append(copy)
        return copies

    def y_place(y):
        return {"gx": 2 * y + zh}

    def x_place(x):
        return {"gy": 2 * x + core}

    def begin_halving(position, place, mirrored, chunk, inbox):
        near, far = position ^ 1, 3 - position
        first, second = (far, near) if mirrored else (near, far)
        beyond = first ^ 1 if mirrored else 3 - first
        copies = [
            remote(chunk(first), inbox.at[0], place(first)), remote(chunk(beyond), inbox.at[1], place(first))
        ]
        for copy in copies:
            copy.start()

        def next_step():
            copies[1].wait()
            ref = chunk(second)
            ref[...] = (ref[...].astype(F32) + inbox[1].astype(F32)).astype(BF)
            last = remote(ref, inbox.at[2], place(second))
            last.start()
            copies[0].wait()

            def finish():
                own = chunk(position)
                total = own[...].astype(F32) + inbox[0].astype(F32)
                last.wait()
                return total + inbox[2].astype(F32)

            return finish

        return next_step

    parts = ((0, 4), (4, 3))
    inbox_a, inbox_b = (gb_ya, gb_ya2), (gb_xb, gb_xb2)
    inbox_c, inbox_d = (gb_xa, gb_xa2), (gb_yb, gb_yb2)
    gb_steps = []
    for i, (t, n) in enumerate(parts):
        gb_steps.append(begin_halving(
            py, y_place, i == 1, lambda y, t=t, n=n: gb_all.at[pl.ds(mine + t, n), y], inbox_a[i]
        ))
        gb_steps.append(begin_halving(
            px, x_place, i == 1, lambda x, t=t, n=n: gb_all.at[pl.ds(mine + 7 + t, n), :, :, x], inbox_b[i]
        ))

    for copy in part_copies:
        copy.wait()
    coarse_grad = part_out[gz].astype(F32)
    for d in range(3):
        coarse_grad = coarse_grad + part_in[d].astype(F32)
    coarse_grad = coarse_grad.astype(BF)
    for s in range(8):
        rows = pl.ds(64 * s, 64)
        spread = matmul_nt(coarse_grad, wd[s]) + cot_sub[rows].astype(F32)
        fine_grad[rows] = (spread * slope_sub[rows]).astype(BF)
    fine_grad[...] = matmul(perm_back[...], fine_grad[...]).astype(BF)

    def fine_taps(base):
        for step in range(4):
            lines = turned[pl.ds(base + 4 * step, 4)].reshape(512, 512)
            term = matmul(lines, fine_grad[...])
            gc_all[pl.ds(base + 4 * step, 4)] = term.astype(BF).reshape(4, 4, 32, 128)

    keep, give = core * 16, (1 - core) * 16
    fine_taps(give)
    gc_first = remote(gc_all.at[pl.ds(give, 16)], gc_one, {"gy": gy ^ 1})
    gc_first.start()
    fine_taps(keep)

    gc_first.wait()

    @pl.loop(0, 16)
    def _(step):
        total = gc_all[keep + step].astype(F32) + gc_one[step].astype(F32)
        gc_all[keep + step] = total.astype(BF)

    gc_second = along_x(lambda x: gc_all.at[pl.ds(keep + 2 * x, 2)], gc_xa)
    gc_second += along_y(lambda y: gc_all.at[pl.ds(keep + 8, 8), y], gc_yb)

    gb_ends = [step() for step in gb_steps]

    def summed(own, taken):
        total = own.astype(F32)
        for d in range(3):
            total = total + taken[d].astype(F32)
        return total

    for copy in gc_second:
        copy.wait()
    gc_a[...] = summed(gc_all[pl.ds(keep + 2 * px, 2)], gc_xa).astype(BF)
    gc_b[...] = summed(gc_all[pl.ds(keep + 8, 8), py], gc_yb).astype(BF)
    gc_third = along_y(lambda y: gc_a.at[:, y], gc_ya)
    gc_third += along_x(lambda x: gc_b.at[pl.ds(2 * x, 2)], gc_xb)

    gb_steps = []
    for i, (t, n) in enumerate(parts):
        gb_a[t : t + n] = gb_ends[2 * i]().astype(BF)
        gb_steps.append(begin_halving(
            px, x_place, i == 1, lambda x, t=t, n=n: gb_a.at[pl.ds(t, n), :, x], inbox_c[i]
        ))
        gb_b[t : t + n] = gb_ends[2 * i + 1]().astype(BF)
        gb_steps.append(begin_halving(
            py, y_place, i == 1, lambda y, t=t, n=n: gb_b.at[pl.ds(t, n), y], inbox_d[i]
        ))

    for copy in gc_third:
        copy.wait()
    gc_e2[0:2] = summed(gc_a[:, py], gc_ya).astype(BF).reshape(2, 2, 16, 128)
    gc_e2[2:4] = summed(gc_b[pl.ds(2 * px, 2)], gc_xb).astype(BF).reshape(2, 2, 16, 128)
    slot = zh * 4 + gz
    gc_fourth = []
    for d in range(4):
        peer = around(gz, d, 4)
        copy = remote(gc_e2.at[:, 1 - zh], gc_z.at[slot], {"gx": gx ^ 1, "gz": peer})
        copy.start()
        gc_fourth.append(copy)
        if d > 0:
            copy = remote(gc_e2.at[:, zh], gc_z.at[slot], {"gz": peer})
            copy.start()
            gc_fourth.append(copy)
    gc_z[slot] = gc_e2[:, zh]

    gb_last = [step() for step in gb_steps]
    for i, (t, n) in enumerate(parts):
        gb_d4[t : t + n] = gb_last[2 * i]().astype(BF)
        gb_d4[7 + t : 7 + t + n] = gb_last[2 * i + 1]().astype(BF)
    gb_fourth = remote(gb_d4.at[:, 1 - zh], gb_four, {"gx": gx ^ 1})
    gb_fourth.start()

    for copy in gc_fourth:
        copy.wait()
    total = gc_z[0].astype(F32)
    for q in range(1, 8):
        total = total + gc_z[q].astype(F32)
    for half in range(2):
        gc_half[half] = total[:, 8 * half : 8 * half + 8]
    gathers = []
    for d in range(1, 8):
        peer = around(gy, d, 8)
        copy = remote(gc_half.at[peer >> 2], gc_g.at[gy], {"gy": peer})
        copy.start()
        gathers.append(copy)
    gc_g[gy] = gc_half[gy >> 2]

    gb_fourth.wait()
    gb_d5[...] = (gb_d4[:, zh].astype(F32) + gb_four[...].astype(F32)).reshape(14, 2, 8, 128)
    gb_fifth = remote(gb_d5.at[:, 1 - core], gb_five, {"gy": gy ^ 1})
    gb_fifth.start()

    gb_fifth.wait()
    gb_ref[pl.ds(mine, 14)] = gb_d5[:, core]
    gb_ref[pl.ds(other, 14)] = gb_five[...]

    for copy in gathers:
        copy.wait()
    place = gy & 3
    for source in range(8):
        block = gc_g[source]
        chosen = jnp.zeros((4, 2, 128), F32)
        for j in range(4):
            chosen = chosen + jnp.where(place == j, block[:, 2 * j : 2 * j + 2, :], 0.0)
        first = (source & 1) * 16 + (source >> 1) * 2
        gc_ref[first : first + 2] = chosen[0:2]
        gc_ref[first + 8 : first + 10] = chosen[2:4]


def deliver_kernel(out_ref, gb_ref, gc_ref, out_final, gb_final, gc_final):
    out_final[...] = out_ref[...]
    gb_final[...] = gb_ref[0:TAPS]
    gc_final[...] = gc_ref[0:TAPS]


def body(volume, cotangent, w_conv, w_down, w_bottle, w_up):
    vmem = pltpu.VMEM
    whole = pl.BlockSpec(memory_space=pl.ANY)
    held = pl.BlockSpec(memory_space=pltpu.VMEM)
    def kept(*shape):
        return vmem(shape, BF)

    scratch = [
        kept(512, 128), kept(512, 128), kept(27, 128, 128), kept(8, 128, 512),
        kept(27, 512, 128), kept(8, 512, 128), pltpu.SemaphoreType.DMA((6,)),
        kept(512, 512), kept(512, 512), kept(512, 512), kept(512, 512), kept(512, 512),
        kept(3, 256, 256), kept(3, 128, 128), kept(256, 256), kept(3, 128, 128),
        kept(2, 64, 128), kept(2, 64, 128), kept(2, 64, 128), kept(2, 80, 128), kept(2, 80, 128),
        kept(2, 48, 128), kept(2, 48, 128),
        vmem((10, 10, 24, 128), F32), kept(27, 512, 128), kept(32, 128, 512), vmem((512, 128), F32),
        kept(512, 128), vmem((512, 128), F32), kept(512, 128),
        kept(4, 64, 128), kept(4, 64, 128), kept(4, 64, 512), kept(4, 32, 512), kept(3, 6, 6, 16, 512),
        kept(2, 64, 512), kept(2, 64, 512), kept(2, 32, 512), kept(4, 32, 512), vmem((256, 128), F32),
        kept(256, 128), kept(3, 6, 6, 16, 128), kept(2, 64, 128), kept(2, 64, 128),
        kept(2, 96, 128), kept(2, 128, 128),
        kept(4, 64, 128), kept(4, 64, 128), vmem((256, 512), F32), kept(4, 64, 512),
        kept(3, 64, 512), kept(512, 128),
        kept(28, 4, 2, 4, 16, 128), kept(14, 4, 2, 4, 16, 128),
        kept(3, 4, 2, 4, 16, 128), kept(3, 3, 2, 4, 16, 128), kept(3, 4, 4, 2, 16, 128), kept(3, 3, 4, 2, 16, 128),
        kept(7, 2, 4, 16, 128), kept(7, 4, 2, 16, 128),
        kept(3, 4, 2, 16, 128), kept(3, 3, 2, 16, 128), kept(3, 4, 2, 16, 128), kept(3, 3, 2, 16, 128),
        kept(14, 2, 16, 128), kept(14, 16, 128), vmem((14, 2, 8, 128), F32), vmem((14, 8, 128), F32),
        kept(32, 4, 32, 128), kept(16, 4, 32, 128), kept(3, 2, 4, 32, 128), kept(3, 8, 32, 128),
        kept(2, 4, 32, 128), kept(8, 32, 128), kept(3, 2, 32, 128), kept(3, 2, 32, 128),
        kept(4, 2, 16, 128), kept(8, 4, 16, 128), vmem((2, 4, 8, 128), F32), vmem((8, 4, 8, 128), F32),
        pltpu.SemaphoreType.DMA((COPIES,)), pltpu.SemaphoreType.DMA((COPIES,)),
    ]
    out, gb, gc = pl.pallas_call(
        level_kernel,
        out_shape=(
            jax.ShapeDtypeStruct((512, 128), BF),
            jax.ShapeDtypeStruct((28, 8, 128), F32),
            jax.ShapeDtypeStruct((32, 2, 128), F32),
        ),
        in_specs=[whole] * 6,
        out_specs=(held,) * 3,
        scratch_shapes=scratch,
        compiler_params=pltpu.CompilerParams(
            collective_id=0, has_side_effects=True, vmem_limit_bytes=60 * 1024 * 1024
        ),
        name="level",
    )(
        volume.reshape(512, 128),
        cotangent.reshape(512, 128),
        jnp.transpose(w_conv, (1, 0, 2)),
        w_down,
        jnp.transpose(w_bottle, (1, 0, 2)),
        w_up,
    )
    out, gb, gc = pl.pallas_call(
        deliver_kernel,
        out_shape=(
            jax.ShapeDtypeStruct(out.shape, BF),
            jax.ShapeDtypeStruct((TAPS, 8, 128), F32),
            jax.ShapeDtypeStruct((TAPS, 2, 128), F32),
        ),
        in_specs=[held] * 3,
        out_specs=(held,) * 3,
        name="deliver",
    )(out, gb, gc)
    return out.reshape(volume.shape), jnp.transpose(gc, (1, 0, 2)), jnp.transpose(gb, (1, 0, 2))


def solution(mesh):
    in_specs = (
        P("gz", "gx", "gy", None),
        P("gz", "gx", "gy", None),
        P(),
        P(),
        P(None, None, "gz"),
        P(),
    )
    out_specs = (
        P("gz", "gx", "gy", None),
        P(("gx", "gy"), None, None),
        P(("gx", "gy"), None, "gz"),
    )
    return jax.shard_map(body, mesh=mesh, in_specs=in_specs, out_specs=out_specs, check_vma=False)
```

```python
import jax
import jax.numpy as jnp
from jax import lax
from jax.experimental import pallas as pl
from jax.experimental.pallas import tpu as pltpu
from jax.sharding import PartitionSpec as P

BF = jnp.bfloat16
F32 = jnp.float32
MESH = pl.DeviceIdType.MESH
TAPS = 27
COPIES = 112


def matmul(left, right):
    return jnp.dot(left, right, preferred_element_type=F32)


def matmul_nt(left, right):
    return lax.dot_general(left, right, (((1,), (1,)), ((), ())), preferred_element_type=F32)


def matmul_tn(left, right):
    return lax.dot_general(left, right, (((0,), (0,)), ((), ())), preferred_element_type=F32)


def slope_of(values):
    sig = jax.nn.sigmoid(values)
    return sig * (1.0 + values * (1.0 - sig))


def selection(rows, columns, column_of):
    row = lax.broadcasted_iota(jnp.int32, (rows, 128), 0)
    lane = lax.broadcasted_iota(jnp.int32, (rows, 128), 1)
    target = column_of(row)
    blocks = [
        jnp.where(target == lane + 128 * block, 1.0, 0.0).astype(BF) for block in range(columns // 128)
    ]
    return jnp.concatenate(blocks, axis=1)


def cell_of_sub(row):
    s, k = row >> 6, row & 63
    x = 2 * (k >> 4) + ((s >> 1) & 1)
    y = 2 * ((k >> 2) & 3) + (s & 1)
    z = 2 * (k & 3) + (s >> 2)
    return x, y, z


def sub_of_cell(x, y, z):
    s = (z & 1) * 4 + (x & 1) * 2 + (y & 1)
    k = ((x >> 1) * 4 + (y >> 1)) * 4 + (z >> 1)
    return s * 64 + k


def level_kernel(
    vol_hbm, cot_hbm, wc_hbm, wd_hbm, wb_hbm, wu_hbm,
    out_ref, gb_ref, gc_ref,
    vol, cot, wc, wd, wb, wu, load_sem,
    perm_xyz, perm_sub, perm_cot, perm_back, perm_out, perm_group, perm_rim, perm_brick, perm_part, lift_z,
    plane_z, face_main, take_main, face_y, take_y, face_x, take_x,
    padded, columns, turned, pre, cot_sub, slope_sub, hidden_sub,
    back_out, back_in, bricks, rims, shifted, rim_out, rim_in, corner_out, corner_in, pre_low,
    grad_now, grad_shift, gface_y, gtake_y, gface_x, gtake_x,
    bottle_out, bottle_in, part_acc, part_out, part_in, fine_grad,
    gb_all, gb_one, gb_ya, gb_ya2, gb_xb, gb_xb2, gb_a, gb_b, gb_xa, gb_xa2, gb_yb, gb_yb2, gb_d4, gb_four, gb_d5, gb_five,
    gc_all, gc_one, gc_xa, gc_yb, gc_a, gc_b, gc_ya, gc_xb, gc_e2, gc_z, gc_half, gc_g,
    send_sem, recv_sem,
):
    gx, gy, gz = lax.axis_index("gx"), lax.axis_index("gy"), lax.axis_index("gz")
    py, zh = gx >> 1, gx & 1
    px, core = gy >> 1, gy & 1
    used = [0]

    def remote(src, dst, device):
        slot = used[0]
        used[0] += 1
        return pltpu.make_async_remote_copy(
            src_ref=src, dst_ref=dst, send_sem=send_sem.at[slot], recv_sem=recv_sem.at[slot],
            device_id=device, device_id_type=MESH,
        )

    def around(position, step, count):
        return lax.rem(position + step, count)

    barrier = pltpu.get_barrier_semaphore()
    partners = [{"gx": around(gx, d, 8)} for d in (1, 2, 4, 6, 7)]
    partners += [{"gy": around(gy, d, 8)} for d in range(1, 8)]
    partners += [{"gz": around(gz, d, 4)} for d in (1, 2, 3)]
    partners += [{"gx": gx ^ 1, "gz": around(gz, d, 4)} for d in (1, 2, 3)]
    for partner in partners:
        pl.semaphore_signal(barrier, inc=1, device_id=partner, device_id_type=MESH)

    loads = [
        pltpu.make_async_copy(src, dst, load_sem.at[i])
        for i, (src, dst) in enumerate(
            ((vol_hbm, vol), (cot_hbm, cot), (wu_hbm, wu), (wc_hbm, wc), (wd_hbm, wd), (wb_hbm, wb))
        )
    ]
    for load in loads:
        load.start()

    def sub_to_xyz(row):
        x, y, z = cell_of_sub(row)
        return (x * 8 + y) * 8 + z

    def sub_to_zxy(row):
        x, y, z = cell_of_sub(row)
        return (z * 8 + x) * 8 + y

    perm_xyz[...] = selection(512, 512, lambda r: ((r & 7) * 8 + (r >> 6)) * 8 + ((r >> 3) & 7))

    loads[0].wait()
    main = matmul(perm_xyz[...], vol[...])
    face_main[0] = main[0:64].astype(BF)
    face_main[1] = main[448:512].astype(BF)
    pl.semaphore_wait(barrier, len(partners))

    def exchange(axis, position, count, low_src, high_dst, high_src, low_dst):
        down = remote(low_src, high_dst, {axis: around(position, count - 1, count)})
        up = remote(high_src, low_dst, {axis: around(position, 1, count)})

        @pl.when(position > 0)
        def _():
            down.start()

        @pl.when(position < count - 1)
        def _():
            up.start()

        def finish(on_low, on_high):
            @pl.when(position > 0)
            def _():
                down.wait_send()
                up.wait_recv()
                on_low()

            @pl.when(position < count - 1)
            def _():
                up.wait_send()
                down.wait_recv()
                on_high()

        return finish

    finish_z = exchange(
        "gz", gz, 4, vol.at[pl.ds(0, 64)], plane_z.at[1], vol.at[pl.ds(448, 64)], plane_z.at[0]
    )

    finish_main = exchange(
        "gx", gx, 8, face_main.at[0], take_main.at[1], face_main.at[1], take_main.at[0]
    )

    padded[...] = jnp.zeros_like(padded)
    for side in (0, 5):
        for a in range(3):
            shifted[a, side] = jnp.zeros((6, 16, 512), BF)
            grad_shift[a, side] = jnp.zeros((6, 16, 128), BF)
    for tap in range(TAPS, 32):
        turned[tap] = jnp.zeros((128, 512), BF)
    gb_all[27] = jnp.zeros((4, 2, 4, 16, 128), BF)
    corner_in[2:4] = jnp.zeros((2, 32, 512), BF)
    for side in range(2):
        gtake_x[side, 96:128] = jnp.zeros((32, 128), BF)

    for side, edge in ((0, 0), (1, 7)):
        @pl.when(gx == edge)
        def _():
            rims[gz, 16 * side : 16 * side + 16] = jnp.zeros((16, 512), BF)
            gtake_x[side, 0:96] = jnp.zeros((96, 128), BF)

        @pl.when(gy == edge)
        def _():
            rim_in[side] = jnp.zeros((64, 512), BF)
            corner_in[side] = jnp.zeros((32, 512), BF)
            gtake_y[side] = jnp.zeros((64, 128), BF)
    padded[1:9, 1:9, 8:16, :] = main.reshape(8, 8, 8, 128)
    perm_cot[...] = selection(512, 512, sub_to_zxy)

    loads[1].wait()
    cot_sub[...] = matmul(perm_cot[...], cot[...]).astype(BF)
    loads[2].wait()
    back = jnp.zeros((64, 512), F32)
    for s in range(8):
        back = back + matmul_nt(cot_sub[pl.ds(64 * s, 64)], wu[s])
    for q in range(4):
        back_out[q] = back[:, 128 * q : 128 * (q + 1)].astype(BF)
    back_copies = []
    for d in (1, 2, 3):
        peer = around(gz, d, 4)
        copy = remote(back_out.at[peer], back_in.at[gz], {"gz": peer})
        copy.start()
        back_copies.append(copy)
    back_in[gz] = back_out[gz]

    flat = padded.reshape(2400, 128)

    def at_row(x, y, z):
        return (x * 10 + y) * 24 + 7 + z

    def put_plane(side, z):
        plane = plane_z[side].astype(F32)
        for x in range(8):
            flat[pl.ds(at_row(x + 1, 1, z), 8, stride=24), :] = plane[8 * x : 8 * x + 8]

    finish_z(lambda: put_plane(0, 0), lambda: put_plane(1, 9))

    for side, y in ((0, 1), (1, 8)):
        face_y[side, 0:64] = padded[1:9, y, 8:16, :].reshape(64, 128).astype(BF)
        edges = [flat[pl.ds(at_row(1, y, z), 8, stride=240), :] for z in (0, 9)]
        face_y[side, 64:80] = jnp.concatenate(edges, axis=0).astype(BF)
    finish_y = exchange("gy", gy, 8, face_y.at[0], take_y.at[1], face_y.at[1], take_y.at[0])

    perm_sub[...] = selection(512, 512, sub_to_xyz)
    perm_back[...] = selection(512, 512, lambda r: sub_of_cell(r >> 6, (r >> 3) & 7, r & 7))
    perm_out[...] = selection(512, 512, lambda r: sub_of_cell((r >> 3) & 7, r & 7, r >> 6))

    perm_part[...] = selection(128, 128, lambda r: ((r & 31) >> 2) * 16 + (r >> 5) * 4 + (r & 3))

    def shifted_z(r, shift, column_of):
        z = (r & 15) + shift
        return jnp.where((z < 0) | (z > 15), -1, column_of(r, z & 15))

    for a in range(3):
        perm_group[a] = selection(
            256, 256, lambda r: shifted_z(r, a - 1, lambda r, z: (z >> 2) * 64 + (r >> 4) * 4 + (z & 3))
        )
        perm_rim[a] = selection(
            128, 128, lambda r: shifted_z(r, a - 1, lambda r, z: (z >> 2) * 32 + (r >> 4) * 4 + (z & 3))
        )
        lift_z[a] = selection(128, 128, lambda r: shifted_z(r, a - 1, lambda r, z: r - (r & 15) + z))
    perm_brick[...] = selection(256, 256, lambda r: ((r & 63) >> 2) * 16 + (r >> 6) * 4 + (r & 3))

    def put_y(side, y):
        face = take_y[side].astype(F32)
        padded[1:9, y, 8:16, :] = face[0:64].reshape(8, 8, 128)
        for i, z in enumerate((0, 9)):
            flat[pl.ds(at_row(1, y, z), 8, stride=240), :] = face[64 + 8 * i : 72 + 8 * i]

    finish_y(lambda: put_y(0, 0), lambda: put_y(1, 9))

    for side, x in ((0, 1), (1, 8)):
        ends = [padded[x, y, 8:16, :] for y in (0, 9)]
        face_x[side, 0:16] = jnp.concatenate(ends, axis=0).astype(BF)
        for i, z in enumerate((0, 9)):
            first = flat[pl.ds(at_row(x, 0, z), 8, stride=24), :]
            rest = flat[pl.ds(at_row(x, 2, z), 8, stride=24), :]
            face_x[side, 16 + 16 * i : 32 + 16 * i] = jnp.concatenate([first, rest], axis=0).astype(BF)
    finish_x = exchange("gx", gx, 8, face_x.at[0], take_x.at[1], face_x.at[1], take_x.at[0])

    loads[3].wait()
    pre[...] = jnp.zeros_like(pre)

    @pl.loop(0, 9, unroll=3)
    def _(step):
        b, c = step // 3, step % 3
        windows = [
            padded[pl.ds(b, 8), pl.ds(c, 8), 7 + a : 15 + a, :].reshape(512, 128).astype(BF) for a in range(3)
        ]
        for a in range(3):
            columns[a * 9 + step] = windows[a]
        weights = jnp.concatenate([wc[a * 9 + step] for a in range(3)], axis=0)
        pre[...] += matmul(jnp.concatenate(windows, axis=1), weights)

    def put_main(side, x):
        padded[x, 1:9, 8:16, :] = take_main[side].astype(F32).reshape(8, 8, 128)

    def put_x(side, x):
        face = take_x[side].astype(F32)
        padded[x, 0, 8:16, :] = face[0:8]
        padded[x, 9, 8:16, :] = face[8:16]
        for i, z in enumerate((0, 9)):
            flat[pl.ds(at_row(x, 0, z), 8, stride=24), :] = face[16 + 16 * i : 24 + 16 * i]
            flat[pl.ds(at_row(x, 2, z), 8, stride=24), :] = face[24 + 16 * i : 32 + 16 * i]

    finish_main(lambda: put_main(0, 0), lambda: put_main(1, 9))
    finish_x(lambda: put_x(0, 0), lambda: put_x(1, 9))

    for c in range(3):
        for x, first, b in ((0, 0, 0), (9, 448, 2)):
            windows = [padded[x, c : c + 8, 7 + a : 15 + a, :].reshape(64, 128).astype(BF) for a in range(3)]
            for a in range(3):
                columns[a * 9 + 3 * b + c, first : first + 64] = windows[a]
            weights = jnp.concatenate([wc[a * 9 + 3 * b + c] for a in range(3)], axis=0)
            pre[first : first + 64] += matmul(jnp.concatenate(windows, axis=1), weights)

    high = pre[...].astype(BF)
    low = (pre[...] - high.astype(F32)).astype(BF)
    pre_sub = matmul(perm_sub[...], high) + matmul(perm_sub[...], low)
    hidden_sub[...] = jax.nn.silu(pre_sub).astype(BF)
    slope_sub[...] = slope_of(pre_sub)

    loads[4].wait()
    coarse = jnp.zeros((64, 512), F32)
    for s in range(8):
        coarse = coarse + matmul(hidden_sub[pl.ds(64 * s, 64)], wd[s])
    bricks[gz] = coarse.astype(BF)

    finish_cx = exchange(
        "gx", gx, 8,
        bricks.at[gz, pl.ds(0, 16)], rims.at[gz, pl.ds(16, 16)],
        bricks.at[gz, pl.ds(48, 16)], rims.at[gz, pl.ds(0, 16)],
    )

    def send_column(ref):
        copies = []
        for d in (1, 2, 3):
            copy = remote(ref.at[gz], ref.at[gz], {"gz": around(gz, d, 4)})
            copy.start()
            copies.append(copy)
        return copies

    brick_copies = send_column(bricks)

    def turn(first, last):
        @pl.loop(first, last)
        def _(tap):
            turned[tap] = columns[tap].T

    turn(0, 16)
    finish_cx(lambda: None, lambda: None)
    rim_copies = send_column(rims)
    turn(16, 27)

    for copy in brick_copies:
        copy.wait()
    stack = bricks[...].reshape(256, 512)
    middle = matmul(perm_group[1], stack).astype(BF).reshape(4, 4, 16, 512)
    for side, y in ((0, 0), (1, 3)):
        rim_out[side] = middle[:, y].reshape(64, 512)
    finish_cy = exchange("gy", gy, 8, rim_out.at[0], rim_in.at[1], rim_out.at[1], rim_in.at[0])
    shifted[1, 1:5, 1:5] = middle
    for a in (0, 2):
        shifted[a, 1:5, 1:5] = matmul(perm_group[a], stack).astype(BF).reshape(4, 4, 16, 512)
    for copy in back_copies:
        copy.wait()
    back_column = matmul(perm_group[1], back_in[...].reshape(256, 128))

    loads[5].wait()
    finish_cy(lambda: None, lambda: None)
    for a in range(3):
        sides = matmul(lift_z[a], rim_in[...].reshape(128, 512)).astype(BF).reshape(2, 4, 16, 512)
        shifted[a, 1:5, 0] = sides[0]
        shifted[a, 1:5, 5] = sides[1]

    pre_low[...] = jnp.zeros_like(pre_low)

    def low_taps(first, last):
        @pl.loop(first, last, unroll=3)
        def _(step):
            b, c = step // 3, step % 3
            total = pre_low[...]
            for a in range(3):
                window = shifted[a, pl.ds(b, 4), pl.ds(c, 4)].reshape(256, 512)
                total = total + matmul(window, wb[a * 9 + step])
            pre_low[...] = total

    low_taps(0, 6)
    for copy in rim_copies:
        copy.wait()
    rim_rows = []
    for a in range(3):
        rim_rows.append(matmul(perm_rim[a], rims[...].reshape(128, 512)).astype(BF).reshape(2, 4, 16, 512))
    for side, y in ((0, 0), (1, 3)):
        corner_out[side] = rim_rows[1][:, y].reshape(32, 512)
    finish_cc = exchange("gy", gy, 8, corner_out.at[0], corner_in.at[1], corner_out.at[1], corner_in.at[0])
    low_taps(6, 9)
    for a in range(3):
        shifted[a, 0, 1:5] = rim_rows[a][0]
        shifted[a, 5, 1:5] = rim_rows[a][1]
    finish_cc(lambda: None, lambda: None)
    for a in range(3):
        corners = matmul(lift_z[a], corner_in[...].reshape(128, 512)).astype(BF).reshape(4, 2, 16, 512)
        for i, y in ((0, 0), (1, 5)):
            shifted[a, 0, y] = corners[i, 0]
            shifted[a, 5, y] = corners[i, 1]

    @pl.loop(0, 3)
    def _(c):
        low, high = pre_low[0:64], pre_low[192:256]
        for a in range(3):
            low = low + matmul(shifted[a, 0, pl.ds(c, 4)].reshape(64, 512), wb[a * 9 + c])
            high = high + matmul(shifted[a, 5, pl.ds(c, 4)].reshape(64, 512), wb[a * 9 + 6 + c])
        pre_low[0:64] = low
        pre_low[192:256] = high

    bottle_grad = (back_column * slope_of(pre_low[...])).astype(BF)
    grad_now[...] = bottle_grad
    middle = bottle_grad.astype(F32).reshape(4, 4, 16, 128)
    for side, y in ((0, 0), (1, 3)):
        gface_y[side] = middle[:, y].reshape(64, 128).astype(BF)
    finish_gy = exchange("gy", gy, 8, gface_y.at[0], gtake_y.at[1], gface_y.at[1], gtake_y.at[0])

    bottle = jax.nn.silu(pre_low[...]).astype(BF)
    bottle_out[...] = matmul(perm_brick[...], bottle).astype(BF).reshape(4, 64, 128)
    bottle_copies = []
    for d in (1, 2, 3):
        peer = around(gz, d, 4)
        copy = remote(bottle_out.at[peer], bottle_in.at[gz], {"gz": peer})
        copy.start()
        bottle_copies.append(copy)
    bottle_in[gz] = bottle_out[gz]

    for a in range(3):
        for half in range(2):
            moved = matmul(lift_z[a], grad_now[pl.ds(128 * half, 128)]).astype(BF)
            grad_shift[a, 1 + 2 * half : 3 + 2 * half, 1:5] = moved.reshape(2, 4, 16, 128)

    mine, other = core * 14, (1 - core) * 14

    def bottle_taps(first, last, base):
        @pl.loop(first, last)
        def _(step):
            tap = base + step
            depth, across = tap // 9, tap % 9
            b, c = across // 3, across % 3
            window = shifted[depth, pl.ds(b, 4), pl.ds(c, 4)].reshape(256, 512)
            gb_all[tap] = matmul_tn(window, grad_now[...]).astype(BF).reshape(4, 2, 4, 16, 128)

    bottle_taps(0, 8, other)
    finish_gy(lambda: None, lambda: None)
    for a in range(3):
        sides = matmul(lift_z[a], gtake_y[...].reshape(128, 128)).astype(BF).reshape(2, 4, 16, 128)
        grad_shift[a, 1:5, 0] = sides[0]
        grad_shift[a, 1:5, 5] = sides[1]
    for side, x in ((0, 1), (1, 4)):
        gface_x[side] = grad_shift[1, x].reshape(96, 128)
    finish_gx = exchange(
        "gx", gx, 8,
        gface_x.at[0], gtake_x.at[1, pl.ds(0, 96)], gface_x.at[1], gtake_x.at[0, pl.ds(0, 96)],
    )

    part_acc[...] = jnp.zeros_like(part_acc)

    @pl.loop(0, 9, unroll=3)
    def _(step):
        b, c = step // 3, step % 3
        windows = [grad_shift[2 - a, pl.ds(2 - b, 4), pl.ds(2 - c, 4)].reshape(256, 128) for a in range(3)]
        weights = jnp.concatenate([wb[a * 9 + step] for a in range(3)], axis=1)
        part_acc[...] += matmul_nt(jnp.concatenate(windows, axis=1), weights)

    part_copies = []

    def send_parts(which, rows):
        part_out[which] = matmul(perm_part[...], rows.astype(BF)).astype(BF).reshape(4, 32, 512)
        for d in (1, 2, 3):
            peer = around(gz, d, 4)
            copy = remote(part_out.at[which, peer], part_in.at[which, d - 1], {"gz": peer})
            copy.start()
            part_copies.append(copy)

    send_parts(0, part_acc[64:192])
    finish_gx(lambda: None, lambda: None)
    for a in range(3):
        for side, x in ((0, 0), (1, 5)):
            moved = matmul(lift_z[a], gtake_x[side]).astype(BF)
            grad_shift[a, x] = moved[0:96].reshape(6, 16, 128)

    @pl.loop(0, 3)
    def _(c):
        for x, rows, b in ((0, 0, 2), (5, 192, 0)):
            windows = [grad_shift[2 - a, x, pl.ds(2 - c, 4)].reshape(64, 128) for a in range(3)]
            weights = jnp.concatenate([wb[a * 9 + 3 * b + c] for a in range(3)], axis=1)
            part_acc[rows : rows + 64] += matmul_nt(jnp.concatenate(windows, axis=1), weights)

    send_parts(1, jnp.concatenate([part_acc[0:64], part_acc[192:256]], axis=0))

    bottle_taps(8, 13 + core, other)
    gb_first = remote(gb_all.at[pl.ds(other, 14)], gb_one, {"gy": gy ^ 1})
    gb_first.start()
    bottle_taps(0, 14 - core, mine)

    gb_first.wait()

    @pl.loop(0, 14)
    def _(step):
        total = gb_all[mine + step].astype(F32) + gb_one[step].astype(F32)
        gb_all[mine + step] = total.astype(BF)

    def along_y(source_of, target):
        copies = []
        for d in (1, 2, 3):
            copy = remote(source_of(around(py, d, 4)), target.at[d - 1], {"gx": around(gx, 2 * d, 8)})
            copy.start()
            copies.append(copy)
        return copies

    def along_x(source_of, target):
        copies = []
        for d in (1, 2, 3):
            copy = remote(source_of(around(px, d, 4)), target.at[d - 1], {"gy": around(gy, 2 * d, 8)})
            copy.start()
            copies.append(copy)
        return copies

    def y_place(y):
        return {"gx": 2 * y + zh}

    def x_place(x):
        return {"gy": 2 * x + core}

    def begin_halving(position, place, mirrored, chunk, inbox):
        near, far = position ^ 1, 3 - position
        first, second = (far, near) if mirrored else (near, far)
        beyond = first ^ 1 if mirrored else 3 - first
        copies = [
            remote(chunk(first), inbox.at[0], place(first)), remote(chunk(beyond), inbox.at[1], place(first))
        ]
        for copy in copies:
            copy.start()

        def next_step():
            copies[1].wait()
            ref = chunk(second)
            ref[...] = (ref[...].astype(F32) + inbox[1].astype(F32)).astype(BF)
            last = remote(ref, inbox.at[2], place(second))
            last.start()
            copies[0].wait()

            def finish():
                own = chunk(position)
                total = own[...].astype(F32) + inbox[0].astype(F32)
                last.wait()
                return total + inbox[2].astype(F32)

            return finish

        return next_step

    parts = ((0, 4), (4, 3))
    inbox_a, inbox_b = (gb_ya, gb_ya2), (gb_xb, gb_xb2)
    inbox_c, inbox_d = (gb_xa, gb_xa2), (gb_yb, gb_yb2)
    gb_steps = []
    for i, (t, n) in enumerate(parts):
        gb_steps.append(begin_halving(
            py, y_place, i == 1, lambda y, t=t, n=n: gb_all.at[pl.ds(mine + t, n), y], inbox_a[i]
        ))
        gb_steps.append(begin_halving(
            px, x_place, i == 1, lambda x, t=t, n=n: gb_all.at[pl.ds(mine + 7 + t, n), :, :, x], inbox_b[i]
        ))

    for copy in part_copies:
        copy.wait()
    sums = []
    for which in range(2):
        total = part_out[which, gz].astype(F32)
        for d in range(3):
            total = total + part_in[which, d].astype(F32)
        sums.append(total)
    inner, outer = sums
    coarse_grad = jnp.concatenate([outer[0:16], inner, outer[16:32]], axis=0).astype(BF)
    for s in range(8):
        rows = pl.ds(64 * s, 64)
        spread = matmul_nt(coarse_grad, wd[s]) + cot_sub[rows].astype(F32)
        fine_grad[rows] = (spread * slope_sub[rows]).astype(BF)
    fine_grad[...] = matmul(perm_back[...], fine_grad[...]).astype(BF)

    def fine_taps(base):
        for step in range(4):
            lines = turned[pl.ds(base + 4 * step, 4)].reshape(512, 512)
            term = matmul(lines, fine_grad[...])
            gc_all[pl.ds(base + 4 * step, 4)] = term.astype(BF).reshape(4, 4, 32, 128)

    keep, give = core * 16, (1 - core) * 16
    fine_taps(give)
    gc_first = remote(gc_all.at[pl.ds(give, 16)], gc_one, {"gy": gy ^ 1})
    gc_first.start()
    fine_taps(keep)

    gc_first.wait()

    @pl.loop(0, 16)
    def _(step):
        total = gc_all[keep + step].astype(F32) + gc_one[step].astype(F32)
        gc_all[keep + step] = total.astype(BF)

    gc_second = along_x(lambda x: gc_all.at[pl.ds(keep + 2 * x, 2)], gc_xa)
    gc_second += along_y(lambda y: gc_all.at[pl.ds(keep + 8, 8), y], gc_yb)

    gb_ends = [step() for step in gb_steps]

    def summed(own, taken):
        total = own.astype(F32)
        for d in range(3):
            total = total + taken[d].astype(F32)
        return total

    for copy in gc_second:
        copy.wait()
    gc_a[...] = summed(gc_all[pl.ds(keep + 2 * px, 2)], gc_xa).astype(BF)
    gc_b[...] = summed(gc_all[pl.ds(keep + 8, 8), py], gc_yb).astype(BF)
    gc_third = along_y(lambda y: gc_a.at[:, y], gc_ya)
    gc_third += along_x(lambda x: gc_b.at[pl.ds(2 * x, 2)], gc_xb)

    gb_steps = []
    for i, (t, n) in enumerate(parts):
        gb_a[t : t + n] = gb_ends[2 * i]().astype(BF)
        gb_steps.append(begin_halving(
            px, x_place, i == 1, lambda x, t=t, n=n: gb_a.at[pl.ds(t, n), :, x], inbox_c[i]
        ))
        gb_b[t : t + n] = gb_ends[2 * i + 1]().astype(BF)
        gb_steps.append(begin_halving(
            py, y_place, i == 1, lambda y, t=t, n=n: gb_b.at[pl.ds(t, n), y], inbox_d[i]
        ))

    for copy in gc_third:
        copy.wait()
    gc_e2[0:2] = summed(gc_a[:, py], gc_ya).astype(BF).reshape(2, 2, 16, 128)
    gc_e2[2:4] = summed(gc_b[pl.ds(2 * px, 2)], gc_xb).astype(BF).reshape(2, 2, 16, 128)
    slot = zh * 4 + gz
    gc_fourth = []
    for d in range(4):
        peer = around(gz, d, 4)
        copy = remote(gc_e2.at[:, 1 - zh], gc_z.at[slot], {"gx": gx ^ 1, "gz": peer})
        copy.start()
        gc_fourth.append(copy)
        if d > 0:
            copy = remote(gc_e2.at[:, zh], gc_z.at[slot], {"gz": peer})
            copy.start()
            gc_fourth.append(copy)
    gc_z[slot] = gc_e2[:, zh]

    gb_last = [step() for step in gb_steps]
    for i, (t, n) in enumerate(parts):
        gb_d4[t : t + n] = gb_last[2 * i]().astype(BF)
        gb_d4[7 + t : 7 + t + n] = gb_last[2 * i + 1]().astype(BF)
    gb_fourth = remote(gb_d4.at[:, 1 - zh], gb_four, {"gx": gx ^ 1})
    gb_fourth.start()

    for copy in bottle_copies:
        copy.wait()
    for s in range(8):
        lifted = jnp.zeros((64, 128), F32)
        for q in range(4):
            lifted = lifted + matmul(bottle_in[q], wu[s, pl.ds(128 * q, 128)])
        total = lifted + hidden_sub[pl.ds(64 * s, 64)].astype(F32)
        fine_grad[pl.ds(64 * s, 64)] = total.astype(BF)
    out_ref[...] = matmul(perm_out[...], fine_grad[...]).astype(BF)

    for copy in gc_fourth:
        copy.wait()
    total = gc_z[0].astype(F32)
    for q in range(1, 8):
        total = total + gc_z[q].astype(F32)
    for half in range(2):
        gc_half[half] = total[:, 8 * half : 8 * half + 8]
    gathers = []
    for d in range(1, 8):
        peer = around(gy, d, 8)
        copy = remote(gc_half.at[peer >> 2], gc_g.at[gy], {"gy": peer})
        copy.start()
        gathers.append(copy)
    gc_g[gy] = gc_half[gy >> 2]

    gb_fourth.wait()
    gb_d5[...] = (gb_d4[:, zh].astype(F32) + gb_four[...].astype(F32)).reshape(14, 2, 8, 128)
    gb_fifth = remote(gb_d5.at[:, 1 - core], gb_five, {"gy": gy ^ 1})
    gb_fifth.start()

    gb_fifth.wait()
    gb_ref[pl.ds(mine, 14)] = gb_d5[:, core]
    gb_ref[pl.ds(other, 14)] = gb_five[...]

    for copy in gathers:
        copy.wait()
    place = gy & 3
    for source in range(8):
        block = gc_g[source]
        chosen = jnp.zeros((4, 2, 128), F32)
        for j in range(4):
            chosen = chosen + jnp.where(place == j, block[:, 2 * j : 2 * j + 2, :], 0.0)
        first = (source & 1) * 16 + (source >> 1) * 2
        gc_ref[first : first + 2] = chosen[0:2]
        gc_ref[first + 8 : first + 10] = chosen[2:4]


def deliver_kernel(out_ref, gb_ref, gc_ref, out_final, gb_final, gc_final):
    out_final[...] = out_ref[...]
    gb_final[...] = gb_ref[0:TAPS]
    gc_final[...] = gc_ref[0:TAPS]


def body(volume, cotangent, w_conv, w_down, w_bottle, w_up):
    vmem = pltpu.VMEM
    whole = pl.BlockSpec(memory_space=pl.ANY)
    held = pl.BlockSpec(memory_space=pltpu.VMEM)
    def kept(*shape):
        return vmem(shape, BF)

    scratch = [
        kept(512, 128), kept(512, 128), kept(27, 128, 128), kept(8, 128, 512),
        kept(27, 512, 128), kept(8, 512, 128), pltpu.SemaphoreType.DMA((6,)),
        kept(512, 512), kept(512, 512), kept(512, 512), kept(512, 512), kept(512, 512),
        kept(3, 256, 256), kept(3, 128, 128), kept(256, 256), kept(128, 128), kept(3, 128, 128),
        kept(2, 64, 128), kept(2, 64, 128), kept(2, 64, 128), kept(2, 80, 128), kept(2, 80, 128),
        kept(2, 48, 128), kept(2, 48, 128),
        vmem((10, 10, 24, 128), F32), kept(27, 512, 128), kept(32, 128, 512), vmem((512, 128), F32),
        kept(512, 128), vmem((512, 128), F32), kept(512, 128),
        kept(4, 64, 128), kept(4, 64, 128), kept(4, 64, 512), kept(4, 32, 512), kept(3, 6, 6, 16, 512),
        kept(2, 64, 512), kept(2, 64, 512), kept(2, 32, 512), kept(4, 32, 512), vmem((256, 128), F32),
        kept(256, 128), kept(3, 6, 6, 16, 128), kept(2, 64, 128), kept(2, 64, 128),
        kept(2, 96, 128), kept(2, 128, 128),
        kept(4, 64, 128), kept(4, 64, 128), vmem((256, 512), F32), kept(2, 4, 32, 512),
        kept(2, 3, 32, 512), kept(512, 128),
        kept(28, 4, 2, 4, 16, 128), kept(14, 4, 2, 4, 16, 128),
        kept(3, 4, 2, 4, 16, 128), kept(3, 3, 2, 4, 16, 128), kept(3, 4, 4, 2, 16, 128), kept(3, 3, 4, 2, 16, 128),
        kept(7, 2, 4, 16, 128), kept(7, 4, 2, 16, 128),
        kept(3, 4, 2, 16, 128), kept(3, 3, 2, 16, 128), kept(3, 4, 2, 16, 128), kept(3, 3, 2, 16, 128),
        kept(14, 2, 16, 128), kept(14, 16, 128), vmem((14, 2, 8, 128), F32), vmem((14, 8, 128), F32),
        kept(32, 4, 32, 128), kept(16, 4, 32, 128), kept(3, 2, 4, 32, 128), kept(3, 8, 32, 128),
        kept(2, 4, 32, 128), kept(8, 32, 128), kept(3, 2, 32, 128), kept(3, 2, 32, 128),
        kept(4, 2, 16, 128), kept(8, 4, 16, 128), vmem((2, 4, 8, 128), F32), vmem((8, 4, 8, 128), F32),
        pltpu.SemaphoreType.DMA((COPIES,)), pltpu.SemaphoreType.DMA((COPIES,)),
    ]
    out, gb, gc = pl.pallas_call(
        level_kernel,
        out_shape=(
            jax.ShapeDtypeStruct((512, 128), BF),
            jax.ShapeDtypeStruct((28, 8, 128), F32),
            jax.ShapeDtypeStruct((32, 2, 128), F32),
        ),
        in_specs=[whole] * 6,
        out_specs=(held,) * 3,
        scratch_shapes=scratch,
        compiler_params=pltpu.CompilerParams(
            collective_id=0, has_side_effects=True, vmem_limit_bytes=60 * 1024 * 1024
        ),
        name="level",
    )(
        volume.reshape(512, 128),
        cotangent.reshape(512, 128),
        jnp.transpose(w_conv, (1, 0, 2)),
        w_down,
        jnp.transpose(w_bottle, (1, 0, 2)),
        w_up,
    )
    out, gb, gc = pl.pallas_call(
        deliver_kernel,
        out_shape=(
            jax.ShapeDtypeStruct(out.shape, BF),
            jax.ShapeDtypeStruct((TAPS, 8, 128), F32),
            jax.ShapeDtypeStruct((TAPS, 2, 128), F32),
        ),
        in_specs=[held] * 3,
        out_specs=(held,) * 3,
        name="deliver",
    )(out, gb, gc)
    return out.reshape(volume.shape), jnp.transpose(gc, (1, 0, 2)), jnp.transpose(gb, (1, 0, 2))


def solution(mesh):
    in_specs = (
        P("gz", "gx", "gy", None),
        P("gz", "gx", "gy", None),
        P(),
        P(),
        P(None, None, "gz"),
        P(),
    )
    out_specs = (
        P("gz", "gx", "gy", None),
        P(("gx", "gy"), None, None),
        P(("gx", "gy"), None, "gz"),
    )
    return jax.shard_map(body, mesh=mesh, in_specs=in_specs, out_specs=out_specs, check_vma=False)
```

```python
import jax
import jax.numpy as jnp
from jax import lax
from jax.experimental import pallas as pl
from jax.experimental.pallas import tpu as pltpu
from jax.sharding import PartitionSpec as P

BF = jnp.bfloat16
F32 = jnp.float32
MESH = pl.DeviceIdType.MESH
TAPS = 27
COPIES = 112


def matmul(left, right):
    return jnp.dot(left, right, preferred_element_type=F32)


def matmul_nt(left, right):
    return lax.dot_general(left, right, (((1,), (1,)), ((), ())), preferred_element_type=F32)


def matmul_tn(left, right):
    return lax.dot_general(left, right, (((0,), (0,)), ((), ())), preferred_element_type=F32)


def slope_of(values):
    sig = jax.nn.sigmoid(values)
    return sig * (1.0 + values * (1.0 - sig))


def selection(rows, columns, column_of):
    row = lax.broadcasted_iota(jnp.int32, (rows, 128), 0)
    lane = lax.broadcasted_iota(jnp.int32, (rows, 128), 1)
    target = column_of(row)
    blocks = [
        jnp.where(target == lane + 128 * block, 1.0, 0.0).astype(BF) for block in range(columns // 128)
    ]
    return jnp.concatenate(blocks, axis=1)


def cell_of_sub(row):
    s, k = row >> 6, row & 63
    x = 2 * (k >> 4) + ((s >> 1) & 1)
    y = 2 * ((k >> 2) & 3) + (s & 1)
    z = 2 * (k & 3) + (s >> 2)
    return x, y, z


def sub_of_cell(x, y, z):
    s = (z & 1) * 4 + (x & 1) * 2 + (y & 1)
    k = ((x >> 1) * 4 + (y >> 1)) * 4 + (z >> 1)
    return s * 64 + k


def level_kernel(
    vol_hbm, cot_hbm, wc_hbm, wd_hbm, wb_hbm, wu_hbm,
    out_ref, gb_ref, gc_ref,
    vol, cot, wc, wd, wb, wu, load_sem,
    perm_xyz, perm_sub, perm_cot, perm_back, perm_out, perm_group, perm_rim, perm_brick, lift_z,
    plane_z, face_main, take_main, face_y, take_y, face_x, take_x,
    padded, columns, turned, pre, cot_sub, slope_sub, hidden_sub,
    back_out, back_in, bricks, rims, shifted, rim_out, rim_in, corner_out, corner_in, pre_low,
    grad_now, grad_shift, gface_y, gtake_y, gface_x, gtake_x,
    bottle_out, bottle_in, part_acc, part_out, part_in, fine_grad,
    gb_all, gb_one, gb_ya, gb_ya2, gb_xb, gb_xb2, gb_a, gb_b, gb_xa, gb_xa2, gb_yb, gb_yb2, gb_d4, gb_four, gb_d5, gb_five,
    gc_all, gc_one, gc_xa, gc_yb, gc_a, gc_b, gc_ya, gc_xb, gc_e2, gc_z, gc_half, gc_g,
    send_sem, recv_sem,
):
    gx, gy, gz = lax.axis_index("gx"), lax.axis_index("gy"), lax.axis_index("gz")
    py, zh = gx >> 1, gx & 1
    px, core = gy >> 1, gy & 1
    used = [0]

    def remote(src, dst, device):
        slot = used[0]
        used[0] += 1
        return pltpu.make_async_remote_copy(
            src_ref=src, dst_ref=dst, send_sem=send_sem.at[slot], recv_sem=recv_sem.at[slot],
            device_id=device, device_id_type=MESH,
        )

    def around(position, step, count):
        return lax.rem(position + step, count)

    barrier = pltpu.get_barrier_semaphore()
    partners = [{"gx": around(gx, d, 8)} for d in (1, 2, 4, 6, 7)]
    partners += [{"gy": around(gy, d, 8)} for d in range(1, 8)]
    partners += [{"gz": around(gz, d, 4)} for d in (1, 2, 3)]
    partners += [{"gx": gx ^ 1, "gz": around(gz, d, 4)} for d in (1, 2, 3)]
    for partner in partners:
        pl.semaphore_signal(barrier, inc=1, device_id=partner, device_id_type=MESH)

    loads = [
        pltpu.make_async_copy(src, dst, load_sem.at[i])
        for i, (src, dst) in enumerate(
            ((vol_hbm, vol), (cot_hbm, cot), (wu_hbm, wu), (wc_hbm, wc), (wd_hbm, wd), (wb_hbm, wb))
        )
    ]
    for load in loads:
        load.start()

    def sub_to_xyz(row):
        x, y, z = cell_of_sub(row)
        return (x * 8 + y) * 8 + z

    def sub_to_zxy(row):
        x, y, z = cell_of_sub(row)
        return (z * 8 + x) * 8 + y

    perm_xyz[...] = selection(512, 512, lambda r: ((r & 7) * 8 + (r >> 6)) * 8 + ((r >> 3) & 7))

    loads[0].wait()
    main = matmul(perm_xyz[...], vol[...])
    face_main[0] = main[0:64].astype(BF)
    face_main[1] = main[448:512].astype(BF)
    pl.semaphore_wait(barrier, len(partners))

    def exchange(axis, position, count, low_src, high_dst, high_src, low_dst):
        down = remote(low_src, high_dst, {axis: around(position, count - 1, count)})
        up = remote(high_src, low_dst, {axis: around(position, 1, count)})

        @pl.when(position > 0)
        def _():
            down.start()

        @pl.when(position < count - 1)
        def _():
            up.start()

        def finish(on_low, on_high):
            @pl.when(position > 0)
            def _():
                down.wait_send()
                up.wait_recv()
                on_low()

            @pl.when(position < count - 1)
            def _():
                up.wait_send()
                down.wait_recv()
                on_high()

        return finish

    finish_z = exchange(
        "gz", gz, 4, vol.at[pl.ds(0, 64)], plane_z.at[1], vol.at[pl.ds(448, 64)], plane_z.at[0]
    )

    finish_main = exchange(
        "gx", gx, 8, face_main.at[0], take_main.at[1], face_main.at[1], take_main.at[0]
    )

    padded[...] = jnp.zeros_like(padded)
    for side in (0, 5):
        for a in range(3):
            shifted[a, side] = jnp.zeros((6, 16, 512), BF)
            grad_shift[a, side] = jnp.zeros((6, 16, 128), BF)
    for tap in range(TAPS, 32):
        turned[tap] = jnp.zeros((128, 512), BF)
    gb_all[27] = jnp.zeros((4, 2, 4, 16, 128), BF)
    corner_in[2:4] = jnp.zeros((2, 32, 512), BF)
    for side in range(2):
        gtake_x[side, 96:128] = jnp.zeros((32, 128), BF)

    for side, edge in ((0, 0), (1, 7)):
        @pl.when(gx == edge)
        def _():
            rims[gz, 16 * side : 16 * side + 16] = jnp.zeros((16, 512), BF)
            gtake_x[side, 0:96] = jnp.zeros((96, 128), BF)

        @pl.when(gy == edge)
        def _():
            rim_in[side] = jnp.zeros((64, 512), BF)
            corner_in[side] = jnp.zeros((32, 512), BF)
            gtake_y[side] = jnp.zeros((64, 128), BF)
    padded[1:9, 1:9, 8:16, :] = main.reshape(8, 8, 8, 128)
    perm_cot[...] = selection(512, 512, sub_to_zxy)

    loads[1].wait()
    cot_sub[...] = matmul(perm_cot[...], cot[...]).astype(BF)
    loads[2].wait()
    back = jnp.zeros((64, 512), F32)
    for s in range(8):
        back = back + matmul_nt(cot_sub[pl.ds(64 * s, 64)], wu[s])
    for q in range(4):
        back_out[q] = back[:, 128 * q : 128 * (q + 1)].astype(BF)
    back_copies = []
    for d in (1, 2, 3):
        peer = around(gz, d, 4)
        copy = remote(back_out.at[peer], back_in.at[gz], {"gz": peer})
        copy.start()
        back_copies.append(copy)
    back_in[gz] = back_out[gz]

    flat = padded.reshape(2400, 128)

    def at_row(x, y, z):
        return (x * 10 + y) * 24 + 7 + z

    def put_plane(side, z):
        plane = plane_z[side].astype(F32)
        for x in range(8):
            flat[pl.ds(at_row(x + 1, 1, z), 8, stride=24), :] = plane[8 * x : 8 * x + 8]

    finish_z(lambda: put_plane(0, 0), lambda: put_plane(1, 9))

    for side, y in ((0, 1), (1, 8)):
        face_y[side, 0:64] = padded[1:9, y, 8:16, :].reshape(64, 128).astype(BF)
        edges = [flat[pl.ds(at_row(1, y, z), 8, stride=240), :] for z in (0, 9)]
        face_y[side, 64:80] = jnp.concatenate(edges, axis=0).astype(BF)
    finish_y = exchange("gy", gy, 8, face_y.at[0], take_y.at[1], face_y.at[1], take_y.at[0])

    perm_sub[...] = selection(512, 512, sub_to_xyz)
    perm_back[...] = selection(512, 512, lambda r: sub_of_cell(r >> 6, (r >> 3) & 7, r & 7))
    perm_out[...] = selection(512, 512, lambda r: sub_of_cell((r >> 3) & 7, r & 7, r >> 6))

    def shifted_z(r, shift, column_of):
        z = (r & 15) + shift
        return jnp.where((z < 0) | (z > 15), -1, column_of(r, z & 15))

    for a in range(3):
        perm_group[a] = selection(
            256, 256, lambda r: shifted_z(r, a - 1, lambda r, z: (z >> 2) * 64 + (r >> 4) * 4 + (z & 3))
        )
        perm_rim[a] = selection(
            128, 128, lambda r: shifted_z(r, a - 1, lambda r, z: (z >> 2) * 32 + (r >> 4) * 4 + (z & 3))
        )
        lift_z[a] = selection(128, 128, lambda r: shifted_z(r, a - 1, lambda r, z: r - (r & 15) + z))
    perm_brick[...] = selection(256, 256, lambda r: ((r & 63) >> 2) * 16 + (r >> 6) * 4 + (r & 3))

    def put_y(side, y):
        face = take_y[side].astype(F32)
        padded[1:9, y, 8:16, :] = face[0:64].reshape(8, 8, 128)
        for i, z in enumerate((0, 9)):
            flat[pl.ds(at_row(1, y, z), 8, stride=240), :] = face[64 + 8 * i : 72 + 8 * i]

    finish_y(lambda: put_y(0, 0), lambda: put_y(1, 9))

    for side, x in ((0, 1), (1, 8)):
        ends = [padded[x, y, 8:16, :] for y in (0, 9)]
        face_x[side, 0:16] = jnp.concatenate(ends, axis=0).astype(BF)
        for i, z in enumerate((0, 9)):
            first = flat[pl.ds(at_row(x, 0, z), 8, stride=24), :]
            rest = flat[pl.ds(at_row(x, 2, z), 8, stride=24), :]
            face_x[side, 16 + 16 * i : 32 + 16 * i] = jnp.concatenate([first, rest], axis=0).astype(BF)
    finish_x = exchange("gx", gx, 8, face_x.at[0], take_x.at[1], face_x.at[1], take_x.at[0])

    loads[3].wait()
    pre[...] = jnp.zeros_like(pre)

    @pl.loop(0, 9, unroll=3)
    def _(step):
        b, c = step // 3, step % 3
        windows = [
            padded[pl.ds(b, 8), pl.ds(c, 8), 7 + a : 15 + a, :].reshape(512, 128).astype(BF) for a in range(3)
        ]
        for a in range(3):
            columns[a * 9 + step] = windows[a]
        weights = jnp.concatenate([wc[a * 9 + step] for a in range(3)], axis=0)
        pre[...] += matmul(jnp.concatenate(windows, axis=1), weights)

    def put_main(side, x):
        padded[x, 1:9, 8:16, :] = take_main[side].astype(F32).reshape(8, 8, 128)

    def put_x(side, x):
        face = take_x[side].astype(F32)
        padded[x, 0, 8:16, :] = face[0:8]
        padded[x, 9, 8:16, :] = face[8:16]
        for i, z in enumerate((0, 9)):
            flat[pl.ds(at_row(x, 0, z), 8, stride=24), :] = face[16 + 16 * i : 24 + 16 * i]
            flat[pl.ds(at_row(x, 2, z), 8, stride=24), :] = face[24 + 16 * i : 32 + 16 * i]

    finish_main(lambda: put_main(0, 0), lambda: put_main(1, 9))
    finish_x(lambda: put_x(0, 0), lambda: put_x(1, 9))

    for c in range(3):
        for x, first, b in ((0, 0, 0), (9, 448, 2)):
            windows = [padded[x, c : c + 8, 7 + a : 15 + a, :].reshape(64, 128).astype(BF) for a in range(3)]
            for a in range(3):
                columns[a * 9 + 3 * b + c, first : first + 64] = windows[a]
            weights = jnp.concatenate([wc[a * 9 + 3 * b + c] for a in range(3)], axis=0)
            pre[first : first + 64] += matmul(jnp.concatenate(windows, axis=1), weights)

    high = pre[...].astype(BF)
    low = (pre[...] - high.astype(F32)).astype(BF)
    pre_sub = matmul(perm_sub[...], high) + matmul(perm_sub[...], low)
    hidden_sub[...] = jax.nn.silu(pre_sub).astype(BF)
    slope_sub[...] = slope_of(pre_sub)

    loads[4].wait()
    coarse = jnp.zeros((64, 512), F32)
    for s in range(8):
        coarse = coarse + matmul(hidden_sub[pl.ds(64 * s, 64)], wd[s])
    bricks[gz] = coarse.astype(BF)

    finish_cx = exchange(
        "gx", gx, 8,
        bricks.at[gz, pl.ds(0, 16)], rims.at[gz, pl.ds(16, 16)],
        bricks.at[gz, pl.ds(48, 16)], rims.at[gz, pl.ds(0, 16)],
    )

    def send_column(ref):
        copies = []
        for d in (1, 2, 3):
            copy = remote(ref.at[gz], ref.at[gz], {"gz": around(gz, d, 4)})
            copy.start()
            copies.append(copy)
        return copies

    brick_copies = send_column(bricks)

    def turn(first, last):
        @pl.loop(first, last)
        def _(tap):
            turned[tap] = columns[tap].T

    turn(0, 16)
    finish_cx(lambda: None, lambda: None)
    rim_copies = send_column(rims)
    turn(16, 27)

    for copy in brick_copies:
        copy.wait()
    stack = bricks[...].reshape(256, 512)
    middle = matmul(perm_group[1], stack).astype(BF).reshape(4, 4, 16, 512)
    for side, y in ((0, 0), (1, 3)):
        rim_out[side] = middle[:, y].reshape(64, 512)
    finish_cy = exchange("gy", gy, 8, rim_out.at[0], rim_in.at[1], rim_out.at[1], rim_in.at[0])
    shifted[1, 1:5, 1:5] = middle
    for a in (0, 2):
        shifted[a, 1:5, 1:5] = matmul(perm_group[a], stack).astype(BF).reshape(4, 4, 16, 512)
    for copy in back_copies:
        copy.wait()
    back_column = matmul(perm_group[1], back_in[...].reshape(256, 128))

    loads[5].wait()
    finish_cy(lambda: None, lambda: None)
    for a in range(3):
        sides = matmul(lift_z[a], rim_in[...].reshape(128, 512)).astype(BF).reshape(2, 4, 16, 512)
        shifted[a, 1:5, 0] = sides[0]
        shifted[a, 1:5, 5] = sides[1]

    pre_low[...] = jnp.zeros_like(pre_low)

    def low_taps(first, last):
        @pl.loop(first, last, unroll=3)
        def _(step):
            b, c = step // 3, step % 3
            total = pre_low[...]
            for a in range(3):
                window = shifted[a, pl.ds(b, 4), pl.ds(c, 4)].reshape(256, 512)
                total = total + matmul(window, wb[a * 9 + step])
            pre_low[...] = total

    low_taps(0, 6)
    for copy in rim_copies:
        copy.wait()
    rim_rows = []
    for a in range(3):
        rim_rows.append(matmul(perm_rim[a], rims[...].reshape(128, 512)).astype(BF).reshape(2, 4, 16, 512))
    for side, y in ((0, 0), (1, 3)):
        corner_out[side] = rim_rows[1][:, y].reshape(32, 512)
    finish_cc = exchange("gy", gy, 8, corner_out.at[0], corner_in.at[1], corner_out.at[1], corner_in.at[0])
    low_taps(6, 9)
    for a in range(3):
        shifted[a, 0, 1:5] = rim_rows[a][0]
        shifted[a, 5, 1:5] = rim_rows[a][1]
    finish_cc(lambda: None, lambda: None)
    for a in range(3):
        corners = matmul(lift_z[a], corner_in[...].reshape(128, 512)).astype(BF).reshape(4, 2, 16, 512)
        for i, y in ((0, 0), (1, 5)):
            shifted[a, 0, y] = corners[i, 0]
            shifted[a, 5, y] = corners[i, 1]

    @pl.loop(0, 3)
    def _(c):
        low, high = pre_low[0:64], pre_low[192:256]
        for a in range(3):
            low = low + matmul(shifted[a, 0, pl.ds(c, 4)].reshape(64, 512), wb[a * 9 + c])
            high = high + matmul(shifted[a, 5, pl.ds(c, 4)].reshape(64, 512), wb[a * 9 + 6 + c])
        pre_low[0:64] = low
        pre_low[192:256] = high

    bottle_grad = (back_column * slope_of(pre_low[...])).astype(BF)
    grad_now[...] = bottle_grad
    middle = bottle_grad.astype(F32).reshape(4, 4, 16, 128)
    for side, y in ((0, 0), (1, 3)):
        gface_y[side] = middle[:, y].reshape(64, 128).astype(BF)
    finish_gy = exchange("gy", gy, 8, gface_y.at[0], gtake_y.at[1], gface_y.at[1], gtake_y.at[0])

    bottle = jax.nn.silu(pre_low[...]).astype(BF)
    bottle_out[...] = matmul(perm_brick[...], bottle).astype(BF).reshape(4, 64, 128)
    bottle_copies = []
    for d in (1, 2, 3):
        peer = around(gz, d, 4)
        copy = remote(bottle_out.at[peer], bottle_in.at[gz], {"gz": peer})
        copy.start()
        bottle_copies.append(copy)
    bottle_in[gz] = bottle_out[gz]

    for a in range(3):
        for half in range(2):
            moved = matmul(lift_z[a], grad_now[pl.ds(128 * half, 128)]).astype(BF)
            grad_shift[a, 1 + 2 * half : 3 + 2 * half, 1:5] = moved.reshape(2, 4, 16, 128)

    mine, other = core * 14, (1 - core) * 14

    def bottle_taps(first, last, base):
        @pl.loop(first, last)
        def _(step):
            tap = base + step
            depth, across = tap // 9, tap % 9
            b, c = across // 3, across % 3
            window = shifted[depth, pl.ds(b, 4), pl.ds(c, 4)].reshape(256, 512)
            gb_all[tap] = matmul_tn(window, grad_now[...]).astype(BF).reshape(4, 2, 4, 16, 128)

    bottle_taps(0, 8, other)
    finish_gy(lambda: None, lambda: None)
    for a in range(3):
        sides = matmul(lift_z[a], gtake_y[...].reshape(128, 128)).astype(BF).reshape(2, 4, 16, 128)
        grad_shift[a, 1:5, 0] = sides[0]
        grad_shift[a, 1:5, 5] = sides[1]
    for side, x in ((0, 1), (1, 4)):
        gface_x[side] = grad_shift[1, x].reshape(96, 128)
    finish_gx = exchange(
        "gx", gx, 8,
        gface_x.at[0], gtake_x.at[1, pl.ds(0, 96)], gface_x.at[1], gtake_x.at[0, pl.ds(0, 96)],
    )

    part_acc[...] = jnp.zeros_like(part_acc)

    @pl.loop(0, 9, unroll=3)
    def _(step):
        b, c = step // 3, step % 3
        windows = [grad_shift[2 - a, pl.ds(2 - b, 4), pl.ds(2 - c, 4)].reshape(256, 128) for a in range(3)]
        weights = jnp.concatenate([wb[a * 9 + step] for a in range(3)], axis=1)
        part_acc[...] += matmul_nt(jnp.concatenate(windows, axis=1), weights)

    finish_gx(lambda: None, lambda: None)
    for a in range(3):
        for side, x in ((0, 0), (1, 5)):
            moved = matmul(lift_z[a], gtake_x[side]).astype(BF)
            grad_shift[a, x] = moved[0:96].reshape(6, 16, 128)

    @pl.loop(0, 3)
    def _(c):
        for x, rows, b in ((0, 0, 2), (5, 192, 0)):
            windows = [grad_shift[2 - a, x, pl.ds(2 - c, 4)].reshape(64, 128) for a in range(3)]
            weights = jnp.concatenate([wb[a * 9 + 3 * b + c] for a in range(3)], axis=1)
            part_acc[rows : rows + 64] += matmul_nt(jnp.concatenate(windows, axis=1), weights)

    part_out[...] = matmul(perm_brick[...], part_acc[...].astype(BF)).astype(BF).reshape(4, 64, 512)
    part_copies = []
    for d in (1, 2, 3):
        peer = around(gz, d, 4)
        copy = remote(part_out.at[peer], part_in.at[d - 1], {"gz": peer})
        copy.start()
        part_copies.append(copy)

    bottle_taps(8, 13 + core, other)
    gb_first = remote(gb_all.at[pl.ds(other, 14)], gb_one, {"gy": gy ^ 1})
    gb_first.start()
    bottle_taps(0, 14 - core, mine)

    gb_first.wait()

    @pl.loop(0, 14)
    def _(step):
        total = gb_all[mine + step].astype(F32) + gb_one[step].astype(F32)
        gb_all[mine + step] = total.astype(BF)

    def along_y(source_of, target):
        copies = []
        for d in (1, 2, 3):
            copy = remote(source_of(around(py, d, 4)), target.at[d - 1], {"gx": around(gx, 2 * d, 8)})
            copy.start()
            copies.append(copy)
        return copies

    def along_x(source_of, target):
        copies = []
        for d in (1, 2, 3):
            copy = remote(source_of(around(px, d, 4)), target.at[d - 1], {"gy": around(gy, 2 * d, 8)})
            copy.start()
            copies.append(copy)
        return copies

    def y_place(y):
        return {"gx": 2 * y + zh}

    def x_place(x):
        return {"gy": 2 * x + core}

    def begin_halving(position, place, mirrored, chunk, inbox):
        near, far = position ^ 1, 3 - position
        first, second = (far, near) if mirrored else (near, far)
        beyond = first ^ 1 if mirrored else 3 - first
        copies = [
            remote(chunk(first), inbox.at[0], place(first)), remote(chunk(beyond), inbox.at[1], place(first))
        ]
        for copy in copies:
            copy.start()

        def next_step():
            copies[1].wait()
            ref = chunk(second)
            ref[...] = (ref[...].astype(F32) + inbox[1].astype(F32)).astype(BF)
            last = remote(ref, inbox.at[2], place(second))
            last.start()
            copies[0].wait()

            def finish():
                own = chunk(position)
                total = own[...].astype(F32) + inbox[0].astype(F32)
                last.wait()
                return total + inbox[2].astype(F32)

            return finish

        return next_step

    parts = ((0, 4), (4, 3))
    inbox_a, inbox_b = (gb_ya, gb_ya2), (gb_xb, gb_xb2)
    inbox_c, inbox_d = (gb_xa, gb_xa2), (gb_yb, gb_yb2)
    gb_steps = []
    for i, (t, n) in enumerate(parts):
        gb_steps.append(begin_halving(
            py, y_place, i == 1, lambda y, t=t, n=n: gb_all.at[pl.ds(mine + t, n), y], inbox_a[i]
        ))
        gb_steps.append(begin_halving(
            px, x_place, i == 1, lambda x, t=t, n=n: gb_all.at[pl.ds(mine + 7 + t, n), :, :, x], inbox_b[i]
        ))

    for copy in part_copies:
        copy.wait()
    coarse_grad = part_out[gz].astype(F32)
    for d in range(3):
        coarse_grad = coarse_grad + part_in[d].astype(F32)
    coarse_grad = coarse_grad.astype(BF)
    for s in range(8):
        rows = pl.ds(64 * s, 64)
        spread = matmul_nt(coarse_grad, wd[s]) + cot_sub[rows].astype(F32)
        fine_grad[rows] = (spread * slope_sub[rows]).astype(BF)
    fine_grad[...] = matmul(perm_back[...], fine_grad[...]).astype(BF)

    def fine_taps(base):
        for step in range(4):
            lines = turned[pl.ds(base + 4 * step, 4)].reshape(512, 512)
            term = matmul(lines, fine_grad[...])
            gc_all[pl.ds(base + 4 * step, 4)] = term.astype(BF).reshape(4, 4, 32, 128)

    keep, give = core * 16, (1 - core) * 16
    fine_taps(give)
    gc_first = remote(gc_all.at[pl.ds(give, 16)], gc_one, {"gy": gy ^ 1})
    gc_first.start()
    fine_taps(keep)

    gc_first.wait()

    @pl.loop(0, 16)
    def _(step):
        total = gc_all[keep + step].astype(F32) + gc_one[step].astype(F32)
        gc_all[keep + step] = total.astype(BF)

    gc_second = along_x(lambda x: gc_all.at[pl.ds(keep + 2 * x, 2)], gc_xa)
    gc_second += along_y(lambda y: gc_all.at[pl.ds(keep + 8, 8), y], gc_yb)

    gb_ends = [step() for step in gb_steps]

    def summed(own, taken):
        total = own.astype(F32)
        for d in range(3):
            total = total + taken[d].astype(F32)
        return total

    for copy in gc_second:
        copy.wait()
    gc_a[...] = summed(gc_all[pl.ds(keep + 2 * px, 2)], gc_xa).astype(BF)
    gc_b[...] = summed(gc_all[pl.ds(keep + 8, 8), py], gc_yb).astype(BF)
    gc_third = along_y(lambda y: gc_a.at[:, y], gc_ya)
    gc_third += along_x(lambda x: gc_b.at[pl.ds(2 * x, 2)], gc_xb)

    gb_steps = []
    for i, (t, n) in enumerate(parts):
        gb_a[t : t + n] = gb_ends[2 * i]().astype(BF)
        gb_steps.append(begin_halving(
            px, x_place, i == 1, lambda x, t=t, n=n: gb_a.at[pl.ds(t, n), :, x], inbox_c[i]
        ))
        gb_b[t : t + n] = gb_ends[2 * i + 1]().astype(BF)
        gb_steps.append(begin_halving(
            py, y_place, i == 1, lambda y, t=t, n=n: gb_b.at[pl.ds(t, n), y], inbox_d[i]
        ))

    for copy in gc_third:
        copy.wait()
    gc_e2[0:2] = summed(gc_a[:, py], gc_ya).astype(BF).reshape(2, 2, 16, 128)
    gc_e2[2:4] = summed(gc_b[pl.ds(2 * px, 2)], gc_xb).astype(BF).reshape(2, 2, 16, 128)
    slot = zh * 4 + gz
    gc_fourth = []
    for d in range(4):
        peer = around(gz, d, 4)
        copy = remote(gc_e2.at[:, 1 - zh], gc_z.at[slot], {"gx": gx ^ 1, "gz": peer})
        copy.start()
        gc_fourth.append(copy)
        if d > 0:
            copy = remote(gc_e2.at[:, zh], gc_z.at[slot], {"gz": peer})
            copy.start()
            gc_fourth.append(copy)
    gc_z[slot] = gc_e2[:, zh]

    gb_last = [step() for step in gb_steps]
    for i, (t, n) in enumerate(parts):
        gb_d4[t : t + n] = gb_last[2 * i]().astype(BF)
        gb_d4[7 + t : 7 + t + n] = gb_last[2 * i + 1]().astype(BF)
    gb_fourth = remote(gb_d4.at[:, 1 - zh], gb_four, {"gx": gx ^ 1})
    gb_fourth.start()

    for copy in bottle_copies:
        copy.wait()
    for s in range(8):
        lifted = jnp.zeros((64, 128), F32)
        for q in range(4):
            lifted = lifted + matmul(bottle_in[q], wu[s, pl.ds(128 * q, 128)])
        total = lifted + hidden_sub[pl.ds(64 * s, 64)].astype(F32)
        fine_grad[pl.ds(64 * s, 64)] = total.astype(BF)
    out_ref[...] = matmul(perm_out[...], fine_grad[...]).astype(BF)

    for copy in gc_fourth:
        copy.wait()
    total = gc_z[0].astype(F32)
    for q in range(1, 8):
        total = total + gc_z[q].astype(F32)
    for half in range(2):
        gc_half[half] = total[:, 8 * half : 8 * half + 8]
    gathers = []
    for d in range(1, 8):
        peer = around(gy, d, 8)
        copy = remote(gc_half.at[peer >> 2], gc_g.at[gy], {"gy": peer})
        copy.start()
        gathers.append(copy)
    gc_g[gy] = gc_half[gy >> 2]

    gb_fourth.wait()
    gb_d5[...] = (gb_d4[:, zh].astype(F32) + gb_four[...].astype(F32)).reshape(14, 2, 8, 128)
    gb_fifth = remote(gb_d5.at[:, 1 - core], gb_five, {"gy": gy ^ 1})
    gb_fifth.start()

    gb_fifth.wait()
    gb_ref[pl.ds(mine, 14)] = gb_d5[:, core]
    gb_ref[pl.ds(other, 14)] = gb_five[...]

    for copy in gathers:
        copy.wait()
    place = gy & 3
    for source in range(8):
        block = gc_g[source]
        chosen = jnp.zeros((4, 2, 128), F32)
        for j in range(4):
            chosen = chosen + jnp.where(place == j, block[:, 2 * j : 2 * j + 2, :], 0.0)
        first = (source & 1) * 16 + (source >> 1) * 2
        gc_ref[first : first + 2] = chosen[0:2]
        gc_ref[first + 8 : first + 10] = chosen[2:4]


def deliver_kernel(out_ref, gb_ref, gc_ref, out_final, gb_final, gc_final):
    out_final[...] = out_ref[...]
    gb_final[...] = gb_ref[0:TAPS]
    gc_final[...] = gc_ref[0:TAPS]


def body(volume, cotangent, w_conv, w_down, w_bottle, w_up):
    vmem = pltpu.VMEM
    whole = pl.BlockSpec(memory_space=pl.ANY)
    held = pl.BlockSpec(memory_space=pltpu.VMEM)
    def kept(*shape):
        return vmem(shape, BF)

    scratch = [
        kept(512, 128), kept(512, 128), kept(27, 128, 128), kept(8, 128, 512),
        kept(27, 512, 128), kept(8, 512, 128), pltpu.SemaphoreType.DMA((6,)),
        kept(512, 512), kept(512, 512), kept(512, 512), kept(512, 512), kept(512, 512),
        kept(3, 256, 256), kept(3, 128, 128), kept(256, 256), kept(3, 128, 128),
        kept(2, 64, 128), kept(2, 64, 128), kept(2, 64, 128), kept(2, 80, 128), kept(2, 80, 128),
        kept(2, 48, 128), kept(2, 48, 128),
        vmem((10, 10, 24, 128), F32), kept(27, 512, 128), kept(32, 128, 512), vmem((512, 128), F32),
        kept(512, 128), vmem((512, 128), F32), kept(512, 128),
        kept(4, 64, 128), kept(4, 64, 128), kept(4, 64, 512), kept(4, 32, 512), kept(3, 6, 6, 16, 512),
        kept(2, 64, 512), kept(2, 64, 512), kept(2, 32, 512), kept(4, 32, 512), vmem((256, 128), F32),
        kept(256, 128), kept(3, 6, 6, 16, 128), kept(2, 64, 128), kept(2, 64, 128),
        kept(2, 96, 128), kept(2, 128, 128),
        kept(4, 64, 128), kept(4, 64, 128), vmem((256, 512), F32), kept(4, 64, 512),
        kept(3, 64, 512), kept(512, 128),
        kept(28, 4, 2, 4, 16, 128), kept(14, 4, 2, 4, 16, 128),
        kept(3, 4, 2, 4, 16, 128), kept(3, 3, 2, 4, 16, 128), kept(3, 4, 4, 2, 16, 128), kept(3, 3, 4, 2, 16, 128),
        kept(7, 2, 4, 16, 128), kept(7, 4, 2, 16, 128),
        kept(3, 4, 2, 16, 128), kept(3, 3, 2, 16, 128), kept(3, 4, 2, 16, 128), kept(3, 3, 2, 16, 128),
        kept(14, 2, 16, 128), kept(14, 16, 128), vmem((14, 2, 8, 128), F32), vmem((14, 8, 128), F32),
        kept(32, 4, 32, 128), kept(16, 4, 32, 128), kept(3, 2, 4, 32, 128), kept(3, 8, 32, 128),
        kept(2, 4, 32, 128), kept(8, 32, 128), kept(3, 2, 32, 128), kept(3, 2, 32, 128),
        kept(4, 2, 16, 128), kept(8, 4, 16, 128), vmem((2, 4, 8, 128), F32), vmem((8, 4, 8, 128), F32),
        pltpu.SemaphoreType.DMA((COPIES,)), pltpu.SemaphoreType.DMA((COPIES,)),
    ]
    out, gb, gc = pl.pallas_call(
        level_kernel,
        out_shape=(
            jax.ShapeDtypeStruct((512, 128), BF),
            jax.ShapeDtypeStruct((28, 8, 128), F32),
            jax.ShapeDtypeStruct((32, 2, 128), F32),
        ),
        in_specs=[whole] * 6,
        out_specs=(held,) * 3,
        scratch_shapes=scratch,
        compiler_params=pltpu.CompilerParams(
            collective_id=0, has_side_effects=True, vmem_limit_bytes=60 * 1024 * 1024
        ),
        name="level",
    )(
        volume.reshape(512, 128),
        cotangent.reshape(512, 128),
        jnp.transpose(w_conv, (1, 0, 2)),
        w_down,
        jnp.transpose(w_bottle, (1, 0, 2)),
        w_up,
    )
    out, gb, gc = pl.pallas_call(
        deliver_kernel,
        out_shape=(
            jax.ShapeDtypeStruct(out.shape, BF),
            jax.ShapeDtypeStruct((TAPS, 8, 128), F32),
            jax.ShapeDtypeStruct((TAPS, 2, 128), F32),
        ),
        in_specs=[held] * 3,
        out_specs=(held,) * 3,
        name="deliver",
    )(out, gb, gc)
    return out.reshape(volume.shape), jnp.transpose(gc, (1, 0, 2)), jnp.transpose(gb, (1, 0, 2))


def solution(mesh):
    in_specs = (
        P("gz", "gx", "gy", None),
        P("gz", "gx", "gy", None),
        P(),
        P(),
        P(None, None, "gz"),
        P(),
    )
    out_specs = (
        P("gz", "gx", "gy", None),
        P(("gx", "gy"), None, None),
        P(("gx", "gy"), None, "gz"),
    )
    return jax.shard_map(body, mesh=mesh, in_specs=in_specs, out_specs=out_specs, check_vma=False)
```
